32 devices in a mesh: gx: 4 (over z), gy: 2 (over y), gz: 4 (over x, core).
Axes of the slice: x: 2, y: 2, z: 4, core: 2. Of those that a mesh axis runs over, the one named last changes fastest.
Arguments:
- cell_state: float32 [3, 32, 32, 512], P(None, 'gx', 'gy', 'gz'), may hold values from 0 to 1, as said below
- old_mass: float32 [3, 32, 32, 512], P(None, 'gx', 'gy', 'gz'), may hold values from 0 to 1.5
- pore_volume: float32 [32, 32, 512], P('gx', 'gy', 'gz'), may hold values from 0.5 to 2
- transmissibility: float32 [13, 32, 32, 512], P(None, 'gx', 'gy', 'gz'), may hold values from 0.02 to 1
- active_mask: int32 [32, 32, 512], P('gx', 'gy', 'gz'), may hold values 0 or 1
- pvt_region: int32 [32, 32, 512], P('gx', 'gy', 'gz'), may hold values from 0 to 7
- formation_factor: float32 [3, 8], replicated, may hold values from 0.6 to 1.5
- compressibility: float32 [3, 8], replicated, may hold values from 0.05 to 0.2
- inverse_viscosity: float32 [3, 8], replicated, may hold values from 0.3 to 3
Outputs:
- residual: float32 [3, 32, 32, 512], P(None, 'gx', 'gy', 'gz')
- pressure_update: float32 [32, 32, 512], P('gx', 'gy', 'gz')
The draws below stay inside these ranges and needn't reach their ends.
Inputs may be any that keep to these rules, and one draw needn't show every extreme that they name: `cell_state`: channel 0 is the pressure; channels 1 and 2 are positive saturations whose sum stays below 1.
All inputs are finite; a program needn't handle non-finite values. No bound on the sum of `active_mask` on one device may be relied on, other than what follows from the above.
Results may differ from the reference program's by a relative error of at most 0.0003.
Values sent between devices are 32-bit elements; how exact they have to be, the bound alone decides.
No kernel may reach another device: no remote copies, remote signals or barrier semaphores. Data moves between devices by JAX's collectives and lax.ppermute only.
A program may use at most 64 MiB of HBM per device.

```python
import math
import jax
import jax.numpy as jnp

REGIONS = 8
SWEEPS = 4
NX = 32
NY = 32
NZ = 512


def draw_cell_state(key, part):
    key_pressure, key_water, key_oil, key_gas = jax.random.split(key, 4)
    shape_cells = (NX, NY, NZ)
    pressure = jax.random.uniform(key_pressure, shape_cells, jnp.float32, 0.0, 1.0)
    water_part = jnp.exp(jax.random.uniform(key_water, shape_cells, jnp.float32, -1.0, 1.0))
    oil_part = jnp.exp(jax.random.uniform(key_oil, shape_cells, jnp.float32, -1.0, 1.0))
    gas_part = jnp.exp(jax.random.uniform(key_gas, shape_cells, jnp.float32, -1.0, 1.0))
    part_sum = water_part + oil_part + gas_part
    return jnp.stack([pressure, water_part / part_sum, gas_part / part_sum]).astype(jnp.float32)


def plant(entries, own_key, smallest, high):
    shape = entries.shape
    spot = [jax.random.randint(jax.random.fold_in(own_key, axis), (), 0, shape[axis]) for axis in range(len(shape))]
    entries = entries.at[tuple(spot)].set(smallest)
    longest = shape.index(max(shape))
    spot[longest] = (spot[longest] + 1) % shape[longest]
    return entries.at[tuple(spot)].set(high)


def block_scale(stream_key, shape, pieces, low, top_value):
    level, own = 1.0, jax.random.fold_in(stream_key, 6)
    for dim, blocks in pieces:
        steps = jnp.exp(jax.random.uniform(jax.random.fold_in(own, dim), (blocks,), jnp.float32, low / len(pieces), top_value / len(pieces)))
        level = level * jnp.repeat(steps, shape[dim] // blocks).reshape([-1 if axis == dim else 1 for axis in range(len(shape))])
    return level


def setup_inputs(seed: int = 0) -> dict:
    key_list = jax.random.split(jax.random.key(seed), 10)
    return {
        "cell_state": draw_cell_state(jax.random.fold_in(key_list[9], 71), 0),
        "old_mass": jnp.clip(1.5 * jax.random.uniform(key_list[1], (3, NX, NY, NZ), jnp.float32) ** block_scale(key_list[1], (3, NX, NY, NZ), ((1, 4), (2, 2), (3, 4)), -0.2, 0.2), 0.0, 1.5),
        "pore_volume": jnp.clip(jnp.exp(math.log(2.0) - 1.3862944 * jax.random.uniform(key_list[2], (NX, NY, NZ), jnp.float32) ** block_scale(key_list[2], (NX, NY, NZ), ((0, 4), (1, 2), (2, 4)), -0.2, 0.2)), 0.5, 2.0),
        "transmissibility": jnp.clip(jnp.exp(math.log(1.0) - 3.912023 * jax.random.uniform(key_list[3], (13, NX, NY, NZ), jnp.float32) ** block_scale(key_list[3], (13, NX, NY, NZ), ((1, 4), (2, 2), (3, 4)), -0.2, 0.2)), 0.02, 1.0),
        "active_mask": plant((jax.random.randint(key_list[4], (NX, NY, NZ), 0, 10) < 9).astype(jnp.int32), jax.random.fold_in(key_list[4], 1), 0, 1),
        "pvt_region": plant(jax.random.randint(key_list[5], (NX, NY, NZ), 0, REGIONS), jax.random.fold_in(key_list[5], 1), 0, REGIONS - 1).astype(jnp.int32),
        "formation_factor": jnp.clip(jnp.exp(jax.random.uniform(key_list[6], (3, REGIONS), jnp.float32, math.log(0.6), math.log(1.5))), 0.6, 1.5),
        "compressibility": jnp.clip(jnp.exp(jax.random.uniform(key_list[7], (3, REGIONS), jnp.float32, math.log(0.05), math.log(0.2))), 0.05, 0.2),
        "inverse_viscosity": jnp.clip(jnp.exp(jax.random.uniform(key_list[8], (3, REGIONS), jnp.float32, math.log(0.3), math.log(3.0))), 0.3, 3.0),
    }


neighbour_offsets = [(along_x, along_y, along_z) for along_x in (-1, 0, 1) for along_y in (-1, 0, 1) for along_z in (-1, 0, 1) if (along_x, along_y, along_z) != (0, 0, 0)]
upper_offsets = [offset for offset in neighbour_offsets if offset > (0, 0, 0)]
relax_weight = 0.7


def window(values_in, offset):
    extent = values_in.shape[-3:]
    return values_in[..., 1 + offset[0]:extent[0] - 1 + offset[0], 1 + offset[1]:extent[1] - 1 + offset[1], 1 + offset[2]:extent[2] - 1 + offset[2]]


def lookup(table_in, region_float):
    looked_up = jnp.zeros((table_in.shape[0],) + region_float.shape, region_float.dtype)
    for level in range(table_in.shape[1]):
        chosen = (region_float == level).astype(region_float.dtype)
        looked_up = looked_up + table_in[:, level][:, None, None, None] * chosen[None]
    return looked_up


def assemble(padded, old_mass, pore_volume, tables):
    formation, compress_table, viscous_inverse = tables
    pressure = padded[0]
    active = padded[3]
    saturation = jnp.stack([padded[1], 1.0 - padded[1] - padded[2], padded[2]])
    compress_rate = lookup(compress_table, padded[4])
    expansion = lookup(formation, padded[4]) * jnp.exp(compress_rate * (pressure[None] - 0.5))
    mobility = lookup(viscous_inverse, padded[4]) * expansion * saturation * saturation
    slope_all = compress_rate * mobility
    centre = (0, 0, 0)
    press_here = window(pressure, centre)
    active_here = window(active, centre)
    mobility_here = window(mobility, centre)
    slope_here = window(slope_all, centre)
    saturation_here = window(saturation, centre)
    expansion_here = window(expansion, centre)
    storage = pore_volume * jnp.sum(window(compress_rate, centre) * saturation_here, axis=0)
    scaling = 1.0 / jnp.where(active_here > 0, storage, 1.0)
    weights = scaling[None] / expansion_here
    flux_total = jnp.zeros_like(saturation_here)
    diagonal = jnp.ones_like(press_here)
    couplings = []
    for offset in neighbour_offsets:
        if offset in upper_offsets:
            link_trans = window(padded[5 + upper_offsets.index(offset)], centre)
        else:
            mirror = (-offset[0], -offset[1], -offset[2])
            link_trans = window(padded[5 + upper_offsets.index(mirror)], offset)
        link_trans = link_trans * active_here * window(active, offset)
        press_drop = press_here - window(pressure, offset)
        mobility_mean = 0.5 * (mobility_here + window(mobility, offset))
        flux_total = flux_total + link_trans * mobility_mean * press_drop
        diagonal = diagonal + link_trans * jnp.sum(weights * (0.5 * slope_here * press_drop + mobility_mean), axis=0)
        couplings.append(link_trans * jnp.sum(weights * (0.5 * window(slope_all, offset) * press_drop - mobility_mean), axis=0))
    residual = active_here * (pore_volume * expansion_here * saturation_here - old_mass + flux_total)
    pressure_rhs = -jnp.sum(weights * residual, axis=0)
    return residual, diagonal, jnp.stack(couplings), pressure_rhs


def relax(padded_update, diagonal, couplings, pressure_rhs):
    centre_update = window(padded_update, (0, 0, 0))
    product = diagonal * centre_update
    for position, offset in enumerate(neighbour_offsets):
        product = product + couplings[position] * window(padded_update, offset)
    return centre_update + relax_weight * (pressure_rhs - product) / diagonal


def reference(cell_state, old_mass, pore_volume, transmissibility, active_mask, pvt_region, formation_factor, compressibility, inverse_viscosity):
    stacked = jnp.concatenate([cell_state, active_mask[None].astype(cell_state.dtype), pvt_region[None].astype(cell_state.dtype), transmissibility], axis=0)
    padded = jnp.pad(stacked, ((0, 0), (1, 1), (1, 1), (1, 1)))
    residual, diagonal, couplings, pressure_rhs = assemble(padded, old_mass, pore_volume, (formation_factor, compressibility, inverse_viscosity))
    update = relax_weight * pressure_rhs / diagonal
    for sweep_index in range(SWEEPS - 1):
        update = relax(jnp.pad(update, 1), diagonal, couplings, pressure_rhs)
    return residual, update
```

```python
import functools

import jax
import jax.numpy as jnp
from jax import lax
from jax.experimental import pallas as pl
from jax.experimental.pallas import tpu as pltpu
from jax.sharding import PartitionSpec as P

SWEEPS = 4
W = SWEEPS
relax_weight = 0.7

neighbour_offsets = [
    (along_x, along_y, along_z)
    for along_x in (-1, 0, 1)
    for along_y in (-1, 0, 1)
    for along_z in (-1, 0, 1)
    if (along_x, along_y, along_z) != (0, 0, 0)
]
upper_offsets = [offset for offset in neighbour_offsets if offset > (0, 0, 0)]
UP = len(upper_offsets)
FLAT = sum(1 for offset in upper_offsets if offset[0] == 0)
STEP = UP - FLAT

FAR = 5 + STEP
CHANNELS = FAR + FLAT + 4
NEAR = W - 1
XMAIN = CHANNELS * NEAR + FAR
XMSG = XMAIN + 2 * W
VMEM = pl.BlockSpec(memory_space=pltpu.VMEM)
ANY = pl.BlockSpec(memory_space=pl.ANY)
f32 = jnp.float32


def t_channel(k):
    return FAR + k if k < FLAT else 5 + k - FLAT


def channel_of(local, c, planes):
    state, mass, pore, trans, active, region = local
    if c < 3:
        return state[c, planes]
    if c == 3:
        return active[planes].astype(f32)
    if c == 4:
        return region[planes].astype(f32)
    if c < FAR:
        return trans[FLAT + c - 5, planes]
    if c < FAR + FLAT:
        return trans[c - FAR, planes]
    if c < CHANNELS - 1:
        return mass[c - FAR - FLAT, planes]
    return pore[planes]


def pick(parity, even, odd):
    shape = (even if odd is None else odd).shape
    if even is None:
        even = jnp.zeros(shape, f32)
    if odd is None:
        odd = jnp.zeros(shape, f32)
    return jnp.where(jnp.full(shape, parity, jnp.int32) == 0, even, odd)


def parity_of(axis):
    return lax.rem(lax.axis_index(axis), 2)


def swaps(axis, first, second):
    count = lax.axis_size(axis)
    got = []
    for start, message in ((0, first), (1, second)):
        pairs = [(i, i + 1) for i in range(start, count - 1, 2)]
        if not pairs:
            got.append(None)
            continue
        got.append(lax.ppermute(message, axis, pairs + [(b, a) for a, b in pairs]))
    return got


def lanes_of(shape):
    return lax.broadcasted_iota(jnp.int32, shape, len(shape) - 1)


def pack_z(axis, *refs):
    local, (first, second) = refs[:6], refs[6:]
    planes, rows, depth = local[2].shape
    even = parity_of(axis)
    lane = lanes_of((rows, depth))

    @pl.loop(0, planes)
    def _(x):
        high = jnp.zeros((rows, depth), f32)
        low = jnp.zeros((rows, depth), f32)
        for c in range(CHANNELS):
            values = channel_of(local, c, x)
            here = (lane >= W * c) & (lane < W * c + W)
            high = jnp.where(here, pltpu.roll(values, (W * c + W) % depth, 1), high)
            low = jnp.where(here, pltpu.roll(values, (W * c) % depth, 1), low)
        first[x] = pick(even, high, low)
        second[x] = pick(even, low, high)


def pack_x(axis, *refs):
    local, outs = refs[:6], refs[6:]
    planes = local[2].shape[0]
    even = parity_of(axis)
    for out, up in zip(outs, (even == 0, even != 0)):
        near = jnp.where(up, planes - NEAR, 0)
        far = jnp.where(up, planes - W, W - 1)
        for c in range(CHANNELS):
            for q in range(NEAR):
                out[c * NEAR + q] = channel_of(local, c, near + q)
            if c < FAR:
                out[CHANNELS * NEAR + c] = channel_of(local, c, far)


def join_x(axis, z_axis, planes, za, zb, a_in, b_in, a_out, b_out, low, high, sems):
    even_z = parity_of(z_axis)
    even = parity_of(axis)
    low[...] = pick(even_z, zb[...], za[...])
    high[...] = pick(even_z, za[...], zb[...])
    copies = []
    for n, (out, up) in enumerate(((a_out, even == 0), (b_out, even != 0))):
        start = jnp.where(up, planes - W, 0)
        for m, source in enumerate((low, high)):
            copies.append(
                pltpu.make_async_copy(
                    source.at[pl.ds(start, W)],
                    out.at[pl.ds(XMAIN + m * W, W)],
                    sems.at[n, m],
                )
            )
    for copy in copies:
        copy.start()
    for copy in copies:
        copy.wait()


def pack_y(axis, z_axis, *refs):
    local, (za, zb), outs = refs[:6], refs[6:8], refs[8:]
    planes, rows = local[2].shape[:2]
    even = parity_of(axis)
    even_z = parity_of(z_axis)
    for n in range(CHANNELS):
        for x in range(planes):
            values = channel_of(local, n, x)
            head, tail = values[:W], values[rows - W :]
            for out, up, down in zip(outs, (tail, head), (head, tail)):
                out[n * planes + x] = pick(even, up, down)
    for x in range(planes):
        for m, values in enumerate((pick(even_z, zb[x], za[x]), pick(even_z, za[x], zb[x]))):
            head, tail = values[:W], values[rows - W :]
            for out, up, down in zip(outs, (tail, head), (head, tail)):
                out[(CHANNELS + m) * planes + x] = pick(even, up, down)


def join_y(axis, x_axis, count, planes, *refs):
    xa, xb = refs[:2]
    outs = refs[2 + count : 2 + 2 * count]
    stage, sems = refs[2 + 2 * count :]
    rows = xa.shape[1]
    even = parity_of(axis)
    even_x = parity_of(x_axis)

    @pl.loop(0, XMSG)
    def _(n):
        a, b = xa[n], xb[n]
        for m, values in enumerate((pick(even_x, b, a), pick(even_x, a, b))):
            head, tail = values[:W], values[rows - W :]
            for i, (up, down) in enumerate(((tail, head), (head, tail))[:count]):
                stage[i, m * XMSG + n] = pick(even, up, down)

    base = (CHANNELS + 2) * planes
    copies = [
        pltpu.make_async_copy(stage.at[i], out.at[pl.ds(base, 2 * XMSG)], sems.at[i])
        for i, out in enumerate(outs)
    ]
    for copy in copies:
        copy.start()
    for copy in copies:
        copy.wait()


PRESS, MOB, SLOPE, ACT = 0, 1, 4, 7
SHIFTED = 8
TOP = 8


def shift_z(first, second, step):
    depth = first.shape[-1]
    lane = lanes_of(first.shape)
    edge = lane == (depth - 1 if step > 0 else 0)
    amount = depth - 1 if step > 0 else 1
    a, b = pltpu.roll(first, amount, 1), pltpu.roll(second, amount, 1)
    return jnp.where(edge, b, a), jnp.where(edge, a, b)


def solve(axes, count_y, *refs):
    local = refs[:6]
    tables = refs[6:9]
    za, zb, xa, xb = refs[9:13]
    ys = refs[13 : 13 + count_y]
    residual, update = refs[13 + count_y : 15 + count_y]
    (zl, zh, raw, fields, lower, weight, coupling, scale, start, store, sol) = refs[15 + count_y :]
    planes, rows, depth = local[2].shape
    even_x, even_y, even_z = (parity_of(axis) for axis in axes)
    ya = ys[0] if count_y > 0 else None
    yb = ys[1] if count_y > 1 else None
    total = planes + 2 * W

    def both(a, b, even):
        return pick(even, b, a), pick(even, a, b)

    def put_halo_rows(target, n):
        low, high = None, None
        a = None if ya is None else ya[n]
        b = None if yb is None else yb[n]
        if a is None:
            low = high = jnp.zeros((W, depth), f32)
        else:
            low, high = pick(even_y, b, a), pick(even_y, a, b)
        target[TOP - W : TOP, :] = low
        target[TOP + rows : TOP + rows + W, :] = high

    body_rows = slice(TOP, TOP + rows)
    x_base = (CHANNELS + 2) * planes

    @pl.loop(0, planes)
    def _(x):
        low, high = both(za[x], zb[x], even_z)
        for m, (target, values) in enumerate(((zl, low), (zh, high))):
            put_halo_rows(target.at[W + x], (CHANNELS + m) * planes + x)
            target[W + x, body_rows, :] = values
        for c in range(CHANNELS):
            put_halo_rows(raw.at[c, W + x, 0], c * planes + x)
            raw[c, W + x, 0, body_rows, :] = channel_of(local, c, x)

    def from_x(target_low, target_high, n):
        low, high = both(xa[n], xb[n], even_x)
        put_halo_rows(target_low, x_base + n)
        target_low[body_rows, :] = low
        put_halo_rows(target_high, x_base + XMSG + n)
        target_high[body_rows, :] = high

    @pl.loop(0, CHANNELS)
    def _(c):
        for q in range(NEAR):
            from_x(raw.at[c, 1 + q, 0], raw.at[c, W + planes + q, 0], c * NEAR + q)

    @pl.loop(0, FAR)
    def _(c):
        from_x(raw.at[c, 0, 0], raw.at[c, total - 1, 0], CHANNELS * NEAR + c)

    for m, target in enumerate((zl, zh)):
        for q in range(W):
            from_x(target.at[q], target.at[W + planes + q], XMAIN + m * W + q)

    tiles = (rows + 2 * W) // 8
    lane = lanes_of((8, depth))

    @pl.loop(0, total)
    def _(x):
        for tile in range(tiles):
            span = slice(TOP - W + 8 * tile, TOP - W + 8 * tile + 8)
            low, high = zl[x, span, :], zh[x, span, :]
            for c in range(CHANNELS):
                above = pltpu.roll(high, (depth - W * c) % depth, 1)
                below = pltpu.roll(low, (2 * depth - W - W * c) % depth, 1)
                raw[c, x, 1, span, :] = jnp.where(lane < W, above, below)

    @pl.loop(0, total)
    def _(x):
        for tile in range(tiles):
            span = slice(TOP - W + 8 * tile, TOP - W + 8 * tile + 8)
            pair = []
            for side in range(2):
                get = lambda c: raw[c, x, side, span, :]
                press, water, gas, active, region = (get(c) for c in range(5))
                looked = [[jnp.full((8, depth), table[c, 0], f32) for c in range(3)] for table in tables]
                for level in range(1, tables[0].shape[1]):
                    chosen = region == level
                    for one, table in zip(looked, tables):
                        for c in range(3):
                            one[c] = jnp.where(chosen, table[c, level], one[c])
                formation, compress, viscous = looked
                sat = (water, 1.0 - water - gas, gas)
                expand = [formation[c] * jnp.exp(compress[c] * (press - 0.5)) for c in range(3)]
                mob = [viscous[c] * expand[c] * sat[c] * sat[c] for c in range(3)]
                pore = get(CHANNELS - 1)
                stored = pore * (compress[0] * sat[0] + compress[1] * sat[1] + compress[2] * sat[2])
                stored = jnp.where(active > 0, stored, 1.0)
                for c in range(3):
                    weight[c, x, side, span, :] = active / (expand[c] * stored)
                    raw[FAR + FLAT + c, x, side, span, :] = (
                        pore * expand[c] * sat[c] - get(FAR + FLAT + c)
                    )
                one = [press] + mob + [compress[c] * mob[c] for c in range(3)] + [active]
                trans = []
                for k in range(UP):
                    half = 0.5 * get(t_channel(k))
                    raw[t_channel(k), x, side, span, :] = half
                    trans.append(half * active)
                pair.append((one, trans))
            for f in range(SHIFTED):
                a, b = pair[0][0][f], pair[1][0][f]
                for step in (-1, 0, 1):
                    u, v = (a, b) if step == 0 else shift_z(a, b, step)
                    fields[f, step + 1, x, 0, span, :] = u
                    fields[f, step + 1, x, 1, span, :] = v
            for k, offset in enumerate(upper_offsets):
                u, v = pair[0][1][k], pair[1][1][k]
                if offset[2] != 0:
                    u, v = shift_z(u, v, -offset[2])
                lower[k, x, 0, span, :] = u
                lower[k, x, 1, span, :] = v

    base = TOP - W + 1

    def put_solution(slot, x, first, a, b):
        for step in (-1, 0, 1):
            u, v = (a, b) if step == 0 else shift_z(a, b, step)
            sol[slot, step + 1, x, 0, pl.ds(first, 8), :] = u
            sol[slot, step + 1, x, 1, pl.ds(first, 8), :] = v

    @pl.loop(1, total - 1)
    def _(x):
        for tile in range(tiles):
            first = base + 8 * tile
            out = slice(8 * tile, 8 * tile + 8)
            pair = []
            for side in range(2):
                def at(f, offset):
                    return fields[
                        f, offset[2] + 1, x + offset[0], side, pl.ds(first + offset[1], 8), :
                    ]

                here = (0, 0, 0)
                press = at(PRESS, here)
                w = [weight[c, x, side, pl.ds(first, 8), :] for c in range(3)]
                mob = [at(MOB + c, here) for c in range(3)]
                own_mob = w[0] * mob[0] + w[1] * mob[1] + w[2] * mob[2]
                own_slope = w[0] * at(SLOPE, here) + w[1] * at(SLOPE + 1, here) + w[2] * at(SLOPE + 2, here)
                flux = [jnp.zeros((8, depth), f32) for _ in range(3)]
                drops = jnp.zeros((8, depth), f32)
                means = jnp.ones((8, depth), f32)
                for n, offset in enumerate(neighbour_offsets):
                    if offset > here:
                        k = upper_offsets.index(offset)
                        link = raw[t_channel(k), x, side, pl.ds(first, 8), :] * at(ACT, offset)
                    else:
                        k = upper_offsets.index(tuple(-o for o in offset))
                        link = lower[k, x + offset[0], side, pl.ds(first + offset[1], 8), :]
                    drop = link * (press - at(PRESS, offset))
                    other = [at(MOB + c, offset) for c in range(3)]
                    for c in range(3):
                        flux[c] = flux[c] + drop * other[c]
                    drops = drops + drop
                    mean = own_mob + (w[0] * other[0] + w[1] * other[1] + w[2] * other[2])
                    slope = (
                        w[0] * at(SLOPE, offset)
                        + w[1] * at(SLOPE + 1, offset)
                        + w[2] * at(SLOPE + 2, offset)
                    )
                    mean = link * mean
                    means = means + mean
                    coupling[n, x, side, out, :] = drop * slope - mean
                active = at(ACT, here)
                res = [
                    active
                    * (raw[FAR + FLAT + c, x, side, pl.ds(first, 8), :] + (flux[c] + mob[c] * drops))
                    for c in range(3)
                ]
                if side == 0:
                    for c in range(3):
                        store[c, x, out, :] = res[c]
                diagonal = means + own_slope * drops
                rate = relax_weight / diagonal
                right = -(w[0] * res[0] + w[1] * res[1] + w[2] * res[2])
                guess = rate * right
                scale[x, side, out, :] = rate
                start[x, side, out, :] = guess
                pair.append(guess)
            put_solution(0, x, first, *pair)

    def relaxed(slot, x, side, first):
        get = lambda offset: sol[
            slot, offset[2] + 1, x + offset[0], side, pl.ds(first + offset[1], 8), :
        ]
        out = pl.ds(first - base, 8)
        parts = [jnp.zeros((8, depth), f32) for _ in range(2)]
        for n, offset in enumerate(neighbour_offsets):
            parts[n % 2] = parts[n % 2] + coupling[n, x, side, out, :] * get(offset)
        return (
            (1.0 - relax_weight) * get((0, 0, 0))
            + start[x, side, out, :]
            - scale[x, side, out, :] * (parts[0] + parts[1])
        )

    for sweep in range(2, SWEEPS):
        slot = sweep % 2

        @pl.loop(sweep, total - sweep)
        def _(x):
            for tile in range(tiles):
                first = base + 8 * tile
                put_solution(1 - slot, x, first, relaxed(slot, x, 0, first), relaxed(slot, x, 1, first))

    @pl.loop(0, planes)
    def _(x):
        for tile in range(rows // 8):
            first = TOP + 8 * tile
            span = slice(8 * tile, 8 * tile + 8)
            update[x, span, :] = relaxed(SWEEPS % 2, W + x, 0, first)
            for c in range(3):
                residual[c, x, span, :] = store[c, W + x, pl.ds(first - base, 8), :]


def params(mib):
    return pltpu.CompilerParams(vmem_limit_bytes=mib << 20)


def body(
    cell_state,
    old_mass,
    pore_volume,
    transmissibility,
    active_mask,
    pvt_region,
    formation_factor,
    compressibility,
    inverse_viscosity,
):
    ax, ay, az = "gx", "gy", "gz"
    planes, rows, depth = pore_volume.shape
    local = (cell_state, old_mass, pore_volume, transmissibility, active_mask, pvt_region)
    like = lambda *shape: jax.ShapeDtypeStruct(shape, f32)
    face = like(planes, rows, depth)
    z_send = pl.pallas_call(
        functools.partial(pack_z, az), out_shape=(face, face), compiler_params=params(16), name="pack_z"
    )(*local)
    za, zb = (
        jnp.zeros(face.shape, f32) if got is None else got for got in swaps(az, *z_send)
    )

    x_shape = like(XMSG, rows, depth)
    x_send = pl.pallas_call(
        functools.partial(pack_x, ax), out_shape=(x_shape, x_shape), compiler_params=params(16), name="pack_x"
    )(*local)
    x_send = pl.pallas_call(
        functools.partial(join_x, ax, az, planes),
        out_shape=(x_shape, x_shape),
        in_specs=[VMEM, VMEM, ANY, ANY],
        out_specs=(ANY, ANY),
        scratch_shapes=[
            pltpu.VMEM(face.shape, f32),
            pltpu.VMEM(face.shape, f32),
            pltpu.SemaphoreType.DMA((2, 2)),
        ],
        input_output_aliases={2: 0, 3: 1},
        compiler_params=params(8),
        name="join_x",
    )(za, zb, *x_send)
    xa, xb = (
        jnp.zeros(x_shape.shape, f32) if got is None else got for got in swaps(ax, *x_send)
    )

    count_y = min(lax.axis_size(ay) - 1, 2)
    ys = []
    if count_y:
        y_shape = like((CHANNELS + 2) * planes + 2 * XMSG, W, depth)
        y_send = pl.pallas_call(
            functools.partial(pack_y, ay, az),
            out_shape=(y_shape,) * count_y,
            compiler_params=params(16),
            name="pack_y",
        )(*local, za, zb)
        y_send = pl.pallas_call(
            functools.partial(join_y, ay, ax, count_y, planes),
            out_shape=(y_shape,) * count_y,
            in_specs=[VMEM, VMEM] + [ANY] * count_y,
            out_specs=(ANY,) * count_y,
            scratch_shapes=[
                pltpu.VMEM((count_y, 2 * XMSG, W, depth), f32),
                pltpu.SemaphoreType.DMA((count_y,)),
            ],
            input_output_aliases={2 + i: i for i in range(count_y)},
            compiler_params=params(16),
            name="join_y",
        )(xa, xb, *y_send)
        ys = swaps(ay, y_send[0], y_send[-1])[:count_y]

    total = planes + 2 * W
    tall = rows + 2 * TOP
    inner = rows + 2 * W
    smem = pl.BlockSpec(memory_space=pltpu.SMEM)
    return pl.pallas_call(
        functools.partial(solve, (ax, ay, az), count_y),
        out_shape=(like(3, planes, rows, depth), face),
        in_specs=[VMEM] * 6 + [smem] * 3 + [VMEM] * (4 + count_y),
        out_specs=(VMEM, VMEM),
        scratch_shapes=[
            pltpu.VMEM((total, tall, depth), f32),
            pltpu.VMEM((total, tall, depth), f32),
            pltpu.VMEM((CHANNELS, total, 2, tall, depth), f32),
            pltpu.VMEM((SHIFTED, 3, total, 2, tall, depth), f32),
            pltpu.VMEM((UP, total, 2, tall, depth), f32),
            pltpu.VMEM((3, total, 2, tall, depth), f32),
            pltpu.VMEM((2 * UP, total, 2, inner, depth), f32),
            pltpu.VMEM((total, 2, inner, depth), f32),
            pltpu.VMEM((total, 2, inner, depth), f32),
            pltpu.VMEM((3, total, inner, depth), f32),
            pltpu.VMEM((2, 3, total, 2, tall, depth), f32),
        ],
        compiler_params=params(60),
        name="solve",
    )(
        *local,
        formation_factor,
        compressibility,
        inverse_viscosity,
        za,
        zb,
        xa,
        xb,
        *ys,
    )


def solution(mesh):
    return jax.shard_map(
        body,
        mesh=mesh,
        in_specs=(
            P(None, "gx", "gy", "gz"),
            P(None, "gx", "gy", "gz"),
            P("gx", "gy", "gz"),
            P(None, "gx", "gy", "gz"),
            P("gx", "gy", "gz"),
            P("gx", "gy", "gz"),
            P(),
            P(),
            P(),
        ),
        out_specs=(P(None, "gx", "gy", "gz"), P("gx", "gy", "gz")),
        check_vma=False,
    )
```

```python
import functools

import jax
import jax.numpy as jnp
from jax import lax
from jax.experimental import pallas as pl
from jax.experimental.pallas import tpu as pltpu
from jax.sharding import PartitionSpec as P

SWEEPS = 4
W = SWEEPS
relax_weight = 0.7

neighbour_offsets = [
    (along_x, along_y, along_z)
    for along_x in (-1, 0, 1)
    for along_y in (-1, 0, 1)
    for along_z in (-1, 0, 1)
    if (along_x, along_y, along_z) != (0, 0, 0)
]
upper_offsets = [offset for offset in neighbour_offsets if offset > (0, 0, 0)]
UP = len(upper_offsets)
FLAT = sum(1 for offset in upper_offsets if offset[0] == 0)
STEP = UP - FLAT

FAR = 5 + STEP
CHANNELS = FAR + FLAT + 4
NEAR = W - 1
XMAIN = CHANNELS * NEAR + FAR
VMEM = pl.BlockSpec(memory_space=pltpu.VMEM)
ANY = pl.BlockSpec(memory_space=pl.ANY)
f32 = jnp.float32


def t_channel(k):
    return FAR + k if k < FLAT else 5 + k - FLAT


def pick(parity, even, odd):
    shape = (even if odd is None else odd).shape
    if even is None:
        even = jnp.zeros(shape, f32)
    if odd is None:
        odd = jnp.zeros(shape, f32)
    return jnp.where(jnp.full(shape, parity, jnp.int32) == 0, even, odd)


def parity_of(axis):
    return lax.rem(lax.axis_index(axis), 2)


def swaps(axis, first, second):
    count = lax.axis_size(axis)
    got = []
    for start, message in ((0, first), (1, second)):
        pairs = [(i, i + 1) for i in range(start, count - 1, 2)]
        if not pairs:
            got.append(None)
            continue
        got.append(lax.ppermute(message, axis, pairs + [(b, a) for a, b in pairs]))
    return got


def lanes_of(shape):
    return lax.broadcasted_iota(jnp.int32, shape, len(shape) - 1)


def span_of(planes):
    return 2 * W * planes


def groups_of(planes, depth):
    per = depth // span_of(planes)
    return per, -(-CHANNELS // per)


def pack_z(axis, *refs):
    state, mass, pore, trans, active, region, local, first, second, flags, sems = refs
    planes, rows, depth = pore.shape
    copies = [
        pltpu.make_async_copy(active, flags.at[0], sems.at[0]),
        pltpu.make_async_copy(region, flags.at[1], sems.at[1]),
        pltpu.make_async_copy(state, local.at[0:3], sems.at[2]),
        pltpu.make_async_copy(trans.at[FLAT:UP], local.at[5:FAR], sems.at[3]),
        pltpu.make_async_copy(trans.at[0:FLAT], local.at[FAR : FAR + FLAT], sems.at[4]),
        pltpu.make_async_copy(mass, local.at[FAR + FLAT : CHANNELS - 1], sems.at[5]),
        pltpu.make_async_copy(pore, local.at[CHANNELS - 1], sems.at[6]),
    ]
    for copy in copies:
        copy.start()
    copies[0].wait()
    copies[1].wait()
    local[3:5] = flags[...].astype(f32)
    for copy in copies[2:]:
        copy.wait()

    per, groups = groups_of(planes, depth)
    even = parity_of(axis)
    lane = lanes_of((8, depth))

    @pl.loop(0, rows // 8)
    def _(tile):
        span = pl.ds(pl.multiple_of(8 * tile, 8), 8)
        for group in range(groups):
            high = jnp.zeros((8, depth), f32)
            low = jnp.zeros((8, depth), f32)
            for c in range(group * per, min(CHANNELS, group * per + per)):
                for x in range(planes):
                    base = (c % per) * span_of(planes) + 2 * W * x
                    values = local[c, x, span, :]
                    here = (lane >= base + W) & (lane < base + 2 * W)
                    high = jnp.where(here, pltpu.roll(values, (base + 2 * W) % depth, 1), high)
                    here = (lane >= base) & (lane < base + W)
                    low = jnp.where(here, pltpu.roll(values, base % depth, 1), low)
            first[group, span, :] = pick(even, high, low)
            second[group, span, :] = pick(even, low, high)


def pack_x(axis, local, *outs):
    planes = local.shape[1]
    even = parity_of(axis)
    for out, up in zip(outs, (even == 0, even != 0)):
        near = jnp.where(up, planes - NEAR, 0)
        far = jnp.where(up, planes - W, W - 1)
        for c in range(CHANNELS):
            for q in range(NEAR):
                out[c * NEAR + q] = local[c, near + q]
            if c < FAR:
                out[CHANNELS * NEAR + c] = local[c, far]


def join_x(za, zb, a_in, b_in, a_out, b_out, columns, sems):
    columns[...] = za[...] + zb[...]
    copies = [
        pltpu.make_async_copy(columns, out.at[pl.ds(XMAIN, columns.shape[0])], sems.at[n])
        for n, out in enumerate((a_out, b_out))
    ]
    for copy in copies:
        copy.start()
    for copy in copies:
        copy.wait()


def put_rows(outs, n, values, even):
    head, tail = values[:W], values[values.shape[0] - W :]
    for out, up, down in zip(outs, (tail, head), (head, tail)):
        out[n] = pick(even, up, down)


def pack_y(axis, local, *outs):
    planes = local.shape[1]
    even = parity_of(axis)
    for c in range(CHANNELS):
        for x in range(planes):
            put_rows(outs, c * planes + x, local[c, x], even)


def join_y(axis, x_axis, count, planes, za, zb, xa, xb, *refs):
    outs, columns = refs[count : 2 * count], refs[2 * count]
    stages, sems = refs[2 * count + 1 : 3 * count + 1], refs[3 * count + 1]
    rows, depth = xa.shape[1:]
    even = parity_of(axis)
    even_x = parity_of(x_axis)
    per, _ = groups_of(planes, depth)
    lane = lanes_of((rows, depth))
    for c in range(CHANNELS):
        group, base = c // per, (c % per) * span_of(planes)
        a, b = xa[XMAIN + group], xb[XMAIN + group]
        own = pltpu.roll(za[group] + zb[group], (2 * W * W - base) % depth, 1)
        below = pltpu.roll(pick(even_x, b, a), (depth - base - 2 * W * (planes - W)) % depth, 1)
        above = pltpu.roll(pick(even_x, a, b), (2 * W * (planes + W) - base) % depth, 1)
        values = jnp.where(lane < 2 * W * W, below, jnp.where(lane < 2 * W * (W + planes), own, above))
        columns[c] = values
        put_rows(stages, 2 * XMAIN + c, values, even)

    @pl.loop(0, XMAIN // 4)
    def _(i):
        for j in range(4):
            n = 4 * i + j
            a, b = xa[n], xb[n]
            put_rows(stages, n, pick(even_x, b, a), even)
            put_rows(stages, XMAIN + n, pick(even_x, a, b), even)

    copies = [
        pltpu.make_async_copy(
            stage, out.at[pl.ds(CHANNELS * planes, 2 * XMAIN + CHANNELS)], sems.at[i]
        )
        for i, (stage, out) in enumerate(zip(stages, outs))
    ]
    for copy in copies:
        copy.start()
    for copy in copies:
        copy.wait()


PRESS, MOB, SLOPE, ACT = 0, 1, 4, 7
SHIFTED = 8


def z_shift(values, columns, plane, step):
    depth = values.shape[-1]
    lane = lanes_of(values.shape)
    if step > 0:
        edge = pltpu.roll(columns, depth - 1 - 2 * W * plane, 1)
        return jnp.where(lane == depth - 1, edge, pltpu.roll(values, depth - 1, 1))
    edge = pltpu.roll(columns, depth - 2 * W * plane - 2 * W + 1, 1)
    return jnp.where(lane == 0, edge, pltpu.roll(values, 1, 1))


def z_shift_columns(values, step):
    return pltpu.roll(values, values.shape[-1] - 1 if step > 0 else 1, 1)


def z_edge(current, values, plane, step):
    lane = lanes_of(values.shape)
    if step > 0:
        at = 2 * W * plane + 2 * W - 1
        return jnp.where(lane == at, pltpu.roll(values, at, 1), current)
    at = 2 * W * plane
    return jnp.where(lane == at, pltpu.roll(values, at + 1, 1), current)


def fill_tables(tables, tabs):
    lane = lanes_of(tabs.shape[1:])
    for n, table in enumerate(tables):
        for c in range(3):
            values = jnp.full(tabs.shape[1:], table[c, 0], f32)
            for level in range(1, table.shape[1]):
                values = jnp.where(lane == level, table[c, level], values)
            tabs[3 * n + c] = values


def properties(get, plane, is_columns, first, tabs, arrays):
    fields, lower, half, weight, accum, centre = arrays
    total = fields.shape[2] - 1
    span = pl.ds(first, 8)
    press, water, gas, active, region = (get(c) for c in range(5))
    index = region.astype(jnp.int32)
    look = [
        jnp.take_along_axis(tabs[n], index, axis=1, mode="promise_in_bounds") for n in range(9)
    ]
    formation, compress, viscous = look[:3], look[3:6], look[6:]
    sat = (water, 1.0 - water - gas, gas)
    expand = [formation[c] * jnp.exp(compress[c] * (press - 0.5)) for c in range(3)]
    mob = [viscous[c] * expand[c] * sat[c] * sat[c] for c in range(3)]
    pore = get(CHANNELS - 1)
    stored = pore * (compress[0] * sat[0] + compress[1] * sat[1] + compress[2] * sat[2])
    stored = jnp.where(active > 0, stored, 1.0)
    for c in range(3):
        weight[c, plane, span, :] = active / (expand[c] * stored)
        accum[c, plane, span, :] = pore * expand[c] * sat[c] - get(FAR + FLAT + c)
    one = [press] + mob + [compress[c] * mob[c] for c in range(3)] + [active]
    for f, values in enumerate(one):
        fields[f, 1, plane, span, :] = values
        for step in (-1, 1):
            if is_columns:
                fields[f, step + 1, plane, span, :] = z_shift_columns(values, step)
            else:
                columns = fields[f, 1, total, span, :]
                fields[f, step + 1, plane, span, :] = z_shift(values, columns, plane, step)
                current = fields[f, step + 1, total, span, :]
                fields[f, step + 1, total, span, :] = z_edge(current, values, plane, step)
    for k, offset in enumerate(upper_offsets):
        values = 0.5 * get(t_channel(k))
        half[k, plane, span, :] = values
        values = values * active
        step = -offset[2]
        if step == 0:
            lower[k, plane, span, :] = values
        elif is_columns:
            centre[k, span, :] = values
            lower[k, plane, span, :] = z_shift_columns(values, step)
        else:
            lower[k, plane, span, :] = z_shift(values, centre[k, span, :], plane, step)
            current = lower[k, total, span, :]
            lower[k, total, span, :] = z_edge(current, values, plane, step)


def x_roll(values, step, is_columns):
    if not is_columns or step == 0:
        return values
    depth = values.shape[-1]
    return pltpu.roll(values, (depth - 2 * W * step) % depth, 1)


def link_cells(plane, is_columns, first, stride, arrays, out, coupling, scale, start):
    fields, lower, half, weight, accum, _ = arrays
    depth = fields.shape[-1]
    here = (0, 0, 0)

    def read(ref, lead, offset):
        dx = 0 if is_columns else offset[0]
        values = ref[(*lead, plane + dx, pl.ds(first + stride * offset[1], 8), slice(None))]
        return x_roll(values, offset[0], is_columns)

    def at(f, offset):
        return read(fields, (f, offset[2] + 1), offset)

    press = at(PRESS, here)
    w = [read(weight, (c,), here) for c in range(3)]
    mob = [at(MOB + c, here) for c in range(3)]
    own_mob = w[0] * mob[0] + w[1] * mob[1] + w[2] * mob[2]
    own_slope = w[0] * at(SLOPE, here) + w[1] * at(SLOPE + 1, here) + w[2] * at(SLOPE + 2, here)
    flux = [jnp.zeros((8, depth), f32) for _ in range(3)]
    drops = jnp.zeros((8, depth), f32)
    means = jnp.ones((8, depth), f32)
    for n, offset in enumerate(neighbour_offsets):
        if offset > here:
            link = read(half, (upper_offsets.index(offset),), here) * at(ACT, offset)
        else:
            k = upper_offsets.index(tuple(-o for o in offset))
            link = read(lower, (k,), offset)
        drop = link * (press - at(PRESS, offset))
        other = [at(MOB + c, offset) for c in range(3)]
        for c in range(3):
            flux[c] = flux[c] + drop * other[c]
        drops = drops + drop
        mean = link * (own_mob + (w[0] * other[0] + w[1] * other[1] + w[2] * other[2]))
        slope = (
            w[0] * at(SLOPE, offset) + w[1] * at(SLOPE + 1, offset) + w[2] * at(SLOPE + 2, offset)
        )
        means = means + mean
        coupling[n, plane, out, :] = drop * slope - mean
    active = at(ACT, here)
    res = [
        active * (read(accum, (c,), here) + (flux[c] + mob[c] * drops)) for c in range(3)
    ]
    rate = relax_weight / (means + own_slope * drops)
    scale[plane, out, :] = rate
    start[plane, out, :] = -rate * (w[0] * res[0] + w[1] * res[1] + w[2] * res[2])
    return res


def inner(x_axis, local, columns, xa, xb, *refs):
    tables, (coupling, scale, start, store) = refs[:3], refs[3:7]
    tabs, arrays = refs[7], refs[8:]
    planes, rows, depth = local.shape[1:]
    total = planes + 2 * W
    even_x = parity_of(x_axis)
    fill_tables(tables, tabs)
    tiles = range(rows // 8)

    def cells(get, plane, is_columns=False):
        for tile in tiles:
            span = slice(8 * tile, 8 * tile + 8)
            properties(lambda c: get(c, span), plane, is_columns, 8 + 8 * tile, tabs, arrays)

    cells(lambda c, span: columns[c, span, :], total, True)

    @pl.loop(0, planes)
    def _(x):
        cells(lambda c, span: local[c, x, span, :], W + x)

    def from_x(n, low):
        a, b = xa, xb
        def get(c, span):
            i = n(c)
            if i is None:
                return jnp.zeros((8, depth), f32)
            u, v = xa[i, span, :], xb[i, span, :]
            return pick(even_x, v, u) if low else pick(even_x, u, v)
        return get

    @pl.loop(0, NEAR)
    def _(q):
        near = lambda c: c * NEAR + q
        cells(from_x(near, True), 1 + q)
        cells(from_x(near, False), W + planes + q)

    far = lambda c: CHANNELS * NEAR + c if c < FAR else None
    cells(from_x(far, True), 0)
    cells(from_x(far, False), total - 1)

    def links(plane, is_columns=False):
        for tile in tiles:
            out = slice(8 * tile, 8 * tile + 8)
            res = link_cells(
                plane, is_columns, 8 + 8 * tile, 1, arrays, out, coupling, scale, start
            )
            if not is_columns:
                for c in range(3):
                    store[c, plane, out, :] = res[c]

    links(total, True)

    @pl.loop(1, total - 1)
    def _(plane):
        links(plane)


RING = 2 * (W + 2)


def finish(axes, count_y, local, columns, xa, xb, *refs):
    tables = refs[:3]
    ys = refs[3 : 3 + count_y]
    coupling, scale, start, store, residual, update = refs[3 + count_y : 9 + count_y]
    tabs, raw, edge_coupling, edge_scale, edge_start, edge_store, sol, edge_sol = refs[
        9 + count_y : 17 + count_y
    ]
    arrays = refs[17 + count_y :]
    planes, rows, depth = local.shape[1:]
    total = planes + 2 * W
    even_x, even_y, _ = (parity_of(axis) for axis in axes)
    fill_tables(tables, tabs)

    def put(c, plane, values, n):
        low = high = jnp.zeros((W, depth), f32)
        if count_y:
            a = ys[0][n]
            b = ys[1][n] if count_y > 1 else None
            low, high = pick(even_y, b, a), pick(even_y, a, b)
        raw[c, plane, pl.ds(0, 2, stride=2), :] = values[rows - 2 :]
        raw[c, plane, pl.ds(4, W, stride=2), :] = high
        raw[c, plane, pl.ds(1, W, stride=2), :] = low
        raw[c, plane, pl.ds(RING - 3, 2, stride=2), :] = values[:2]
        raw[c, plane, RING:16, :] = jnp.zeros((16 - RING, depth), f32)

    base = CHANNELS * planes

    @pl.loop(0, CHANNELS)
    def _(c):
        for x in range(planes):
            put(c, W + x, local[c, x], c * planes + x)
        for q in range(NEAR):
            n = c * NEAR + q
            a, b = xa[n], xb[n]
            put(c, 1 + q, pick(even_x, b, a), base + n)
            put(c, W + planes + q, pick(even_x, a, b), base + XMAIN + n)
        put(c, total, columns[c], base + 2 * XMAIN + c)

    @pl.loop(0, FAR)
    def _(c):
        n = CHANNELS * NEAR + c
        a, b = xa[n], xb[n]
        put(c, 0, pick(even_x, b, a), base + n)
        put(c, total - 1, pick(even_x, a, b), base + XMAIN + n)

    for c in range(FAR, CHANNELS):
        for plane in (0, total - 1):
            raw[c, plane] = jnp.zeros((16, depth), f32)

    def cells(plane, is_columns=False):
        for tile in range(2):
            span = slice(8 * tile, 8 * tile + 8)
            properties(
                lambda c: raw[c, plane, span, :], plane, is_columns, 8 * tile, tabs, arrays
            )

    cells(total, True)

    @pl.loop(0, total)
    def _(plane):
        cells(plane)

    def links(plane, is_columns=False):
        res = link_cells(
            plane, is_columns, 2, 2, arrays, slice(0, 8), edge_coupling, edge_scale, edge_start
        )
        if not is_columns:
            for c in range(3):
                edge_store[c, plane] = res[c]

    links(total, True)

    @pl.loop(1, total - 1)
    def _(plane):
        links(plane)

    tiles = rows // 8

    def put_rows_of(slot, step, plane, mains, edge):
        to = lambda row: (slot, step + 1, plane, slice(row, row + 1), slice(None))
        for tile, values in enumerate(mains):
            sol[slot, step + 1, plane, 8 + 8 * tile : 16 + 8 * tile, :] = values
        edge_sol[slot, step + 1, plane, 2:10, :] = edge
        sol[to(7)] = edge[5:6]
        sol[to(8)] = edge[7:8]
        sol[to(7 + rows)] = edge[0:1]
        sol[to(8 + rows)] = edge[2:3]
        edge_sol[to(0)] = mains[-1][6:7]
        edge_sol[to(RING - 1)] = mains[0][1:2]

    def parts_of(slot, step, plane):
        mains = [
            sol[slot, step + 1, plane, 8 + 8 * tile : 16 + 8 * tile, :] for tile in range(tiles)
        ]
        return mains, edge_sol[slot, step + 1, plane, 2:10, :]

    def put_solution(slot, plane, mains, edge, is_columns=False):
        put_rows_of(slot, 0, plane, mains, edge)
        for step in (-1, 1):
            if is_columns:
                shift = lambda values: z_shift_columns(values, step)
                put_rows_of(slot, step, plane, [shift(values) for values in mains], shift(edge))
                continue
            column_mains, column_edge = parts_of(slot, 0, total)
            put_rows_of(
                slot,
                step,
                plane,
                [z_shift(u, v, plane, step) for u, v in zip(mains, column_mains)],
                z_shift(edge, column_edge, plane, step),
            )
            own_mains, own_edge = parts_of(slot, 0, plane)
            column_mains, column_edge = parts_of(slot, step, total)
            put_rows_of(
                slot,
                step,
                total,
                [z_edge(u, v, plane, step) for u, v in zip(column_mains, own_mains)],
                z_edge(column_edge, own_edge, plane, step),
            )

    def relaxed(slot, plane, tile, is_columns=False):
        if tile is None:
            ref, first, stride, out = edge_sol, 2, 2, slice(0, 8)
            factors = (edge_coupling, edge_scale, edge_start)
        else:
            ref, first, stride, out = sol, 8 + 8 * tile, 1, slice(8 * tile, 8 * tile + 8)
            factors = (coupling, scale, start)

        def get(offset):
            dx = 0 if is_columns else offset[0]
            values = ref[slot, offset[2] + 1, plane + dx, pl.ds(first + stride * offset[1], 8), :]
            return x_roll(values, offset[0], is_columns)

        parts = [jnp.zeros((8, depth), f32) for _ in range(2)]
        for n, offset in enumerate(neighbour_offsets):
            parts[n % 2] = parts[n % 2] + factors[0][n, plane, out, :] * get(offset)
        return (
            (1.0 - relax_weight) * get((0, 0, 0))
            + factors[2][plane, out, :]
            - factors[1][plane, out, :] * (parts[0] + parts[1])
        )

    def first_sweep(plane, is_columns=False):
        mains = [start[plane, 8 * tile : 8 * tile + 8, :] for tile in range(tiles)]
        put_solution(0, plane, mains, edge_start[plane], is_columns)

    first_sweep(total, True)

    @pl.loop(1, total - 1)
    def _(plane):
        first_sweep(plane)

    def sweep_of(slot, plane, is_columns=False):
        mains = [relaxed(slot, plane, tile, is_columns) for tile in range(tiles)]
        put_solution(1 - slot, plane, mains, relaxed(slot, plane, None, is_columns), is_columns)

    for sweep in range(2, SWEEPS):
        slot = sweep % 2
        sweep_of(slot, total, True)

        @pl.loop(sweep, total - sweep)
        def _(plane):
            sweep_of(slot, plane)

    @pl.loop(0, planes)
    def _(x):
        slot, plane = SWEEPS % 2, W + x
        edge = relaxed(slot, plane, None)
        for tile in range(tiles):
            span = slice(8 * tile, 8 * tile + 8)
            update[x, span, :] = relaxed(slot, plane, tile)
            for c in range(3):
                residual[c, x, span, :] = store[c, plane, span, :]
        update[x, 0:1, :] = edge[7:8]
        update[x, rows - 1 : rows, :] = edge[0:1]
        for c in range(3):
            residual[c, x, 0:1, :] = edge_store[c, plane, 7:8, :]
            residual[c, x, rows - 1 : rows, :] = edge_store[c, plane, 0:1, :]


def call(kernel, name, mib, **options):
    return pl.pallas_call(
        kernel,
        name=name,
        compiler_params=pltpu.CompilerParams(vmem_limit_bytes=mib << 20),
        **options,
    )


def cell_arrays(total, height, depth):
    return [
        pltpu.VMEM((SHIFTED, 3, total + 1, height, depth), f32),
        pltpu.VMEM((UP, total + 1, height, depth), f32),
        pltpu.VMEM((UP, total + 1, height, depth), f32),
        pltpu.VMEM((3, total + 1, height, depth), f32),
        pltpu.VMEM((3, total + 1, height, depth), f32),
        pltpu.VMEM((UP, height, depth), f32),
    ]


def body(
    cell_state,
    old_mass,
    pore_volume,
    transmissibility,
    active_mask,
    pvt_region,
    formation_factor,
    compressibility,
    inverse_viscosity,
):
    ax, ay, az = "gx", "gy", "gz"
    planes, rows, depth = pore_volume.shape
    total = planes + 2 * W
    per, groups = groups_of(planes, depth)
    assert per >= 1 and 2 * W * total <= depth and rows % 8 == 0 and RING <= 16
    tables = (formation_factor, compressibility, inverse_viscosity)
    like = lambda *shape: jax.ShapeDtypeStruct(shape, f32)
    fill = lambda shape, got: [jnp.zeros(shape.shape, f32) if one is None else one for one in got]

    z_shape = like(groups, rows, depth)
    local, *z_send = call(
        functools.partial(pack_z, az),
        "pack_z",
        8,
        out_shape=(like(CHANNELS, planes, rows, depth), z_shape, z_shape),
        in_specs=[ANY] * 6,
        out_specs=(VMEM,) * 3,
        scratch_shapes=[
            pltpu.VMEM((2, planes, rows, depth), jnp.int32),
            pltpu.SemaphoreType.DMA((7,)),
        ],
    )(cell_state, old_mass, pore_volume, transmissibility, active_mask, pvt_region)
    za, zb = fill(z_shape, swaps(az, *z_send))

    x_shape = like(XMAIN + groups, rows, depth)
    x_send = call(
        functools.partial(pack_x, ax), "pack_x", 8, out_shape=(x_shape, x_shape)
    )(local)
    x_send = call(
        join_x,
        "join_x",
        8,
        out_shape=(x_shape, x_shape),
        in_specs=[VMEM, VMEM, ANY, ANY],
        out_specs=(ANY, ANY),
        scratch_shapes=[pltpu.VMEM(z_shape.shape, f32), pltpu.SemaphoreType.DMA((2,))],
        input_output_aliases={2: 0, 3: 1},
    )(za, zb, *x_send)
    xa, xb = fill(x_shape, swaps(ax, *x_send))

    count_y = min(lax.axis_size(ay) - 1, 2)
    extra = 2 * XMAIN + CHANNELS
    y_shape = like(CHANNELS * planes + extra, W, depth)
    y_send = ()
    if count_y:
        y_send = call(
            functools.partial(pack_y, ay), "pack_y", 8, out_shape=(y_shape,) * count_y
        )(local)
    *y_send, columns = call(
        functools.partial(join_y, ay, ax, count_y, planes),
        "join_y",
        8,
        out_shape=(y_shape,) * count_y + (like(CHANNELS, rows, depth),),
        in_specs=[VMEM] * 4 + [ANY] * count_y,
        out_specs=(ANY,) * count_y + (VMEM,),
        scratch_shapes=[pltpu.VMEM((extra, W, depth), f32)] * count_y
        + [pltpu.SemaphoreType.DMA((max(count_y, 1),))],
        input_output_aliases={4 + i: i for i in range(count_y)},
    )(za, zb, xa, xb, *y_send)
    ys = swaps(ay, y_send[0], y_send[-1])[:count_y] if count_y else []

    smem = pl.BlockSpec(memory_space=pltpu.SMEM)
    tabs = pltpu.VMEM((9, 8, depth), f32)
    halves = call(
        functools.partial(inner, ax),
        "inner",
        24,
        out_shape=(
            like(2 * UP, total + 1, rows, depth),
            like(total + 1, rows, depth),
            like(total + 1, rows, depth),
            like(3, total, rows, depth),
        ),
        in_specs=[VMEM] * 4 + [smem] * 3,
        out_specs=(VMEM,) * 4,
        scratch_shapes=[tabs] + cell_arrays(total, rows + 16, depth),
    )(local, columns, xa, xb, *tables)

    return call(
        functools.partial(finish, (ax, ay, az), count_y),
        "finish",
        24,
        out_shape=(like(3, planes, rows, depth), like(planes, rows, depth)),
        in_specs=[VMEM] * 4 + [smem] * 3 + [VMEM] * (count_y + 4),
        out_specs=(VMEM, VMEM),
        scratch_shapes=[
            tabs,
            pltpu.VMEM((CHANNELS, total + 1, 16, depth), f32),
            pltpu.VMEM((2 * UP, total + 1, 8, depth), f32),
            pltpu.VMEM((total + 1, 8, depth), f32),
            pltpu.VMEM((total + 1, 8, depth), f32),
            pltpu.VMEM((3, total, 8, depth), f32),
            pltpu.VMEM((2, 3, total + 1, rows + 16, depth), f32),
            pltpu.VMEM((2, 3, total + 1, 16, depth), f32),
        ]
        + cell_arrays(total, 16, depth),
    )(local, columns, xa, xb, *tables, *ys, *halves)


def solution(mesh):
    return jax.shard_map(
        body,
        mesh=mesh,
        in_specs=(
            P(None, "gx", "gy", "gz"),
            P(None, "gx", "gy", "gz"),
            P("gx", "gy", "gz"),
            P(None, "gx", "gy", "gz"),
            P("gx", "gy", "gz"),
            P("gx", "gy", "gz"),
            P(),
            P(),
            P(),
        ),
        out_specs=(P(None, "gx", "gy", "gz"), P("gx", "gy", "gz")),
        check_vma=False,
    )
```

```python
import functools

import jax
import jax.numpy as jnp
from jax import lax
from jax.experimental import pallas as pl
from jax.experimental.pallas import tpu as pltpu
from jax.sharding import PartitionSpec as P

SWEEPS = 4
W = SWEEPS
relax_weight = 0.7

neighbour_offsets = [
    (along_x, along_y, along_z)
    for along_x in (-1, 0, 1)
    for along_y in (-1, 0, 1)
    for along_z in (-1, 0, 1)
    if (along_x, along_y, along_z) != (0, 0, 0)
]
upper_offsets = [offset for offset in neighbour_offsets if offset > (0, 0, 0)]
UP = len(upper_offsets)
FLAT = sum(1 for offset in upper_offsets if offset[0] == 0)
STEP = UP - FLAT

FAR = 5 + STEP
CHANNELS = FAR + FLAT + 4
NEAR = W - 1
XMAIN = CHANNELS * NEAR + FAR
VMEM = pl.BlockSpec(memory_space=pltpu.VMEM)
ANY = pl.BlockSpec(memory_space=pl.ANY)
HBM = pl.BlockSpec(memory_space=pltpu.MemorySpace.HBM)
f32 = jnp.float32


def t_channel(k):
    return FAR + k if k < FLAT else 5 + k - FLAT


def pick(parity, even, odd):
    shape = (even if odd is None else odd).shape
    if even is None:
        even = jnp.zeros(shape, f32)
    if odd is None:
        odd = jnp.zeros(shape, f32)
    return jnp.where(jnp.full(shape, parity, jnp.int32) == 0, even, odd)


def parity_of(axis):
    return lax.rem(lax.axis_index(axis), 2)


def swaps(axis, first, second):
    count = lax.axis_size(axis)
    got = []
    for start, message in ((0, first), (1, second)):
        pairs = [(i, i + 1) for i in range(start, count - 1, 2)]
        if not pairs:
            got.append(None)
            continue
        got.append(lax.ppermute(message, axis, pairs + [(b, a) for a, b in pairs]))
    return got


def lanes_of(shape):
    return lax.broadcasted_iota(jnp.int32, shape, len(shape) - 1)


def span_of(planes):
    return 2 * W * planes


def groups_of(planes, depth):
    per = depth // span_of(planes)
    return per, -(-CHANNELS // per)


def pack_z(axis, *refs):
    state, mass, pore, trans, active, region, local, first, second, flags, sems = refs
    planes, rows, depth = pore.shape
    copies = [
        pltpu.make_async_copy(active, flags.at[0], sems.at[0]),
        pltpu.make_async_copy(region, flags.at[1], sems.at[1]),
        pltpu.make_async_copy(state, local.at[0:3], sems.at[2]),
        pltpu.make_async_copy(trans.at[FLAT:UP], local.at[5:FAR], sems.at[3]),
        pltpu.make_async_copy(trans.at[0:FLAT], local.at[FAR : FAR + FLAT], sems.at[4]),
        pltpu.make_async_copy(mass, local.at[FAR + FLAT : CHANNELS - 1], sems.at[5]),
        pltpu.make_async_copy(pore, local.at[CHANNELS - 1], sems.at[6]),
    ]
    for copy in copies:
        copy.start()
    copies[0].wait()
    copies[1].wait()
    local[3:5] = flags[...].astype(f32)
    for copy in copies[2:]:
        copy.wait()

    per, groups = groups_of(planes, depth)
    even = parity_of(axis)
    lane = lanes_of((8, depth))

    @pl.loop(0, rows // 8)
    def _(tile):
        span = pl.ds(pl.multiple_of(8 * tile, 8), 8)
        for group in range(groups):
            high = jnp.zeros((8, depth), f32)
            low = jnp.zeros((8, depth), f32)
            for c in range(group * per, min(CHANNELS, group * per + per)):
                for x in range(planes):
                    base = (c % per) * span_of(planes) + 2 * W * x
                    values = local[c, x, span, :]
                    here = (lane >= base + W) & (lane < base + 2 * W)
                    high = jnp.where(here, pltpu.roll(values, (base + 2 * W) % depth, 1), high)
                    here = (lane >= base) & (lane < base + W)
                    low = jnp.where(here, pltpu.roll(values, base % depth, 1), low)
            first[group, span, :] = pick(even, high, low)
            second[group, span, :] = pick(even, low, high)


def pack_x(axis, local, *outs):
    planes = local.shape[1]
    even = parity_of(axis)
    for out, up in zip(outs, (even == 0, even != 0)):
        near = jnp.where(up, planes - NEAR, 0)
        far = jnp.where(up, planes - W, W - 1)
        for c in range(CHANNELS):
            for q in range(NEAR):
                out[c * NEAR + q] = local[c, near + q]
            if c < FAR:
                out[CHANNELS * NEAR + c] = local[c, far]


def join_x(za, zb, a_in, b_in, a_out, b_out, columns, sems):
    columns[...] = za[...] + zb[...]
    copies = [
        pltpu.make_async_copy(columns, out.at[pl.ds(XMAIN, columns.shape[0])], sems.at[n])
        for n, out in enumerate((a_out, b_out))
    ]
    for copy in copies:
        copy.start()
    for copy in copies:
        copy.wait()


def put_rows(outs, n, values, even):
    head, tail = values[:W], values[values.shape[0] - W :]
    for out, up, down in zip(outs, (tail, head), (head, tail)):
        out[n] = pick(even, up, down)


def pack_y(axis, local, *outs):
    planes = local.shape[1]
    even = parity_of(axis)
    for c in range(CHANNELS):
        for x in range(planes):
            put_rows(outs, c * planes + x, local[c, x], even)


def join_y(axis, x_axis, count, planes, za, zb, xa, xb, *refs):
    outs, columns = refs[count : 2 * count], refs[2 * count]
    stages, sems = refs[2 * count + 1 : 3 * count + 1], refs[3 * count + 1]
    rows, depth = xa.shape[1:]
    even = parity_of(axis)
    even_x = parity_of(x_axis)
    per, _ = groups_of(planes, depth)
    lane = lanes_of((rows, depth))
    for c in range(CHANNELS):
        group, base = c // per, (c % per) * span_of(planes)
        a, b = xa[XMAIN + group], xb[XMAIN + group]
        own = pltpu.roll(za[group] + zb[group], (2 * W * W - base) % depth, 1)
        below = pltpu.roll(pick(even_x, b, a), (depth - base - 2 * W * (planes - W)) % depth, 1)
        above = pltpu.roll(pick(even_x, a, b), (2 * W * (planes + W) - base) % depth, 1)
        values = jnp.where(lane < 2 * W * W, below, jnp.where(lane < 2 * W * (W + planes), own, above))
        columns[c] = values
        put_rows(stages, 2 * XMAIN + c, values, even)

    @pl.loop(0, XMAIN // 4)
    def _(i):
        for j in range(4):
            n = 4 * i + j
            a, b = xa[n], xb[n]
            put_rows(stages, n, pick(even_x, b, a), even)
            put_rows(stages, XMAIN + n, pick(even_x, a, b), even)

    copies = [
        pltpu.make_async_copy(
            stage, out.at[pl.ds(CHANNELS * planes, 2 * XMAIN + CHANNELS)], sems.at[i]
        )
        for i, (stage, out) in enumerate(zip(stages, outs))
    ]
    for copy in copies:
        copy.start()
    for copy in copies:
        copy.wait()


PRESS, MOB, SLOPE, ACT = 0, 1, 4, 7
SHIFTED = 8


def z_shift(values, columns, plane, step):
    depth = values.shape[-1]
    lane = lanes_of(values.shape)
    if step > 0:
        edge = pltpu.roll(columns, depth - 1 - 2 * W * plane, 1)
        return jnp.where(lane == depth - 1, edge, pltpu.roll(values, depth - 1, 1))
    edge = pltpu.roll(columns, depth - 2 * W * plane - 2 * W + 1, 1)
    return jnp.where(lane == 0, edge, pltpu.roll(values, 1, 1))


def z_shift_columns(values, step):
    return pltpu.roll(values, values.shape[-1] - 1 if step > 0 else 1, 1)


def z_edge(current, values, plane, step):
    lane = lanes_of(values.shape)
    if step > 0:
        at = 2 * W * plane + 2 * W - 1
        return jnp.where(lane == at, pltpu.roll(values, at, 1), current)
    at = 2 * W * plane
    return jnp.where(lane == at, pltpu.roll(values, at + 1, 1), current)


def fill_tables(tables, tabs):
    lane = lanes_of(tabs.shape[1:])
    for n, table in enumerate(tables):
        for c in range(3):
            values = jnp.full(tabs.shape[1:], table[c, 0], f32)
            for level in range(1, table.shape[1]):
                values = jnp.where(lane == level, table[c, level], values)
            tabs[3 * n + c] = values


def properties(get, plane, is_columns, first, tabs, arrays, halo):
    fields, lower, half, weight, accum, _ = halo if is_columns else arrays
    halo_fields, halo_lower, centre = halo[0], halo[1], halo[5]
    span = pl.ds(first, 8)
    press, water, gas, active, region = (get(c) for c in range(5))
    index = region.astype(jnp.int32)
    look = [
        jnp.take_along_axis(tabs[n], index, axis=1, mode="promise_in_bounds") for n in range(9)
    ]
    formation, compress, viscous = look[:3], look[3:6], look[6:]
    sat = (water, 1.0 - water - gas, gas)
    expand = [formation[c] * jnp.exp(compress[c] * (press - 0.5)) for c in range(3)]
    mob = [viscous[c] * expand[c] * sat[c] * sat[c] for c in range(3)]
    pore = get(CHANNELS - 1)
    stored = pore * (compress[0] * sat[0] + compress[1] * sat[1] + compress[2] * sat[2])
    stored = jnp.where(active > 0, stored, 1.0)
    for c in range(3):
        weight[c, plane, span, :] = active / (expand[c] * stored)
        accum[c, plane, span, :] = pore * expand[c] * sat[c] - get(FAR + FLAT + c)
    one = [press] + mob + [compress[c] * mob[c] for c in range(3)] + [active]
    for f, values in enumerate(one):
        fields[f, 1, plane, span, :] = values
        for step in (-1, 1):
            if is_columns:
                fields[f, step + 1, plane, span, :] = z_shift_columns(values, step)
            else:
                columns = halo_fields[f, 1, 0, span, :]
                fields[f, step + 1, plane, span, :] = z_shift(values, columns, plane, step)
                current = halo_fields[f, step + 1, 0, span, :]
                halo_fields[f, step + 1, 0, span, :] = z_edge(current, values, plane, step)
    for k, offset in enumerate(upper_offsets):
        values = 0.5 * get(t_channel(k))
        half[k, plane, span, :] = values
        values = values * active
        step = -offset[2]
        if step == 0:
            lower[k, plane, span, :] = values
        elif is_columns:
            centre[k, span, :] = values
            lower[k, plane, span, :] = z_shift_columns(values, step)
        else:
            lower[k, plane, span, :] = z_shift(values, centre[k, span, :], plane, step)
            current = halo_lower[k, 0, span, :]
            halo_lower[k, 0, span, :] = z_edge(current, values, plane, step)


def x_roll(values, step, is_columns):
    if not is_columns or step == 0:
        return values
    depth = values.shape[-1]
    return pltpu.roll(values, (depth - 2 * W * step) % depth, 1)


def link_cells(plane, is_columns, first, stride, arrays, out, results):
    fields, lower, half, weight, accum, _ = arrays
    coupling, scale, start = results
    depth = fields.shape[-1]
    here = (0, 0, 0)

    def read(ref, lead, offset):
        dx = 0 if is_columns else offset[0]
        values = ref[(*lead, plane + dx, pl.ds(first + stride * offset[1], 8), slice(None))]
        return x_roll(values, offset[0], is_columns)

    def at(f, offset):
        return read(fields, (f, offset[2] + 1), offset)

    press = at(PRESS, here)
    w = [read(weight, (c,), here) for c in range(3)]
    mob = [at(MOB + c, here) for c in range(3)]
    own_mob = w[0] * mob[0] + w[1] * mob[1] + w[2] * mob[2]
    own_slope = w[0] * at(SLOPE, here) + w[1] * at(SLOPE + 1, here) + w[2] * at(SLOPE + 2, here)
    flux = [jnp.zeros((8, depth), f32) for _ in range(3)]
    drops = jnp.zeros((8, depth), f32)
    means = jnp.ones((8, depth), f32)
    for n, offset in enumerate(neighbour_offsets):
        if offset > here:
            link = read(half, (upper_offsets.index(offset),), here) * at(ACT, offset)
        else:
            k = upper_offsets.index(tuple(-o for o in offset))
            link = read(lower, (k,), offset)
        drop = link * (press - at(PRESS, offset))
        other = [at(MOB + c, offset) for c in range(3)]
        for c in range(3):
            flux[c] = flux[c] + drop * other[c]
        drops = drops + drop
        mean = link * (own_mob + (w[0] * other[0] + w[1] * other[1] + w[2] * other[2]))
        slope = (
            w[0] * at(SLOPE, offset) + w[1] * at(SLOPE + 1, offset) + w[2] * at(SLOPE + 2, offset)
        )
        means = means + mean
        coupling[n, plane, out, :] = drop * slope - mean
    active = at(ACT, here)
    res = [
        active * (read(accum, (c,), here) + (flux[c] + mob[c] * drops)) for c in range(3)
    ]
    rate = relax_weight / (means + own_slope * drops)
    scale[plane, out, :] = rate
    start[plane, out, :] = -rate * (w[0] * res[0] + w[1] * res[1] + w[2] * res[2])
    return res


def inner(x_axis, local, columns, xa, xb, *refs):
    tables, results, halo_results, store = refs[:3], refs[3:6], refs[6:9], refs[9]
    tabs, arrays, halo = refs[10], refs[11:17], refs[17:]
    planes, rows, depth = local.shape[1:]
    total = planes + 2 * W
    even_x = parity_of(x_axis)
    fill_tables(tables, tabs)
    tiles = range(rows // 8)

    def cells(get, plane, is_columns=False):
        for tile in tiles:
            span = slice(8 * tile, 8 * tile + 8)
            properties(lambda c: get(c, span), plane, is_columns, 8 + 8 * tile, tabs, arrays, halo)

    cells(lambda c, span: columns[c, span, :], 0, True)

    @pl.loop(0, planes)
    def _(x):
        cells(lambda c, span: local[c, x, span, :], W + x)

    def from_x(n, low):
        a, b = xa, xb
        def get(c, span):
            i = n(c)
            if i is None:
                return jnp.zeros((8, depth), f32)
            u, v = xa[i, span, :], xb[i, span, :]
            return pick(even_x, v, u) if low else pick(even_x, u, v)
        return get

    @pl.loop(0, NEAR)
    def _(q):
        near = lambda c: c * NEAR + q
        cells(from_x(near, True), 1 + q)
        cells(from_x(near, False), W + planes + q)

    far = lambda c: CHANNELS * NEAR + c if c < FAR else None
    cells(from_x(far, True), 0)
    cells(from_x(far, False), total - 1)

    def links(plane, is_columns=False):
        for tile in tiles:
            out = slice(8 * tile, 8 * tile + 8)
            own = (halo, out, halo_results) if is_columns else (arrays, out, results)
            res = link_cells(plane, is_columns, 8 + 8 * tile, 1, *own)
            if not is_columns:
                for c in range(3):
                    store[c, plane, out, :] = res[c]

    links(0, True)

    @pl.loop(1, total - 1)
    def _(plane):
        links(plane)


RING = 2 * (W + 2)


def finish(axes, count_y, local, columns, xa, xb, *refs):
    tables = refs[:3]
    ys = refs[3 : 3 + count_y]
    results, halo_results, store, residual, update = (
        refs[3 + count_y : 6 + count_y],
        refs[6 + count_y : 9 + count_y],
        *refs[9 + count_y : 12 + count_y],
    )
    refs = refs[12 + count_y :]
    tabs, raw, edge_store = refs[:3]
    edge_results, edge_halo_results = refs[3:6], refs[6:9]
    sol, halo_sol, edge_sol, edge_halo_sol = refs[9:13]
    arrays, halo = refs[13:19], refs[19:]
    planes, rows, depth = local.shape[1:]
    total = planes + 2 * W
    even_x, even_y, _ = (parity_of(axis) for axis in axes)
    fill_tables(tables, tabs)

    def put(c, plane, values, n):
        low = high = jnp.zeros((W, depth), f32)
        if count_y:
            a = ys[0][n]
            b = ys[1][n] if count_y > 1 else None
            low, high = pick(even_y, b, a), pick(even_y, a, b)
        raw[c, plane, pl.ds(0, 2, stride=2), :] = values[rows - 2 :]
        raw[c, plane, pl.ds(4, W, stride=2), :] = high
        raw[c, plane, pl.ds(1, W, stride=2), :] = low
        raw[c, plane, pl.ds(RING - 3, 2, stride=2), :] = values[:2]
        raw[c, plane, RING:16, :] = jnp.zeros((16 - RING, depth), f32)

    base = CHANNELS * planes

    @pl.loop(0, CHANNELS)
    def _(c):
        for x in range(planes):
            put(c, W + x, local[c, x], c * planes + x)
        for q in range(NEAR):
            n = c * NEAR + q
            a, b = xa[n], xb[n]
            put(c, 1 + q, pick(even_x, b, a), base + n)
            put(c, W + planes + q, pick(even_x, a, b), base + XMAIN + n)
        put(c, total, columns[c], base + 2 * XMAIN + c)

    @pl.loop(0, FAR)
    def _(c):
        n = CHANNELS * NEAR + c
        a, b = xa[n], xb[n]
        put(c, 0, pick(even_x, b, a), base + n)
        put(c, total - 1, pick(even_x, a, b), base + XMAIN + n)

    for c in range(FAR, CHANNELS):
        for plane in (0, total - 1):
            raw[c, plane] = jnp.zeros((16, depth), f32)

    def cells(plane, is_columns=False):
        for tile in range(2):
            span = slice(8 * tile, 8 * tile + 8)
            get = lambda c: raw[c, plane, span, :]
            properties(get, 0 if is_columns else plane, is_columns, 8 * tile, tabs, arrays, halo)

    cells(total, True)

    @pl.loop(0, total)
    def _(plane):
        cells(plane)

    def links(plane, is_columns=False):
        out = slice(0, 8)
        own = (halo, out, edge_halo_results) if is_columns else (arrays, out, edge_results)
        res = link_cells(plane, is_columns, 2, 2, *own)
        if not is_columns:
            for c in range(3):
                edge_store[c, plane] = res[c]

    links(0, True)

    @pl.loop(1, total - 1)
    def _(plane):
        links(plane)

    tiles = rows // 8

    row = lax.broadcasted_iota(jnp.int32, (8, depth), 0)

    def merged(mains, edge):
        first, last = pltpu.roll(edge, 1, 0), pltpu.roll(edge, 7, 0)
        mains = [jnp.where(row == 0, first, mains[0])] + mains[1:]
        return mains[:-1] + [jnp.where(row == 7, last, mains[-1])]

    def put_parts(is_columns, slot, step, plane, mains, edge):
        to, edge_to = (halo_sol, edge_halo_sol) if is_columns else (sol, edge_sol)
        for tile, values in enumerate(mains):
            to[slot, step + 1, plane, 8 + 8 * tile : 16 + 8 * tile, :] = values
        edge_to[slot, step + 1, plane, 2:10, :] = edge
        to[slot, step + 1, plane, 7:8, :] = edge[5:6]
        to[slot, step + 1, plane, 8 + rows : 9 + rows, :] = edge[2:3]
        edge_to[slot, step + 1, plane, 0:1, :] = mains[-1][6:7]
        edge_to[slot, step + 1, plane, RING - 1 : RING, :] = mains[0][1:2]

    def halo_parts(slot, step):
        mains = [
            halo_sol[slot, step + 1, 0, 8 + 8 * tile : 16 + 8 * tile, :] for tile in range(tiles)
        ]
        return mains, edge_halo_sol[slot, step + 1, 0, 2:10, :]

    def put_solution(slot, plane, mains, edge, is_columns=False):
        mains = merged(mains, edge)
        put_parts(is_columns, slot, 0, plane, mains, edge)
        for step in (-1, 1):
            if is_columns:
                shift = lambda values: z_shift_columns(values, step)
                put_parts(True, slot, step, plane, [shift(u) for u in mains], shift(edge))
                continue
            shift = lambda u, v: z_shift(u, v, plane, step)
            halo_mains, halo_edge = halo_parts(slot, 0)
            shifted = [shift(u, v) for u, v in zip(mains, halo_mains)]
            put_parts(False, slot, step, plane, shifted, shift(edge, halo_edge))
            shift = lambda u, v: z_edge(u, v, plane, step)
            halo_mains, halo_edge = halo_parts(slot, step)
            shifted = [shift(u, v) for u, v in zip(halo_mains, mains)]
            put_parts(True, slot, step, 0, shifted, shift(halo_edge, edge))

    def relaxed(slot, plane, tile, is_columns=False):
        if tile is None:
            ref, first, stride, out = (edge_halo_sol if is_columns else edge_sol), 2, 2, slice(0, 8)
            coupling, scale, start = edge_halo_results if is_columns else edge_results
        else:
            ref, first, stride = (halo_sol if is_columns else sol), 8 + 8 * tile, 1
            out = slice(8 * tile, 8 * tile + 8)
            coupling, scale, start = halo_results if is_columns else results

        def get(offset):
            dx = 0 if is_columns else offset[0]
            values = ref[slot, offset[2] + 1, plane + dx, pl.ds(first + stride * offset[1], 8), :]
            return x_roll(values, offset[0], is_columns)

        parts = [jnp.zeros((8, depth), f32) for _ in range(2)]
        for n, offset in enumerate(neighbour_offsets):
            parts[n % 2] = parts[n % 2] + coupling[n, plane, out, :] * get(offset)
        return (
            (1.0 - relax_weight) * get((0, 0, 0))
            + start[plane, out, :]
            - scale[plane, out, :] * (parts[0] + parts[1])
        )

    def first_sweep(plane, is_columns=False):
        start = (halo_results if is_columns else results)[2]
        edge = (edge_halo_results if is_columns else edge_results)[2]
        mains = [start[plane, 8 * tile : 8 * tile + 8, :] for tile in range(tiles)]
        put_solution(0, plane, mains, edge[plane], is_columns)

    first_sweep(0, True)

    @pl.loop(1, total - 1)
    def _(plane):
        first_sweep(plane)

    def sweep_of(slot, plane, is_columns=False):
        mains = [relaxed(slot, plane, tile, is_columns) for tile in range(tiles)]
        put_solution(1 - slot, plane, mains, relaxed(slot, plane, None, is_columns), is_columns)

    for sweep in range(2, SWEEPS):
        slot = sweep % 2
        sweep_of(slot, 0, True)

        @pl.loop(sweep, total - sweep)
        def _(plane):
            sweep_of(slot, plane)

    @pl.loop(0, planes)
    def _(x):
        slot, plane = SWEEPS % 2, W + x
        edge = relaxed(slot, plane, None)
        for tile in range(tiles):
            span = slice(8 * tile, 8 * tile + 8)
            update[x, span, :] = relaxed(slot, plane, tile)
            for c in range(3):
                residual[c, x, span, :] = store[c, plane, span, :]
        update[x, 0:1, :] = edge[7:8]
        update[x, rows - 1 : rows, :] = edge[0:1]
        for c in range(3):
            residual[c, x, 0:1, :] = edge_store[c, plane, 7:8, :]
            residual[c, x, rows - 1 : rows, :] = edge_store[c, plane, 0:1, :]


def call(kernel, name, mib, **options):
    return pl.pallas_call(
        kernel,
        name=name,
        compiler_params=pltpu.CompilerParams(vmem_limit_bytes=mib << 20),
        **options,
    )


def cell_arrays(total, height, depth):
    return [
        pltpu.VMEM(shape, f32)
        for count in (total, 1)
        for shape in (
            (SHIFTED, 3, count, height, depth),
            (UP, count, height, depth),
            (UP, count, height, depth),
            (3, count, height, depth),
            (3, count, height, depth),
            (UP, height, depth),
        )
    ]


def result_shapes(total, height, depth):
    return [
        shape
        for count in (total, 1)
        for shape in ((2 * UP, count, height, depth), (count, height, depth), (count, height, depth))
    ]


def body(
    cell_state,
    old_mass,
    pore_volume,
    transmissibility,
    active_mask,
    pvt_region,
    formation_factor,
    compressibility,
    inverse_viscosity,
):
    ax, ay, az = "gx", "gy", "gz"
    planes, rows, depth = pore_volume.shape
    total = planes + 2 * W
    per, groups = groups_of(planes, depth)
    assert per >= 1 and 2 * W * total <= depth and rows % 8 == 0 and RING <= 16
    tables = (formation_factor, compressibility, inverse_viscosity)
    like = lambda *shape: jax.ShapeDtypeStruct(shape, f32)
    fill = lambda shape, got: [jnp.zeros(shape.shape, f32) if one is None else one for one in got]

    z_shape = like(groups, rows, depth)
    local, *z_send = call(
        functools.partial(pack_z, az),
        "pack_z",
        8,
        out_shape=(like(CHANNELS, planes, rows, depth), z_shape, z_shape),
        in_specs=[HBM] * 6,
        out_specs=(VMEM,) * 3,
        scratch_shapes=[
            pltpu.VMEM((2, planes, rows, depth), jnp.int32),
            pltpu.SemaphoreType.DMA((7,)),
        ],
    )(cell_state, old_mass, pore_volume, transmissibility, active_mask, pvt_region)
    za, zb = fill(z_shape, swaps(az, *z_send))

    x_shape = like(XMAIN + groups, rows, depth)
    x_send = call(
        functools.partial(pack_x, ax), "pack_x", 8, out_shape=(x_shape, x_shape)
    )(local)
    x_send = call(
        join_x,
        "join_x",
        8,
        out_shape=(x_shape, x_shape),
        in_specs=[VMEM, VMEM, ANY, ANY],
        out_specs=(ANY, ANY),
        scratch_shapes=[pltpu.VMEM(z_shape.shape, f32), pltpu.SemaphoreType.DMA((2,))],
        input_output_aliases={2: 0, 3: 1},
    )(za, zb, *x_send)
    xa, xb = fill(x_shape, swaps(ax, *x_send))

    count_y = min(lax.axis_size(ay) - 1, 2)
    extra = 2 * XMAIN + CHANNELS
    y_shape = like(CHANNELS * planes + extra, W, depth)
    y_send = ()
    if count_y:
        y_send = call(
            functools.partial(pack_y, ay), "pack_y", 8, out_shape=(y_shape,) * count_y
        )(local)
    *y_send, columns = call(
        functools.partial(join_y, ay, ax, count_y, planes),
        "join_y",
        8,
        out_shape=(y_shape,) * count_y + (like(CHANNELS, rows, depth),),
        in_specs=[VMEM] * 4 + [ANY] * count_y,
        out_specs=(ANY,) * count_y + (VMEM,),
        scratch_shapes=[pltpu.VMEM((extra, W, depth), f32)] * count_y
        + [pltpu.SemaphoreType.DMA((max(count_y, 1),))],
        input_output_aliases={4 + i: i for i in range(count_y)},
    )(za, zb, xa, xb, *y_send)
    ys = swaps(ay, y_send[0], y_send[-1])[:count_y] if count_y else []

    smem = pl.BlockSpec(memory_space=pltpu.SMEM)
    tabs = pltpu.VMEM((9, 8, depth), f32)
    halves = call(
        functools.partial(inner, ax),
        "inner",
        24,
        out_shape=[like(*shape) for shape in result_shapes(total, rows, depth)]
        + [like(3, total, rows, depth)],
        in_specs=[VMEM] * 4 + [smem] * 3,
        out_specs=[VMEM] * 7,
        scratch_shapes=[tabs] + cell_arrays(total, rows + 16, depth),
    )(local, columns, xa, xb, *tables)

    return call(
        functools.partial(finish, (ax, ay, az), count_y),
        "finish",
        24,
        out_shape=(like(3, planes, rows, depth), like(planes, rows, depth)),
        in_specs=[VMEM] * 4 + [smem] * 3 + [VMEM] * (count_y + 7),
        out_specs=(VMEM, VMEM),
        scratch_shapes=[
            tabs,
            pltpu.VMEM((CHANNELS, total + 1, 16, depth), f32),
            pltpu.VMEM((3, total, 8, depth), f32),
            *(pltpu.VMEM(shape, f32) for shape in result_shapes(total, 8, depth)),
            pltpu.VMEM((2, 3, total, rows + 16, depth), f32),
            pltpu.VMEM((2, 3, 1, rows + 16, depth), f32),
            pltpu.VMEM((2, 3, total, 16, depth), f32),
            pltpu.VMEM((2, 3, 1, 16, depth), f32),
        ]
        + cell_arrays(total, 16, depth),
    )(local, columns, xa, xb, *tables, *ys, *halves)


def solution(mesh):
    return jax.shard_map(
        body,
        mesh=mesh,
        in_specs=(
            P(None, "gx", "gy", "gz"),
            P(None, "gx", "gy", "gz"),
            P("gx", "gy", "gz"),
            P(None, "gx", "gy", "gz"),
            P("gx", "gy", "gz"),
            P("gx", "gy", "gz"),
            P(),
            P(),
            P(),
        ),
        out_specs=(P(None, "gx", "gy", "gz"), P("gx", "gy", "gz")),
        check_vma=False,
    )
```

```python
import functools

import jax
import jax.numpy as jnp
from jax import lax
from jax.experimental import pallas as pl
from jax.experimental.pallas import tpu as pltpu
from jax.sharding import PartitionSpec as P

SWEEPS = 4
W = SWEEPS
relax_weight = 0.7

neighbour_offsets = [
    (along_x, along_y, along_z)
    for along_x in (-1, 0, 1)
    for along_y in (-1, 0, 1)
    for along_z in (-1, 0, 1)
    if (along_x, along_y, along_z) != (0, 0, 0)
]
upper_offsets = [offset for offset in neighbour_offsets if offset > (0, 0, 0)]
UP = len(upper_offsets)
FLAT = sum(1 for offset in upper_offsets if offset[0] == 0)
STEP = UP - FLAT

FAR = 5 + STEP
CHANNELS = FAR + FLAT + 4
NEAR = W - 1
XMAIN = CHANNELS * NEAR + FAR
VMEM = pl.BlockSpec(memory_space=pltpu.VMEM)
ANY = pl.BlockSpec(memory_space=pl.ANY)
HBM = pl.BlockSpec(memory_space=pltpu.MemorySpace.HBM)
f32 = jnp.float32


def t_channel(k):
    return FAR + k if k < FLAT else 5 + k - FLAT


def pick(parity, even, odd):
    shape = (even if odd is None else odd).shape
    if even is None:
        even = jnp.zeros(shape, f32)
    if odd is None:
        odd = jnp.zeros(shape, f32)
    return jnp.where(jnp.full(shape, parity, jnp.int32) == 0, even, odd)


def parity_of(axis):
    return lax.rem(lax.axis_index(axis), 2)


def swaps(axis, first, second):
    count = lax.axis_size(axis)
    got = []
    for start, message in ((0, first), (1, second)):
        pairs = [(i, i + 1) for i in range(start, count - 1, 2)]
        if not pairs:
            got.append(None)
            continue
        got.append(lax.ppermute(message, axis, pairs + [(b, a) for a, b in pairs]))
    return got


def lanes_of(shape):
    return lax.broadcasted_iota(jnp.int32, shape, len(shape) - 1)


def span_of(planes):
    return 2 * W * planes


def groups_of(planes, depth):
    per = depth // span_of(planes)
    return per, -(-CHANNELS // per)


def pack_z(axis, *refs):
    state, mass, pore, trans, active, region, local, first, second, flags, sems = refs
    planes, rows, depth = pore.shape
    copies = [
        pltpu.make_async_copy(active, flags.at[0], sems.at[0]),
        pltpu.make_async_copy(region, flags.at[1], sems.at[1]),
        pltpu.make_async_copy(state, local.at[0:3], sems.at[2]),
        pltpu.make_async_copy(trans.at[FLAT:UP], local.at[5:FAR], sems.at[3]),
        pltpu.make_async_copy(trans.at[0:FLAT], local.at[FAR : FAR + FLAT], sems.at[4]),
        pltpu.make_async_copy(mass, local.at[FAR + FLAT : CHANNELS - 1], sems.at[5]),
        pltpu.make_async_copy(pore, local.at[CHANNELS - 1], sems.at[6]),
    ]
    for copy in copies:
        copy.start()
    copies[0].wait()
    copies[1].wait()
    local[3:5] = flags[...].astype(f32)
    for copy in copies[2:]:
        copy.wait()

    per, groups = groups_of(planes, depth)
    even = parity_of(axis)
    lane = lanes_of((8, depth))

    @pl.loop(0, rows // 8)
    def _(tile):
        span = pl.ds(pl.multiple_of(8 * tile, 8), 8)
        for group in range(groups):
            high = jnp.zeros((8, depth), f32)
            low = jnp.zeros((8, depth), f32)
            for c in range(group * per, min(CHANNELS, group * per + per)):
                for x in range(planes):
                    base = (c % per) * span_of(planes) + 2 * W * x
                    values = local[c, x, span, :]
                    here = (lane >= base + W) & (lane < base + 2 * W)
                    high = jnp.where(here, pltpu.roll(values, (base + 2 * W) % depth, 1), high)
                    here = (lane >= base) & (lane < base + W)
                    low = jnp.where(here, pltpu.roll(values, base % depth, 1), low)
            first[group, span, :] = pick(even, high, low)
            second[group, span, :] = pick(even, low, high)


def pack_x(axis, local, *outs):
    planes = local.shape[1]
    even = parity_of(axis)
    for out, up in zip(outs, (even == 0, even != 0)):
        near = jnp.where(up, planes - NEAR, 0)
        far = jnp.where(up, planes - W, W - 1)
        for c in range(CHANNELS):
            for q in range(NEAR):
                out[c * NEAR + q] = local[c, near + q]
            if c < FAR:
                out[CHANNELS * NEAR + c] = local[c, far]


def join_x(za, zb, a_in, b_in, a_out, b_out, columns, sems):
    columns[...] = za[...] + zb[...]
    copies = [
        pltpu.make_async_copy(columns, out.at[pl.ds(XMAIN, columns.shape[0])], sems.at[n])
        for n, out in enumerate((a_out, b_out))
    ]
    for copy in copies:
        copy.start()
    for copy in copies:
        copy.wait()


def put_rows(outs, n, values, even):
    head, tail = values[:W], values[values.shape[0] - W :]
    for out, up, down in zip(outs, (tail, head), (head, tail)):
        out[n] = pick(even, up, down)


def pack_y(axis, local, *outs):
    planes = local.shape[1]
    even = parity_of(axis)
    for c in range(CHANNELS):
        for x in range(planes):
            put_rows(outs, c * planes + x, local[c, x], even)


def join_y(axis, x_axis, count, planes, za, zb, xa, xb, *refs):
    outs, columns = refs[count : 2 * count], refs[2 * count]
    stages, sems = refs[2 * count + 1 : 3 * count + 1], refs[3 * count + 1]
    rows, depth = xa.shape[1:]
    even = parity_of(axis)
    even_x = parity_of(x_axis)
    per, _ = groups_of(planes, depth)
    lane = lanes_of((rows, depth))
    for c in range(CHANNELS):
        group, base = c // per, (c % per) * span_of(planes)
        a, b = xa[XMAIN + group], xb[XMAIN + group]
        own = pltpu.roll(za[group] + zb[group], (2 * W * W - base) % depth, 1)
        below = pltpu.roll(pick(even_x, b, a), (depth - base - 2 * W * (planes - W)) % depth, 1)
        above = pltpu.roll(pick(even_x, a, b), (2 * W * (planes + W) - base) % depth, 1)
        values = jnp.where(lane < 2 * W * W, below, jnp.where(lane < 2 * W * (W + planes), own, above))
        columns[c] = values
        put_rows(stages, 2 * XMAIN + c, values, even)

    @pl.loop(0, XMAIN // 4)
    def _(i):
        for j in range(4):
            n = 4 * i + j
            a, b = xa[n], xb[n]
            put_rows(stages, n, pick(even_x, b, a), even)
            put_rows(stages, XMAIN + n, pick(even_x, a, b), even)

    copies = [
        pltpu.make_async_copy(
            stage, out.at[pl.ds(CHANNELS * planes, 2 * XMAIN + CHANNELS)], sems.at[i]
        )
        for i, (stage, out) in enumerate(zip(stages, outs))
    ]
    for copy in copies:
        copy.start()
    for copy in copies:
        copy.wait()


PRESS, MOB, SLOPE, ACT = 0, 1, 4, 7
SHIFTED = 8


def z_shift(values, columns, plane, step):
    depth = values.shape[-1]
    lane = lanes_of(values.shape)
    if step > 0:
        edge = pltpu.roll(columns, depth - 1 - 2 * W * plane, 1)
        return jnp.where(lane == depth - 1, edge, pltpu.roll(values, depth - 1, 1))
    edge = pltpu.roll(columns, depth - 2 * W * plane - 2 * W + 1, 1)
    return jnp.where(lane == 0, edge, pltpu.roll(values, 1, 1))


def z_shift_columns(values, step):
    return pltpu.roll(values, values.shape[-1] - 1 if step > 0 else 1, 1)


def z_edge(current, values, plane, step):
    lane = lanes_of(values.shape)
    if step > 0:
        at = 2 * W * plane + 2 * W - 1
        return jnp.where(lane == at, pltpu.roll(values, at, 1), current)
    at = 2 * W * plane
    return jnp.where(lane == at, pltpu.roll(values, at + 1, 1), current)


def fill_tables(tables, tabs):
    lane = lanes_of(tabs.shape[1:])
    for n, table in enumerate(tables):
        for c in range(3):
            values = jnp.full(tabs.shape[1:], table[c, 0], f32)
            for level in range(1, table.shape[1]):
                values = jnp.where(lane == level, table[c, level], values)
            tabs[3 * n + c] = values


def properties(get, plane, is_columns, first, tabs, arrays, halo):
    fields, lower, half, weight, accum, _ = halo if is_columns else arrays
    halo_fields, halo_lower, centre = halo[0], halo[1], halo[5]
    span = pl.ds(first, 8)
    press, water, gas, active, region = (get(c) for c in range(5))
    index = region.astype(jnp.int32)
    look = [
        jnp.take_along_axis(tabs[n], index, axis=1, mode="promise_in_bounds") for n in range(9)
    ]
    formation, compress, viscous = look[:3], look[3:6], look[6:]
    sat = (water, 1.0 - water - gas, gas)
    expand = [formation[c] * jnp.exp(compress[c] * (press - 0.5)) for c in range(3)]
    mob = [viscous[c] * expand[c] * sat[c] * sat[c] for c in range(3)]
    pore = get(CHANNELS - 1)
    stored = pore * (compress[0] * sat[0] + compress[1] * sat[1] + compress[2] * sat[2])
    stored = jnp.where(active > 0, stored, 1.0)
    for c in range(3):
        weight[c, plane, span, :] = active / (expand[c] * stored)
        accum[c, plane, span, :] = pore * expand[c] * sat[c] - get(FAR + FLAT + c)
    one = [press] + mob + [compress[c] * mob[c] for c in range(3)] + [active]
    for f, values in enumerate(one):
        fields[f, 1, plane, span, :] = values
        for step in (-1, 1):
            if is_columns:
                fields[f, step + 1, plane, span, :] = z_shift_columns(values, step)
            else:
                columns = halo_fields[f, 1, 0, span, :]
                fields[f, step + 1, plane, span, :] = z_shift(values, columns, plane, step)
                current = halo_fields[f, step + 1, 0, span, :]
                halo_fields[f, step + 1, 0, span, :] = z_edge(current, values, plane, step)
    for k, offset in enumerate(upper_offsets):
        values = 0.5 * get(t_channel(k))
        half[k, plane, span, :] = values
        values = values * active
        step = -offset[2]
        if step == 0:
            lower[k, plane, span, :] = values
        elif is_columns:
            centre[k, span, :] = values
            lower[k, plane, span, :] = z_shift_columns(values, step)
        else:
            lower[k, plane, span, :] = z_shift(values, centre[k, span, :], plane, step)
            current = halo_lower[k, 0, span, :]
            halo_lower[k, 0, span, :] = z_edge(current, values, plane, step)


def x_roll(values, step, is_columns):
    if not is_columns or step == 0:
        return values
    depth = values.shape[-1]
    return pltpu.roll(values, (depth - 2 * W * step) % depth, 1)


def link_cells(plane, is_columns, first, stride, arrays, out, results):
    fields, lower, half, weight, accum, _ = arrays
    coupling, scale, start = results
    depth = fields.shape[-1]
    here = (0, 0, 0)

    def read(ref, lead, offset):
        dx = 0 if is_columns else offset[0]
        values = ref[(*lead, plane + dx, pl.ds(first + stride * offset[1], 8), slice(None))]
        return x_roll(values, offset[0], is_columns)

    def at(f, offset):
        return read(fields, (f, offset[2] + 1), offset)

    press = at(PRESS, here)
    w = [read(weight, (c,), here) for c in range(3)]
    mob = [at(MOB + c, here) for c in range(3)]
    own_mob = w[0] * mob[0] + w[1] * mob[1] + w[2] * mob[2]
    own_slope = w[0] * at(SLOPE, here) + w[1] * at(SLOPE + 1, here) + w[2] * at(SLOPE + 2, here)
    flux = [jnp.zeros((8, depth), f32) for _ in range(3)]
    drops = jnp.zeros((8, depth), f32)
    means = jnp.ones((8, depth), f32)
    for n, offset in enumerate(neighbour_offsets):
        if offset > here:
            link = read(half, (upper_offsets.index(offset),), here) * at(ACT, offset)
        else:
            k = upper_offsets.index(tuple(-o for o in offset))
            link = read(lower, (k,), offset)
        drop = link * (press - at(PRESS, offset))
        other = [at(MOB + c, offset) for c in range(3)]
        for c in range(3):
            flux[c] = flux[c] + drop * other[c]
        drops = drops + drop
        mean = link * (own_mob + (w[0] * other[0] + w[1] * other[1] + w[2] * other[2]))
        slope = (
            w[0] * at(SLOPE, offset) + w[1] * at(SLOPE + 1, offset) + w[2] * at(SLOPE + 2, offset)
        )
        means = means + mean
        coupling[n, plane, out, :] = drop * slope - mean
    active = at(ACT, here)
    res = [
        active * (read(accum, (c,), here) + (flux[c] + mob[c] * drops)) for c in range(3)
    ]
    rate = relax_weight / (means + own_slope * drops)
    scale[plane, out, :] = rate
    start[plane, out, :] = -rate * (w[0] * res[0] + w[1] * res[1] + w[2] * res[2])
    return res


def inner(x_axis, local, columns, xa, xb, *refs):
    tables, results, halo_results, store = refs[:3], refs[3:6], refs[6:9], refs[9]
    tabs, arrays, halo = refs[10], refs[11:17], refs[17:]
    planes, rows, depth = local.shape[1:]
    total = planes + 2 * W
    even_x = parity_of(x_axis)
    fill_tables(tables, tabs)
    tiles = range(rows // 8)

    def cells(get, plane, is_columns=False):
        for tile in tiles:
            span = slice(8 * tile, 8 * tile + 8)
            properties(lambda c: get(c, span), plane, is_columns, 8 + 8 * tile, tabs, arrays, halo)

    cells(lambda c, span: columns[c, span, :], 0, True)

    @pl.loop(0, planes)
    def _(x):
        cells(lambda c, span: local[c, x, span, :], W + x)

    def from_x(n, low):
        a, b = xa, xb
        def get(c, span):
            i = n(c)
            if i is None:
                return jnp.zeros((8, depth), f32)
            u, v = xa[i, span, :], xb[i, span, :]
            return pick(even_x, v, u) if low else pick(even_x, u, v)
        return get

    @pl.loop(0, NEAR)
    def _(q):
        near = lambda c: c * NEAR + q
        cells(from_x(near, True), 1 + q)
        cells(from_x(near, False), W + planes + q)

    far = lambda c: CHANNELS * NEAR + c if c < FAR else None
    cells(from_x(far, True), 0)
    cells(from_x(far, False), total - 1)

    def links(plane, is_columns=False):
        for tile in tiles:
            out = slice(8 * tile, 8 * tile + 8)
            own = (halo, out, halo_results) if is_columns else (arrays, out, results)
            res = link_cells(plane, is_columns, 8 + 8 * tile, 1, *own)
            if not is_columns:
                for c in range(3):
                    store[c, plane, out, :] = res[c]

    links(0, True)

    @pl.loop(1, total - 1)
    def _(plane):
        links(plane)


RING = 2 * (W + 2)


def finish(axes, count_y, local, columns, xa, xb, *refs):
    tables = refs[:3]
    ys = refs[3 : 3 + count_y]
    results, halo_results, store, residual, update = (
        refs[3 + count_y : 6 + count_y],
        refs[6 + count_y : 9 + count_y],
        *refs[9 + count_y : 12 + count_y],
    )
    refs = refs[12 + count_y :]
    tabs, raw, edge_store = refs[:3]
    edge_results, edge_halo_results = refs[3:6], refs[6:9]
    sols, halo_sols, edge_sols, edge_halo_sols = (refs[9 + 2 * i : 11 + 2 * i] for i in range(4))
    arrays, halo = refs[17:23], refs[23:]
    planes, rows, depth = local.shape[1:]
    total = planes + 2 * W
    even_x, even_y, _ = (parity_of(axis) for axis in axes)
    fill_tables(tables, tabs)

    def put(c, plane, values, n):
        low = high = jnp.zeros((W, depth), f32)
        if count_y:
            a = ys[0][n]
            b = ys[1][n] if count_y > 1 else None
            low, high = pick(even_y, b, a), pick(even_y, a, b)
        raw[c, plane, pl.ds(0, 2, stride=2), :] = values[rows - 2 :]
        raw[c, plane, pl.ds(4, W, stride=2), :] = high
        raw[c, plane, pl.ds(1, W, stride=2), :] = low
        raw[c, plane, pl.ds(RING - 3, 2, stride=2), :] = values[:2]
        raw[c, plane, RING:16, :] = jnp.zeros((16 - RING, depth), f32)

    base = CHANNELS * planes

    @pl.loop(0, CHANNELS)
    def _(c):
        for x in range(planes):
            put(c, W + x, local[c, x], c * planes + x)
        for q in range(NEAR):
            n = c * NEAR + q
            a, b = xa[n], xb[n]
            put(c, 1 + q, pick(even_x, b, a), base + n)
            put(c, W + planes + q, pick(even_x, a, b), base + XMAIN + n)
        put(c, total, columns[c], base + 2 * XMAIN + c)

    @pl.loop(0, FAR)
    def _(c):
        n = CHANNELS * NEAR + c
        a, b = xa[n], xb[n]
        put(c, 0, pick(even_x, b, a), base + n)
        put(c, total - 1, pick(even_x, a, b), base + XMAIN + n)

    for c in range(FAR, CHANNELS):
        for plane in (0, total - 1):
            raw[c, plane] = jnp.zeros((16, depth), f32)

    def cells(plane, is_columns=False):
        for tile in range(2):
            span = slice(8 * tile, 8 * tile + 8)
            get = lambda c: raw[c, plane, span, :]
            properties(get, 0 if is_columns else plane, is_columns, 8 * tile, tabs, arrays, halo)

    cells(total, True)

    @pl.loop(0, total, unroll=2)
    def _(plane):
        cells(plane)

    def links(plane, is_columns=False):
        out = slice(0, 8)
        own = (halo, out, edge_halo_results) if is_columns else (arrays, out, edge_results)
        res = link_cells(plane, is_columns, 2, 2, *own)
        if not is_columns:
            for c in range(3):
                edge_store[c, plane] = res[c]

    links(0, True)

    @pl.loop(1, total - 1)
    def _(plane):
        links(plane)

    tiles = rows // 8

    row = lax.broadcasted_iota(jnp.int32, (8, depth), 0)

    def merged(mains, edge):
        first, last = pltpu.roll(edge, 1, 0), pltpu.roll(edge, 7, 0)
        mains = [jnp.where(row == 0, first, mains[0])] + mains[1:]
        return mains[:-1] + [jnp.where(row == 7, last, mains[-1])]

    def put_parts(is_columns, slot, step, plane, mains, edge):
        to, edge_to = (
            (halo_sols[slot], edge_halo_sols[slot]) if is_columns else (sols[slot], edge_sols[slot])
        )
        for tile, values in enumerate(mains):
            to[step + 1, plane, 8 + 8 * tile : 16 + 8 * tile, :] = values
        edge_to[step + 1, plane, 2:10, :] = edge
        to[step + 1, plane, 7:8, :] = edge[5:6]
        to[step + 1, plane, 8 + rows : 9 + rows, :] = edge[2:3]
        edge_to[step + 1, plane, 0:1, :] = mains[-1][6:7]
        edge_to[step + 1, plane, RING - 1 : RING, :] = mains[0][1:2]

    def halo_parts(slot, step):
        mains = [
            halo_sols[slot][step + 1, 0, 8 + 8 * tile : 16 + 8 * tile, :] for tile in range(tiles)
        ]
        return mains, edge_halo_sols[slot][step + 1, 0, 2:10, :]

    def put_solution(slot, plane, mains, edge, is_columns=False):
        mains = merged(mains, edge)
        put_parts(is_columns, slot, 0, plane, mains, edge)
        for step in (-1, 1):
            if is_columns:
                shift = lambda values: z_shift_columns(values, step)
                put_parts(True, slot, step, plane, [shift(u) for u in mains], shift(edge))
                continue
            shift = lambda u, v: z_shift(u, v, plane, step)
            halo_mains, halo_edge = halo_parts(slot, 0)
            shifted = [shift(u, v) for u, v in zip(mains, halo_mains)]
            put_parts(False, slot, step, plane, shifted, shift(edge, halo_edge))
            shift = lambda u, v: z_edge(u, v, plane, step)
            halo_mains, halo_edge = halo_parts(slot, step)
            shifted = [shift(u, v) for u, v in zip(halo_mains, mains)]
            put_parts(True, slot, step, 0, shifted, shift(halo_edge, edge))

    def relaxed(slot, plane, tile, is_columns=False):
        if tile is None:
            ref = (edge_halo_sols if is_columns else edge_sols)[slot]
            first, stride, out = 2, 2, slice(0, 8)
            coupling, scale, start = edge_halo_results if is_columns else edge_results
        else:
            ref = (halo_sols if is_columns else sols)[slot]
            first, stride = 8 + 8 * tile, 1
            out = slice(8 * tile, 8 * tile + 8)
            coupling, scale, start = halo_results if is_columns else results

        def get(offset):
            dx = 0 if is_columns else offset[0]
            values = ref[offset[2] + 1, plane + dx, pl.ds(first + stride * offset[1], 8), :]
            return x_roll(values, offset[0], is_columns)

        parts = [jnp.zeros((8, depth), f32) for _ in range(2)]
        for n, offset in enumerate(neighbour_offsets):
            parts[n % 2] = parts[n % 2] + coupling[n, plane, out, :] * get(offset)
        return (
            (1.0 - relax_weight) * get((0, 0, 0))
            + start[plane, out, :]
            - scale[plane, out, :] * (parts[0] + parts[1])
        )

    def first_sweep(plane, is_columns=False):
        start = (halo_results if is_columns else results)[2]
        edge = (edge_halo_results if is_columns else edge_results)[2]
        mains = [start[plane, 8 * tile : 8 * tile + 8, :] for tile in range(tiles)]
        put_solution(0, plane, mains, edge[plane], is_columns)

    first_sweep(0, True)

    @pl.loop(1, total - 1, unroll=2)
    def _(plane):
        first_sweep(plane)

    def sweep_of(slot, plane, is_columns=False):
        mains = [relaxed(slot, plane, tile, is_columns) for tile in range(tiles)]
        put_solution(1 - slot, plane, mains, relaxed(slot, plane, None, is_columns), is_columns)

    for sweep in range(2, SWEEPS):
        slot = sweep % 2
        sweep_of(slot, 0, True)

        @pl.loop(sweep, total - sweep, unroll=2)
        def _(plane):
            sweep_of(slot, plane)

    @pl.loop(0, planes, unroll=2)
    def _(x):
        slot, plane = SWEEPS % 2, W + x
        edge = relaxed(slot, plane, None)
        for tile in range(tiles):
            span = slice(8 * tile, 8 * tile + 8)
            update[x, span, :] = relaxed(slot, plane, tile)
            for c in range(3):
                residual[c, x, span, :] = store[c, plane, span, :]
        update[x, 0:1, :] = edge[7:8]
        update[x, rows - 1 : rows, :] = edge[0:1]
        for c in range(3):
            residual[c, x, 0:1, :] = edge_store[c, plane, 7:8, :]
            residual[c, x, rows - 1 : rows, :] = edge_store[c, plane, 0:1, :]


def call(kernel, name, mib, **options):
    return pl.pallas_call(
        kernel,
        name=name,
        compiler_params=pltpu.CompilerParams(vmem_limit_bytes=mib << 20),
        **options,
    )


def cell_arrays(total, height, depth):
    return [
        pltpu.VMEM(shape, f32)
        for count in (total, 1)
        for shape in (
            (SHIFTED, 3, count, height, depth),
            (UP, count, height, depth),
            (UP, count, height, depth),
            (3, count, height, depth),
            (3, count, height, depth),
            (UP, height, depth),
        )
    ]


def result_shapes(total, height, depth):
    return [
        shape
        for count in (total, 1)
        for shape in ((2 * UP, count, height, depth), (count, height, depth), (count, height, depth))
    ]


def body(
    cell_state,
    old_mass,
    pore_volume,
    transmissibility,
    active_mask,
    pvt_region,
    formation_factor,
    compressibility,
    inverse_viscosity,
):
    ax, ay, az = "gx", "gy", "gz"
    planes, rows, depth = pore_volume.shape
    total = planes + 2 * W
    per, groups = groups_of(planes, depth)
    assert per >= 1 and 2 * W * total <= depth and rows % 8 == 0 and RING <= 16
    tables = (formation_factor, compressibility, inverse_viscosity)
    like = lambda *shape: jax.ShapeDtypeStruct(shape, f32)
    fill = lambda shape, got: [jnp.zeros(shape.shape, f32) if one is None else one for one in got]

    arguments = (cell_state, old_mass, pore_volume, transmissibility, active_mask, pvt_region)
    z_shape = like(groups, rows, depth)
    local, *z_send = call(
        functools.partial(pack_z, az),
        "pack_z",
        8,
        out_shape=(like(CHANNELS, planes, rows, depth), z_shape, z_shape),
        in_specs=[HBM] * 6,
        out_specs=(VMEM,) * 3,
        scratch_shapes=[
            pltpu.VMEM((2, planes, rows, depth), jnp.int32),
            pltpu.SemaphoreType.DMA((7,)),
        ],
    )(*(pltpu.with_memory_space_constraint(array, pltpu.MemorySpace.HBM) for array in arguments))
    za, zb = fill(z_shape, swaps(az, *z_send))

    x_shape = like(XMAIN + groups, rows, depth)
    x_send = call(
        functools.partial(pack_x, ax), "pack_x", 8, out_shape=(x_shape, x_shape)
    )(local)
    x_send = call(
        join_x,
        "join_x",
        8,
        out_shape=(x_shape, x_shape),
        in_specs=[VMEM, VMEM, ANY, ANY],
        out_specs=(ANY, ANY),
        scratch_shapes=[pltpu.VMEM(z_shape.shape, f32), pltpu.SemaphoreType.DMA((2,))],
        input_output_aliases={2: 0, 3: 1},
    )(za, zb, *x_send)
    xa, xb = fill(x_shape, swaps(ax, *x_send))

    count_y = min(lax.axis_size(ay) - 1, 2)
    extra = 2 * XMAIN + CHANNELS
    y_shape = like(CHANNELS * planes + extra, W, depth)
    y_send = ()
    if count_y:
        y_send = call(
            functools.partial(pack_y, ay), "pack_y", 8, out_shape=(y_shape,) * count_y
        )(local)
    *y_send, columns = call(
        functools.partial(join_y, ay, ax, count_y, planes),
        "join_y",
        8,
        out_shape=(y_shape,) * count_y + (like(CHANNELS, rows, depth),),
        in_specs=[VMEM] * 4 + [ANY] * count_y,
        out_specs=(ANY,) * count_y + (VMEM,),
        scratch_shapes=[pltpu.VMEM((extra, W, depth), f32)] * count_y
        + [pltpu.SemaphoreType.DMA((max(count_y, 1),))],
        input_output_aliases={4 + i: i for i in range(count_y)},
    )(za, zb, xa, xb, *y_send)
    ys = swaps(ay, y_send[0], y_send[-1])[:count_y] if count_y else []

    smem = pl.BlockSpec(memory_space=pltpu.SMEM)
    tabs = pltpu.VMEM((9, 8, depth), f32)
    halves = call(
        functools.partial(inner, ax),
        "inner",
        24,
        out_shape=[like(*shape) for shape in result_shapes(total, rows, depth)]
        + [like(3, total, rows, depth)],
        in_specs=[VMEM] * 4 + [smem] * 3,
        out_specs=[VMEM] * 7,
        scratch_shapes=[tabs] + cell_arrays(total, rows + 16, depth),
    )(local, columns, xa, xb, *tables)

    return call(
        functools.partial(finish, (ax, ay, az), count_y),
        "finish",
        24,
        out_shape=(like(3, planes, rows, depth), like(planes, rows, depth)),
        in_specs=[VMEM] * 4 + [smem] * 3 + [VMEM] * (count_y + 7),
        out_specs=(VMEM, VMEM),
        scratch_shapes=[
            tabs,
            pltpu.VMEM((CHANNELS, total + 1, 16, depth), f32),
            pltpu.VMEM((3, total, 8, depth), f32),
            *(pltpu.VMEM(shape, f32) for shape in result_shapes(total, 8, depth)),
            *[pltpu.VMEM((3, total, rows + 16, depth), f32)] * 2,
            *[pltpu.VMEM((3, 1, rows + 16, depth), f32)] * 2,
            *[pltpu.VMEM((3, total, 16, depth), f32)] * 2,
            *[pltpu.VMEM((3, 1, 16, depth), f32)] * 2,
        ]
        + cell_arrays(total, 16, depth),
    )(local, columns, xa, xb, *tables, *ys, *halves)


def solution(mesh):
    return jax.shard_map(
        body,
        mesh=mesh,
        in_specs=(
            P(None, "gx", "gy", "gz"),
            P(None, "gx", "gy", "gz"),
            P("gx", "gy", "gz"),
            P(None, "gx", "gy", "gz"),
            P("gx", "gy", "gz"),
            P("gx", "gy", "gz"),
            P(),
            P(),
            P(),
        ),
        out_specs=(P(None, "gx", "gy", "gz"), P("gx", "gy", "gz")),
        check_vma=False,
    )
```

```python
import functools
import itertools

import jax
import jax.numpy as jnp
from jax import lax
from jax.experimental import pallas as pl
from jax.experimental.pallas import tpu as pltpu
from jax.sharding import PartitionSpec as P

SWEEPS = 4
W = SWEEPS
relax_weight = 0.7

neighbour_offsets = [
    (along_x, along_y, along_z)
    for along_x in (-1, 0, 1)
    for along_y in (-1, 0, 1)
    for along_z in (-1, 0, 1)
    if (along_x, along_y, along_z) != (0, 0, 0)
]
upper_offsets = [offset for offset in neighbour_offsets if offset > (0, 0, 0)]
UP = len(upper_offsets)
FLAT = sum(1 for offset in upper_offsets if offset[0] == 0)
STEP = UP - FLAT

FAR = 5 + STEP
CHANNELS = FAR + FLAT + 2
STORAGE, OWN = FAR + FLAT, FAR + FLAT + 1
NEAR = W - 1
XMAIN = CHANNELS * NEAR + FAR
VMEM = pl.BlockSpec(memory_space=pltpu.VMEM)
ANY = pl.BlockSpec(memory_space=pl.ANY)
HBM = pl.BlockSpec(memory_space=pltpu.MemorySpace.HBM)
f32 = jnp.float32


def t_channel(k):
    return FAR + k if k < FLAT else 5 + k - FLAT


def pick(parity, even, odd):
    shape = (even if odd is None else odd).shape
    if even is None:
        even = jnp.zeros(shape, f32)
    if odd is None:
        odd = jnp.zeros(shape, f32)
    return jnp.where(jnp.full(shape, parity, jnp.int32) == 0, even, odd)


def parity_of(axis):
    return lax.rem(lax.axis_index(axis), 2)


def swaps(axis, first, second):
    count = lax.axis_size(axis)
    got = []
    for start, message in ((0, first), (1, second)):
        pairs = [(i, i + 1) for i in range(start, count - 1, 2)]
        if not pairs:
            got.append(None)
            continue
        got.append(lax.ppermute(message, axis, pairs + [(b, a) for a, b in pairs]))
    return got


def lanes_of(shape):
    return lax.broadcasted_iota(jnp.int32, shape, len(shape) - 1)


def span_of(planes):
    return 2 * W * planes


def groups_of(planes, depth):
    per = depth // span_of(planes)
    return per, -(-CHANNELS // per)


def lookups(tabs, region, numbers):
    index = region.astype(jnp.int32)
    return [
        jnp.take_along_axis(tabs[n], index, axis=1, mode="promise_in_bounds") for n in numbers
    ]


def pack_z(axis, *refs):
    state, mass, pore, trans, active, region, *tables = refs[:9]
    local, accum, tabs, first, second = refs[9:14]
    flags, masses, pores, small, sems = refs[14:]
    planes, rows, depth = pore.shape
    copies = [
        pltpu.make_async_copy(active, flags.at[0], sems.at[0]),
        pltpu.make_async_copy(region, flags.at[1], sems.at[1]),
        pltpu.make_async_copy(state, local.at[0:3], sems.at[2]),
        pltpu.make_async_copy(mass, masses, sems.at[3]),
        pltpu.make_async_copy(pore, pores, sems.at[4]),
    ]
    copies += [
        pltpu.make_async_copy(table, small.at[n], sems.at[5 + n]) for n, table in enumerate(tables)
    ]
    late = [
        pltpu.make_async_copy(trans.at[FLAT:UP], local.at[5:FAR], sems.at[8]),
        pltpu.make_async_copy(trans.at[0:FLAT], local.at[FAR : FAR + FLAT], sems.at[9]),
    ]
    for copy in copies + late:
        copy.start()
    for copy in copies:
        copy.wait()
    regions = tables[0].shape[1]
    for n in range(3):
        for c in range(3):
            tabs[3 * n + c, :, 0:regions] = jnp.broadcast_to(small[n, c : c + 1, :], (8, regions))
    for x in range(planes):
        for tile in range(rows // 8):
            span = slice(8 * tile, 8 * tile + 8)
            on = flags[0, x, span, :].astype(f32)
            level = flags[1, x, span, :]
            local[3, x, span, :] = on
            local[4, x, span, :] = level.astype(f32)
            press, water, gas = (local[c, x, span, :] for c in range(3))
            look = lookups(tabs, level, range(6))
            sat = (water, 1.0 - water - gas, gas)
            expand = [look[c] * jnp.exp(look[3 + c] * (press - 0.5)) for c in range(3)]
            volume = pores[x, span, :]
            stored = volume * (look[3] * sat[0] + look[4] * sat[1] + look[5] * sat[2])
            stored = jnp.where(on > 0, stored, 1.0)
            own = jnp.zeros((8, depth), f32)
            for c in range(3):
                value = volume * expand[c] * sat[c] - masses[c, x, span, :]
                accum[c, x, span, :] = value
                own = own + value / (expand[c] * stored)
            local[STORAGE, x, span, :] = stored
            local[OWN, x, span, :] = on * own
    for copy in late:
        copy.wait()

    per, groups = groups_of(planes, depth)
    even = parity_of(axis)
    lane = lanes_of((8, depth))

    @pl.loop(0, rows // 8)
    def _(tile):
        span = pl.ds(pl.multiple_of(8 * tile, 8), 8)
        for group in range(groups):
            high = jnp.zeros((8, depth), f32)
            low = jnp.zeros((8, depth), f32)
            for c in range(group * per, min(CHANNELS, group * per + per)):
                for x in range(planes):
                    base = (c % per) * span_of(planes) + 2 * W * x
                    values = local[c, x, span, :]
                    here = (lane >= base + W) & (lane < base + 2 * W)
                    high = jnp.where(here, pltpu.roll(values, (base + 2 * W) % depth, 1), high)
                    here = (lane >= base) & (lane < base + W)
                    low = jnp.where(here, pltpu.roll(values, base % depth, 1), low)
            first[group, span, :] = pick(even, high, low)
            second[group, span, :] = pick(even, low, high)


def pack_x(axis, local, *outs):
    planes = local.shape[1]
    even = parity_of(axis)
    for out, up in zip(outs, (even == 0, even != 0)):
        near = jnp.where(up, planes - NEAR, 0)
        far = jnp.where(up, planes - W, W - 1)
        for c in range(CHANNELS):
            for q in range(NEAR):
                out[c * NEAR + q] = local[c, near + q]
            if c < FAR:
                out[CHANNELS * NEAR + c] = local[c, far]


def join_x(axis, planes, za, zb, a_in, b_in, a_out, b_out, columns, sems):
    rows, depth = za.shape[1:]
    even = parity_of(axis)
    per, _ = groups_of(planes, depth)
    per_x, groups_x = groups_of(W, depth)
    lane = lanes_of((rows, depth))
    for group in range(groups_x):
        sides = [jnp.zeros((rows, depth), f32) for _ in range(2)]
        for c in range(group * per_x, min(CHANNELS, group * per_x + per_x)):
            values = za[c // per] + zb[c // per]
            to = (c % per_x) * span_of(W)
            here = (lane >= to) & (lane < to + span_of(W))
            for n, plane in enumerate((planes - W, 0)):
                source = (c % per) * span_of(planes) + 2 * W * plane
                sides[n] = jnp.where(here, pltpu.roll(values, (to - source) % depth, 1), sides[n])
        columns[0, group] = pick(even, *sides)
        columns[1, group] = pick(even, *sides[::-1])
    copies = [
        pltpu.make_async_copy(columns.at[n], out.at[pl.ds(XMAIN, groups_x)], sems.at[n])
        for n, out in enumerate((a_out, b_out))
    ]
    for copy in copies:
        copy.start()
    for copy in copies:
        copy.wait()


def put_rows(outs, n, values, even):
    head, tail = values[:W], values[values.shape[0] - W :]
    for out, up, down in zip(outs, (tail, head), (head, tail)):
        out[n] = pick(even, up, down)


def pack_y(axis, local, *outs):
    planes = local.shape[1]
    even = parity_of(axis)
    for c in range(CHANNELS):
        for x in range(planes):
            put_rows(outs, c * planes + x, local[c, x], even)


def join_y(axis, x_axis, count, planes, za, zb, xa, xb, *refs):
    outs, columns = refs[count : 2 * count], refs[2 * count]
    stages, sems = refs[2 * count + 1 : 3 * count + 1], refs[3 * count + 1]
    rows, depth = xa.shape[1:]
    even = parity_of(axis)
    even_x = parity_of(x_axis)
    per, _ = groups_of(planes, depth)
    per_x, _ = groups_of(W, depth)
    lane = lanes_of((rows, depth))
    for c in range(CHANNELS):
        group, base = c // per, (c % per) * span_of(planes)
        own = pltpu.roll(za[group] + zb[group], (2 * W * W - base) % depth, 1)
        group, base = c // per_x, (c % per_x) * span_of(W)
        a, b = xa[XMAIN + group], xb[XMAIN + group]
        below = pltpu.roll(pick(even_x, b, a), (depth - base) % depth, 1)
        above = pltpu.roll(pick(even_x, a, b), (2 * W * (planes + W) - base) % depth, 1)
        values = jnp.where(lane < 2 * W * W, below, jnp.where(lane < 2 * W * (W + planes), own, above))
        columns[c] = values
        put_rows(stages, 2 * XMAIN + c, values, even)

    @pl.loop(0, XMAIN // 2)
    def _(i):
        for j in range(2):
            n = 2 * i + j
            a, b = xa[n], xb[n]
            put_rows(stages, n, pick(even_x, b, a), even)
            put_rows(stages, XMAIN + n, pick(even_x, a, b), even)

    copies = [
        pltpu.make_async_copy(
            stage, out.at[pl.ds(CHANNELS * planes, 2 * XMAIN + CHANNELS)], sems.at[i]
        )
        for i, (stage, out) in enumerate(zip(stages, outs))
    ]
    for copy in copies:
        copy.start()
    for copy in copies:
        copy.wait()


PRESS, MOB, SLOPE, ACT = 0, 1, 4, 7
SHIFTED = 8


def z_shift(values, columns, plane, step):
    depth = values.shape[-1]
    lane = lanes_of(values.shape)
    if step > 0:
        edge = pltpu.roll(columns, depth - 1 - 2 * W * plane, 1)
        return jnp.where(lane == depth - 1, edge, pltpu.roll(values, depth - 1, 1))
    edge = pltpu.roll(columns, depth - 2 * W * plane - 2 * W + 1, 1)
    return jnp.where(lane == 0, edge, pltpu.roll(values, 1, 1))


def z_shift_columns(values, step):
    return pltpu.roll(values, values.shape[-1] - 1 if step > 0 else 1, 1)


def z_edge(current, values, plane, step):
    lane = lanes_of(values.shape)
    if step > 0:
        at = 2 * W * plane + 2 * W - 1
        return jnp.where(lane == at, pltpu.roll(values, at, 1), current)
    at = 2 * W * plane
    return jnp.where(lane == at, pltpu.roll(values, at + 1, 1), current)


def properties(get, plane, is_columns, put, tabs, arrays, halo, centre, span):
    fields, lower, half, weight, base = halo if is_columns else arrays
    halo_fields, halo_lower = halo[:2]
    press, water, gas, active, region = (get(c) for c in range(5))
    look = lookups(tabs, region, range(9))
    formation, compress, viscous = look[:3], look[3:6], look[6:]
    sat = (water, 1.0 - water - gas, gas)
    expand = [formation[c] * jnp.exp(compress[c] * (press - 0.5)) for c in range(3)]
    mob = [viscous[c] * expand[c] * sat[c] * sat[c] for c in range(3)]
    stored = get(STORAGE)
    stored = jnp.where(stored > 0, stored, 1.0)
    for c in range(3):
        put(weight, (c, plane), active / (expand[c] * stored))
    put(base, (plane,), get(OWN))
    shifts = []
    one = [press] + mob + [compress[c] * mob[c] for c in range(3)] + [active]
    for f, values in enumerate(one):
        put(fields, (f, 1, plane), values)
        shifts += [(0, (f, step + 1), step, values, f) for step in (-1, 1)]
    for k, offset in enumerate(upper_offsets):
        values = 0.5 * get(t_channel(k))
        put(half, (k, plane), values)
        values = values * active
        if offset[2] == 0:
            put(lower, (k, plane), values)
        else:
            shifts.append((1, (k,), -offset[2], values, SHIFTED + k))
    for array, lead, step, values, slot in shifts:
        if is_columns:
            centre[slot, span, :] = values
            put((fields, lower)[array], (*lead, 0), z_shift_columns(values, step))
        else:
            put((fields, lower)[array], (*lead, plane), z_shift(values, centre[slot, span, :], plane, step))
            put((halo_fields, halo_lower)[array], (*lead, 0), None, lambda now: z_edge(now, values, plane, step))


def x_roll(values, step, is_columns):
    if not is_columns or step == 0:
        return values
    depth = values.shape[-1]
    return pltpu.roll(values, (depth - 2 * W * step) % depth, 1)


def link_cells(plane, is_columns, first, stride, arrays, out, results):
    fields, lower, half, weight, base = arrays
    coupling, scale, start = results
    depth = fields.shape[-1]
    here = (0, 0, 0)

    def read(ref, lead, offset):
        dx = 0 if is_columns else offset[0]
        values = ref[(*lead, plane + dx, pl.ds(first + stride * offset[1], 8), slice(None))]
        return x_roll(values, offset[0], is_columns)

    def at(f, offset):
        return read(fields, (f, offset[2] + 1), offset)

    press = at(PRESS, here)
    w = [read(weight, (c,), here) for c in range(3)]
    mob = [at(MOB + c, here) for c in range(3)]
    own_mob = w[0] * mob[0] + w[1] * mob[1] + w[2] * mob[2]
    own_slope = w[0] * at(SLOPE, here) + w[1] * at(SLOPE + 1, here) + w[2] * at(SLOPE + 2, here)
    flux = [jnp.zeros((8, depth), f32) for _ in range(3)]
    drops = jnp.zeros((8, depth), f32)
    means = jnp.ones((8, depth), f32)
    for n, offset in enumerate(neighbour_offsets):
        if offset > here:
            link = read(half, (upper_offsets.index(offset),), here) * at(ACT, offset)
        else:
            k = upper_offsets.index(tuple(-o for o in offset))
            link = read(lower, (k,), offset)
        drop = link * (press - at(PRESS, offset))
        other = [at(MOB + c, offset) for c in range(3)]
        for c in range(3):
            flux[c] = flux[c] + drop * other[c]
        drops = drops + drop
        mean = link * (own_mob + (w[0] * other[0] + w[1] * other[1] + w[2] * other[2]))
        slope = (
            w[0] * at(SLOPE, offset) + w[1] * at(SLOPE + 1, offset) + w[2] * at(SLOPE + 2, offset)
        )
        means = means + mean
        coupling[n, plane, out, :] = drop * slope - mean
    flux = [flux[c] + mob[c] * drops for c in range(3)]
    rate = relax_weight / (means + own_slope * drops)
    right = read(base, (), here) + (w[0] * flux[0] + w[1] * flux[1] + w[2] * flux[2])
    scale[plane, out, :] = rate
    start[plane, out, :] = -rate * right
    return flux


def inner(x_axis, local, columns, xa, xb, *refs):
    tabs, results, halo_results, store = refs[0], refs[1:4], refs[4:7], refs[7]
    edges, arrays, halo, centre = refs[8:18], refs[18:23], refs[23:28], refs[28]
    planes, rows, depth = local.shape[1:]
    total = planes + 2 * W
    even_x = parity_of(x_axis)
    tiles = range(rows // 8)

    def cells(get, plane, is_columns=False):
        for tile in tiles:
            span = slice(8 * tile, 8 * tile + 8)
            to = slice(8 + 8 * tile, 16 + 8 * tile)

            def put(ref, lead, values, change=None):
                at = (*lead, to, slice(None))
                ref[at] = values if change is None else change(ref[at])

            properties(lambda c: get(c, span), plane, is_columns, put, tabs, arrays, halo, centre, span)

    cells(lambda c, span: columns[c, span, :], 0, True)

    @pl.loop(0, planes)
    def _(x):
        cells(lambda c, span: local[c, x, span, :], W + x)

    def from_x(n, low):
        a, b = xa, xb
        def get(c, span):
            i = n(c)
            if i is None:
                return jnp.zeros((8, depth), f32)
            u, v = xa[i, span, :], xb[i, span, :]
            return pick(even_x, v, u) if low else pick(even_x, u, v)
        return get

    @pl.loop(0, NEAR)
    def _(q):
        near = lambda c: c * NEAR + q
        cells(from_x(near, True), 1 + q)
        cells(from_x(near, False), W + planes + q)

    far = lambda c: CHANNELS * NEAR + c if c < FAR else None
    cells(from_x(far, True), 0)
    cells(from_x(far, False), total - 1)

    def hand_on(sources, targets, plane):
        for source, target in zip(sources, targets):
            for lead in itertools.product(*(range(n) for n in source.shape[:-3])):
                last = source[(*lead, plane, slice(6 + rows, 8 + rows), slice(None))]
                head = source[(*lead, plane, slice(8, 10), slice(None))]
                target[(*lead, plane, pl.ds(0, 2, stride=2), slice(None))] = last
                target[(*lead, plane, pl.ds(RING - 3, 2, stride=2), slice(None))] = head

    hand_on(halo, edges[5:], 0)

    @pl.loop(0, total)
    def _(plane):
        hand_on(arrays, edges[:5], plane)

    def links(plane, is_columns=False):
        for tile in tiles:
            out = slice(8 * tile, 8 * tile + 8)
            own = (halo, out, halo_results) if is_columns else (arrays, out, results)
            res = link_cells(plane, is_columns, 8 + 8 * tile, 1, *own)
            if not is_columns:
                for c in range(3):
                    store[c, plane, out, :] = res[c]

    links(0, True)

    @pl.loop(1, total - 1)
    def _(plane):
        links(plane)


RING = 2 * (W + 2)


def finish(axis, count_y, local, *refs):
    tabs, accum, ys = refs[0], refs[1], refs[2 : 2 + count_y]
    refs = refs[2 + count_y :]
    results, halo_results, store = refs[:3], refs[3:6], refs[6]
    residual, update = refs[17:19]
    arrays, halo = refs[19:24], refs[24:29]
    edge_store, raw, centre = refs[29:32]
    edge_results, edge_halo_results = refs[32:35], refs[35:38]
    sols, halo_sols, edge_sols, edge_halo_sols = (refs[38 + 2 * i : 40 + 2 * i] for i in range(4))
    planes, rows, depth = local.shape[1:]
    total = planes + 2 * W
    even_y = parity_of(axis)

    def halo_rows(c, plane, n):
        low = high = jnp.zeros((W, depth), f32)
        if count_y:
            a = ys[0][n]
            b = ys[1][n] if count_y > 1 else None
            low, high = pick(even_y, b, a), pick(even_y, a, b)
        raw[c, plane, 0:W, :] = low
        raw[c, plane, W : 2 * W, :] = high

    base = CHANNELS * planes

    @pl.loop(0, CHANNELS)
    def _(c):
        for x in range(planes):
            halo_rows(c, W + x, c * planes + x)
        for q in range(NEAR):
            halo_rows(c, 1 + q, base + c * NEAR + q)
            halo_rows(c, W + planes + q, base + XMAIN + c * NEAR + q)
        halo_rows(c, total, base + 2 * XMAIN + c)

    @pl.loop(0, FAR)
    def _(c):
        halo_rows(c, 0, base + CHANNELS * NEAR + c)
        halo_rows(c, total - 1, base + XMAIN + CHANNELS * NEAR + c)

    for c in range(FAR, CHANNELS):
        for plane in (0, total - 1):
            raw[c, plane] = jnp.zeros((2 * W, depth), f32)

    def cells(plane, is_columns=False):
        def put(ref, lead, values, change=None):
            low = (*lead, pl.ds(1, W, stride=2), slice(None))
            high = (*lead, pl.ds(4, W, stride=2), slice(None))
            if change is not None:
                values = change(jnp.concatenate([ref[low], ref[high]], axis=0))
            ref[low] = values[:W]
            ref[high] = values[W:]

        get = lambda c: raw[c, plane, :, :]
        properties(
            get, 0 if is_columns else plane, is_columns, put, tabs, arrays, halo, centre, slice(0, 8)
        )

    cells(total, True)

    @pl.loop(0, total, unroll=2)
    def _(plane):
        cells(plane)

    def links(plane, is_columns=False):
        out = slice(0, 8)
        own = (halo, out, edge_halo_results) if is_columns else (arrays, out, edge_results)
        res = link_cells(plane, is_columns, 2, 2, *own)
        if not is_columns:
            for c in range(3):
                edge_store[c, plane] = res[c]

    links(0, True)

    @pl.loop(1, total - 1)
    def _(plane):
        links(plane)

    tiles = rows // 8

    row = lax.broadcasted_iota(jnp.int32, (8, depth), 0)

    def merged(mains, edge):
        first, last = pltpu.roll(edge, 1, 0), pltpu.roll(edge, 7, 0)
        mains = [jnp.where(row == 0, first, mains[0])] + mains[1:]
        return mains[:-1] + [jnp.where(row == 7, last, mains[-1])]

    def put_parts(is_columns, slot, step, plane, mains, edge):
        to, edge_to = (
            (halo_sols[slot], edge_halo_sols[slot]) if is_columns else (sols[slot], edge_sols[slot])
        )
        for tile, values in enumerate(mains):
            to[step + 1, plane, 8 + 8 * tile : 16 + 8 * tile, :] = values
        edge_to[step + 1, plane, 2:10, :] = edge
        to[step + 1, plane, 7:8, :] = edge[5:6]
        to[step + 1, plane, 8 + rows : 9 + rows, :] = edge[2:3]
        edge_to[step + 1, plane, 0:1, :] = mains[-1][6:7]
        edge_to[step + 1, plane, RING - 1 : RING, :] = mains[0][1:2]

    def halo_parts(slot, step):
        mains = [
            halo_sols[slot][step + 1, 0, 8 + 8 * tile : 16 + 8 * tile, :] for tile in range(tiles)
        ]
        return mains, edge_halo_sols[slot][step + 1, 0, 2:10, :]

    def put_solution(slot, plane, mains, edge, is_columns=False):
        mains = merged(mains, edge)
        put_parts(is_columns, slot, 0, plane, mains, edge)
        for step in (-1, 1):
            if is_columns:
                shift = lambda values: z_shift_columns(values, step)
                put_parts(True, slot, step, plane, [shift(u) for u in mains], shift(edge))
                continue
            shift = lambda u, v: z_shift(u, v, plane, step)
            halo_mains, halo_edge = halo_parts(slot, 0)
            shifted = [shift(u, v) for u, v in zip(mains, halo_mains)]
            put_parts(False, slot, step, plane, shifted, shift(edge, halo_edge))
            shift = lambda u, v: z_edge(u, v, plane, step)
            halo_mains, halo_edge = halo_parts(slot, step)
            shifted = [shift(u, v) for u, v in zip(halo_mains, mains)]
            put_parts(True, slot, step, 0, shifted, shift(halo_edge, edge))

    def relaxed(slot, plane, tile, is_columns=False):
        if tile is None:
            ref = (edge_halo_sols if is_columns else edge_sols)[slot]
            first, stride, out = 2, 2, slice(0, 8)
            coupling, scale, start = edge_halo_results if is_columns else edge_results
        else:
            ref = (halo_sols if is_columns else sols)[slot]
            first, stride = 8 + 8 * tile, 1
            out = slice(8 * tile, 8 * tile + 8)
            coupling, scale, start = halo_results if is_columns else results

        def get(offset):
            dx = 0 if is_columns else offset[0]
            values = ref[offset[2] + 1, plane + dx, pl.ds(first + stride * offset[1], 8), :]
            return x_roll(values, offset[0], is_columns)

        parts = [jnp.zeros((8, depth), f32) for _ in range(2)]
        for n, offset in enumerate(neighbour_offsets):
            parts[n % 2] = parts[n % 2] + coupling[n, plane, out, :] * get(offset)
        return (
            (1.0 - relax_weight) * get((0, 0, 0))
            + start[plane, out, :]
            - scale[plane, out, :] * (parts[0] + parts[1])
        )

    def first_sweep(plane, is_columns=False):
        start = (halo_results if is_columns else results)[2]
        edge = (edge_halo_results if is_columns else edge_results)[2]
        mains = [start[plane, 8 * tile : 8 * tile + 8, :] for tile in range(tiles)]
        put_solution(0, plane, mains, edge[plane], is_columns)

    first_sweep(0, True)

    @pl.loop(1, total - 1, unroll=2)
    def _(plane):
        first_sweep(plane)

    def sweep_of(slot, plane, is_columns=False):
        mains = [relaxed(slot, plane, tile, is_columns) for tile in range(tiles)]
        put_solution(1 - slot, plane, mains, relaxed(slot, plane, None, is_columns), is_columns)

    for sweep in range(2, SWEEPS):
        slot = sweep % 2
        sweep_of(slot, 0, True)

        @pl.loop(sweep, total - sweep, unroll=2)
        def _(plane):
            sweep_of(slot, plane)

    @pl.loop(0, planes, unroll=2)
    def _(x):
        slot, plane = SWEEPS % 2, W + x
        edge = relaxed(slot, plane, None)
        for tile in range(tiles):
            span = slice(8 * tile, 8 * tile + 8)
            update[x, span, :] = relaxed(slot, plane, tile)
            active = local[3, x, span, :]
            for c in range(3):
                flow = store[c, plane, span, :]
                residual[c, x, span, :] = active * (accum[c, x, span, :] + flow)
        for row_of, edge_row in ((0, 7), (rows - 1, 0)):
            to, source = slice(row_of, row_of + 1), slice(edge_row, edge_row + 1)
            update[x, to, :] = edge[source]
            active = local[3, x, to, :]
            for c in range(3):
                flow = edge_store[c, plane, source, :]
                residual[c, x, to, :] = active * (accum[c, x, to, :] + flow)


def call(kernel, name, mib, **options):
    return pl.pallas_call(
        kernel,
        name=name,
        compiler_params=pltpu.CompilerParams(vmem_limit_bytes=mib << 20),
        **options,
    )


def cell_shapes(total, height, depth):
    return [
        (*lead, count, height, depth)
        for count in (total, 1)
        for lead in ((SHIFTED, 3), (UP,), (UP,), (3,), ())
    ]


def result_shapes(total, height, depth):
    return [
        shape
        for count in (total, 1)
        for shape in ((2 * UP, count, height, depth), (count, height, depth), (count, height, depth))
    ]


def body(
    cell_state,
    old_mass,
    pore_volume,
    transmissibility,
    active_mask,
    pvt_region,
    formation_factor,
    compressibility,
    inverse_viscosity,
):
    ax, ay, az = "gx", "gy", "gz"
    planes, rows, depth = pore_volume.shape
    total = planes + 2 * W
    per, groups = groups_of(planes, depth)
    assert per >= 1 and 2 * W * total <= depth and rows % 8 == 0 and RING <= 16
    tables = (formation_factor, compressibility, inverse_viscosity)
    like = lambda *shape: jax.ShapeDtypeStruct(shape, f32)
    fill = lambda shape, got: [jnp.zeros(shape.shape, f32) if one is None else one for one in got]

    arguments = (
        *(cell_state, old_mass, pore_volume, transmissibility, active_mask, pvt_region),
        *tables,
    )
    z_shape = like(groups, rows, depth)
    cells = like(3, planes, rows, depth)
    local, accum, tabs, *z_send = call(
        functools.partial(pack_z, az),
        "pack_z",
        8,
        out_shape=(like(CHANNELS, planes, rows, depth), cells, like(9, 8, depth), z_shape, z_shape),
        in_specs=[HBM] * 9,
        out_specs=(VMEM,) * 5,
        scratch_shapes=[
            pltpu.VMEM((2, planes, rows, depth), jnp.int32),
            pltpu.VMEM(cells.shape, f32),
            pltpu.VMEM((planes, rows, depth), f32),
            pltpu.VMEM((3, *formation_factor.shape), f32),
            pltpu.SemaphoreType.DMA((10,)),
        ],
    )(*(pltpu.with_memory_space_constraint(array, pltpu.MemorySpace.HBM) for array in arguments))
    za, zb = fill(z_shape, swaps(az, *z_send))

    _, groups_x = groups_of(W, depth)
    x_shape = like(XMAIN + groups_x, rows, depth)
    x_send = call(
        functools.partial(pack_x, ax), "pack_x", 8, out_shape=(x_shape, x_shape)
    )(local)
    x_send = call(
        functools.partial(join_x, ax, planes),
        "join_x",
        8,
        out_shape=(x_shape, x_shape),
        in_specs=[VMEM, VMEM, ANY, ANY],
        out_specs=(ANY, ANY),
        scratch_shapes=[
            pltpu.VMEM((2, groups_x, rows, depth), f32),
            pltpu.SemaphoreType.DMA((2,)),
        ],
        input_output_aliases={2: 0, 3: 1},
    )(za, zb, *x_send)
    xa, xb = fill(x_shape, swaps(ax, *x_send))

    count_y = min(lax.axis_size(ay) - 1, 2)
    extra = 2 * XMAIN + CHANNELS
    y_shape = like(CHANNELS * planes + extra, W, depth)
    y_send = ()
    if count_y:
        y_send = call(
            functools.partial(pack_y, ay), "pack_y", 8, out_shape=(y_shape,) * count_y
        )(local)
    *y_send, columns = call(
        functools.partial(join_y, ay, ax, count_y, planes),
        "join_y",
        8,
        out_shape=(y_shape,) * count_y + (like(CHANNELS, rows, depth),),
        in_specs=[VMEM] * 4 + [ANY] * count_y,
        out_specs=(ANY,) * count_y + (VMEM,),
        scratch_shapes=[pltpu.VMEM((extra, W, depth), f32)] * count_y
        + [pltpu.SemaphoreType.DMA((max(count_y, 1),))],
        input_output_aliases={4 + i: i for i in range(count_y)},
    )(za, zb, xa, xb, *y_send)
    ys = swaps(ay, y_send[0], y_send[-1])[:count_y] if count_y else []

    vmem = lambda shapes: [pltpu.VMEM(shape, f32) for shape in shapes]
    flow = (3, total, rows, depth)
    edges = cell_shapes(total, 16, depth)
    shapes = result_shapes(total, rows, depth) + [flow] + edges
    halves = call(
        functools.partial(inner, ax),
        "inner",
        24,
        out_shape=[like(*shape) for shape in shapes],
        in_specs=[VMEM] * 5,
        out_specs=[VMEM] * len(shapes),
        scratch_shapes=vmem(cell_shapes(total, rows + 16, depth) + [(SHIFTED + UP, rows, depth)]),
    )(local, columns, xa, xb, tabs)

    solutions = [
        (3, count, height, depth) for height in (rows + 16, 16) for count in (total, 1) for _ in range(2)
    ]
    before = 3 + count_y + 7
    residual, update, *_ = call(
        functools.partial(finish, ay, count_y),
        "finish",
        24,
        out_shape=[cells, like(planes, rows, depth)] + [like(*shape) for shape in edges],
        in_specs=[VMEM] * (before + len(edges)),
        out_specs=[VMEM] * (2 + len(edges)),
        scratch_shapes=vmem(
            [
                (3, total, 8, depth),
                (CHANNELS, total + 1, 2 * W, depth),
                (SHIFTED + UP, 2 * W, depth),
                *result_shapes(total, 8, depth),
                *solutions,
            ]
        ),
        input_output_aliases={before + i: 2 + i for i in range(len(edges))},
    )(local, tabs, accum, *ys, *halves)
    return residual, update


def solution(mesh):
    return jax.shard_map(
        body,
        mesh=mesh,
        in_specs=(
            P(None, "gx", "gy", "gz"),
            P(None, "gx", "gy", "gz"),
            P("gx", "gy", "gz"),
            P(None, "gx", "gy", "gz"),
            P("gx", "gy", "gz"),
            P("gx", "gy", "gz"),
            P(),
            P(),
            P(),
        ),
        out_specs=(P(None, "gx", "gy", "gz"), P("gx", "gy", "gz")),
        check_vma=False,
    )
```

```python
import functools
import itertools

import jax
import jax.numpy as jnp
from jax import lax
from jax.experimental import pallas as pl
from jax.experimental.pallas import tpu as pltpu
from jax.sharding import PartitionSpec as P

SWEEPS = 4
W = SWEEPS
relax_weight = 0.7

neighbour_offsets = [
    (along_x, along_y, along_z)
    for along_x in (-1, 0, 1)
    for along_y in (-1, 0, 1)
    for along_z in (-1, 0, 1)
    if (along_x, along_y, along_z) != (0, 0, 0)
]
upper_offsets = [offset for offset in neighbour_offsets if offset > (0, 0, 0)]
UP = len(upper_offsets)
FLAT = sum(1 for offset in upper_offsets if offset[0] == 0)
STEP = UP - FLAT

FAR = 5 + STEP
CHANNELS = FAR + FLAT + 2
STORAGE, OWN = FAR + FLAT, FAR + FLAT + 1
NEAR = W - 1
XMAIN = CHANNELS * NEAR + FAR
VMEM = pl.BlockSpec(memory_space=pltpu.VMEM)
ANY = pl.BlockSpec(memory_space=pl.ANY)
HBM = pl.BlockSpec(memory_space=pltpu.MemorySpace.HBM)
f32 = jnp.float32


def t_channel(k):
    return FAR + k if k < FLAT else 5 + k - FLAT


def pick(parity, even, odd):
    shape = (even if odd is None else odd).shape
    if even is None:
        even = jnp.zeros(shape, f32)
    if odd is None:
        odd = jnp.zeros(shape, f32)
    return jnp.where(jnp.full(shape, parity, jnp.int32) == 0, even, odd)


def parity_of(axis):
    return lax.rem(lax.axis_index(axis), 2)


def swaps(axis, first, second):
    count = lax.axis_size(axis)
    got = []
    for start, message in ((0, first), (1, second)):
        pairs = [(i, i + 1) for i in range(start, count - 1, 2)]
        if not pairs:
            got.append(None)
            continue
        got.append(lax.ppermute(message, axis, pairs + [(b, a) for a, b in pairs]))
    return got


def lanes_of(shape):
    return lax.broadcasted_iota(jnp.int32, shape, len(shape) - 1)


def span_of(planes):
    return 2 * W * planes


def groups_of(planes, depth):
    per = depth // span_of(planes)
    return per, -(-CHANNELS // per)


def lookups(tabs, region, numbers):
    index = region.astype(jnp.int32)
    return [
        jnp.take_along_axis(tabs[n], index, axis=1, mode="promise_in_bounds") for n in numbers
    ]


def pack_z(axis, *refs):
    state, mass, pore, trans, active, region, *tables = refs[:9]
    local, accum, tabs, first, second = refs[9:14]
    flags, masses, pores, small, sems = refs[14:]
    planes, rows, depth = pore.shape
    copies = [
        pltpu.make_async_copy(active, flags.at[0], sems.at[0]),
        pltpu.make_async_copy(region, flags.at[1], sems.at[1]),
        pltpu.make_async_copy(state, local.at[0:3], sems.at[2]),
        pltpu.make_async_copy(mass, masses, sems.at[3]),
        pltpu.make_async_copy(pore, pores, sems.at[4]),
    ]
    copies += [
        pltpu.make_async_copy(table, small.at[n], sems.at[5 + n]) for n, table in enumerate(tables)
    ]
    late = [
        pltpu.make_async_copy(trans.at[FLAT:UP], local.at[5:FAR], sems.at[8]),
        pltpu.make_async_copy(trans.at[0:FLAT], local.at[FAR : FAR + FLAT], sems.at[9]),
    ]
    for copy in copies + late:
        copy.start()
    for copy in copies:
        copy.wait()
    regions = tables[0].shape[1]
    for n in range(3):
        for c in range(3):
            tabs[3 * n + c, :, 0:regions] = jnp.broadcast_to(small[n, c : c + 1, :], (8, regions))
    for x in range(planes):
        for tile in range(rows // 8):
            span = slice(8 * tile, 8 * tile + 8)
            on = flags[0, x, span, :].astype(f32)
            level = flags[1, x, span, :]
            local[3, x, span, :] = on
            local[4, x, span, :] = level.astype(f32)
            press, water, gas = (local[c, x, span, :] for c in range(3))
            look = lookups(tabs, level, range(6))
            sat = (water, 1.0 - water - gas, gas)
            expand = [look[c] * jnp.exp(look[3 + c] * (press - 0.5)) for c in range(3)]
            volume = pores[x, span, :]
            stored = volume * (look[3] * sat[0] + look[4] * sat[1] + look[5] * sat[2])
            stored = jnp.where(on > 0, stored, 1.0)
            own = jnp.zeros((8, depth), f32)
            for c in range(3):
                value = volume * expand[c] * sat[c] - masses[c, x, span, :]
                accum[c, x, span, :] = value
                own = own + value / (expand[c] * stored)
            local[STORAGE, x, span, :] = stored
            local[OWN, x, span, :] = on * own
    for copy in late:
        copy.wait()

    per, groups = groups_of(planes, depth)
    even = parity_of(axis)
    lane = lanes_of((8, depth))

    @pl.loop(0, rows // 8)
    def _(tile):
        span = pl.ds(pl.multiple_of(8 * tile, 8), 8)
        for group in range(groups):
            high = jnp.zeros((8, depth), f32)
            low = jnp.zeros((8, depth), f32)
            for c in range(group * per, min(CHANNELS, group * per + per)):
                for x in range(planes):
                    base = (c % per) * span_of(planes) + 2 * W * x
                    values = local[c, x, span, :]
                    here = (lane >= base + W) & (lane < base + 2 * W)
                    high = jnp.where(here, pltpu.roll(values, (base + 2 * W) % depth, 1), high)
                    here = (lane >= base) & (lane < base + W)
                    low = jnp.where(here, pltpu.roll(values, base % depth, 1), low)
            first[group, span, :] = pick(even, high, low)
            second[group, span, :] = pick(even, low, high)


def pack_x(axis, local, *outs):
    planes = local.shape[1]
    even = parity_of(axis)
    for out, up in zip(outs, (even == 0, even != 0)):
        near = jnp.where(up, planes - NEAR, 0)
        far = jnp.where(up, planes - W, W - 1)
        for c in range(CHANNELS):
            for q in range(NEAR):
                out[c * NEAR + q] = local[c, near + q]
            if c < FAR:
                out[CHANNELS * NEAR + c] = local[c, far]


def put_rows(outs, n, values, even):
    head, tail = values[:W], values[values.shape[0] - W :]
    for out, up, down in zip(outs, (tail, head), (head, tail)):
        out[n] = pick(even, up, down)


def join_x(axis, y_axis, za, zb, local, *outs):
    planes = local.shape[1]
    even_y = parity_of(y_axis)
    for c in range(CHANNELS):
        for x in range(planes):
            put_rows(outs[2:], c * planes + x, local[c, x], even_y)
    rows, depth = za.shape[1:]
    even = parity_of(axis)
    per, _ = groups_of(planes, depth)
    per_x, groups_x = groups_of(W, depth)
    lane = lanes_of((rows, depth))
    for group in range(groups_x):
        sides = [jnp.zeros((rows, depth), f32) for _ in range(2)]
        for c in range(group * per_x, min(CHANNELS, group * per_x + per_x)):
            values = za[c // per] + zb[c // per]
            to = (c % per_x) * span_of(W)
            here = (lane >= to) & (lane < to + span_of(W))
            for n, plane in enumerate((planes - W, 0)):
                source = (c % per) * span_of(planes) + 2 * W * plane
                sides[n] = jnp.where(here, pltpu.roll(values, (to - source) % depth, 1), sides[n])
        outs[0][group] = pick(even, *sides)
        outs[1][group] = pick(even, *sides[::-1])


def join_y(axis, x_axis, planes, za, zb, xa, xb, ca, cb, *refs):
    count = len(refs) // 2
    columns, *outs = refs[count:]
    rows, depth = xa.shape[1:]
    even = parity_of(axis)
    even_x = parity_of(x_axis)
    per, _ = groups_of(planes, depth)
    per_x, _ = groups_of(W, depth)
    lane = lanes_of((rows, depth))
    for c in range(CHANNELS):
        group, base = c // per, (c % per) * span_of(planes)
        own = pltpu.roll(za[group] + zb[group], (2 * W * W - base) % depth, 1)
        group, base = c // per_x, (c % per_x) * span_of(W)
        a, b = ca[group], cb[group]
        below = pltpu.roll(pick(even_x, b, a), (depth - base) % depth, 1)
        above = pltpu.roll(pick(even_x, a, b), (2 * W * (planes + W) - base) % depth, 1)
        values = jnp.where(lane < 2 * W * W, below, jnp.where(lane < 2 * W * (W + planes), own, above))
        columns[c] = values
        put_rows(outs, 2 * XMAIN + c, values, even)

    @pl.loop(0, XMAIN // 2)
    def _(i):
        for j in range(2):
            n = 2 * i + j
            a, b = xa[n], xb[n]
            put_rows(outs, n, pick(even_x, b, a), even)
            put_rows(outs, XMAIN + n, pick(even_x, a, b), even)


PRESS, MOB, SLOPE, ACT = 0, 1, 4, 7
SHIFTED = 8


def z_shift(values, columns, plane, step):
    depth = values.shape[-1]
    lane = lanes_of(values.shape)
    if step > 0:
        edge = pltpu.roll(columns, depth - 1 - 2 * W * plane, 1)
        return jnp.where(lane == depth - 1, edge, pltpu.roll(values, depth - 1, 1))
    edge = pltpu.roll(columns, depth - 2 * W * plane - 2 * W + 1, 1)
    return jnp.where(lane == 0, edge, pltpu.roll(values, 1, 1))


def z_shift_columns(values, step):
    return pltpu.roll(values, values.shape[-1] - 1 if step > 0 else 1, 1)


def z_edge(current, values, plane, step):
    lane = lanes_of(values.shape)
    if step > 0:
        at = 2 * W * plane + 2 * W - 1
        return jnp.where(lane == at, pltpu.roll(values, at, 1), current)
    at = 2 * W * plane
    return jnp.where(lane == at, pltpu.roll(values, at + 1, 1), current)


def properties(get, plane, is_columns, put, tabs, arrays, halo, centre, span):
    fields, lower, half, weight, base = halo if is_columns else arrays
    halo_fields, halo_lower = halo[:2]
    press, water, gas, active, region = (get(c) for c in range(5))
    look = lookups(tabs, region, range(9))
    formation, compress, viscous = look[:3], look[3:6], look[6:]
    sat = (water, 1.0 - water - gas, gas)
    expand = [formation[c] * jnp.exp(compress[c] * (press - 0.5)) for c in range(3)]
    mob = [viscous[c] * expand[c] * sat[c] * sat[c] for c in range(3)]
    stored = get(STORAGE)
    stored = jnp.where(stored > 0, stored, 1.0)
    for c in range(3):
        put(weight, (c, plane), active / (expand[c] * stored))
    put(base, (plane,), get(OWN))
    shifts = []
    one = [press] + mob + [compress[c] * mob[c] for c in range(3)] + [active]
    for f, values in enumerate(one):
        put(fields, (f, 1, plane), values)
        shifts += [(0, (f, step + 1), step, values, f) for step in (-1, 1)]
    for k, offset in enumerate(upper_offsets):
        values = 0.5 * get(t_channel(k))
        put(half, (k, plane), values)
        values = values * active
        if offset[2] == 0:
            put(lower, (k, plane), values)
        else:
            shifts.append((1, (k,), -offset[2], values, SHIFTED + k))
    for array, lead, step, values, slot in shifts:
        if is_columns:
            centre[slot, span, :] = values
            put((fields, lower)[array], (*lead, 0), z_shift_columns(values, step))
        else:
            put((fields, lower)[array], (*lead, plane), z_shift(values, centre[slot, span, :], plane, step))
            put((halo_fields, halo_lower)[array], (*lead, 0), None, lambda now: z_edge(now, values, plane, step))


def x_roll(values, step, is_columns):
    if not is_columns or step == 0:
        return values
    depth = values.shape[-1]
    return pltpu.roll(values, (depth - 2 * W * step) % depth, 1)


def link_cells(plane, is_columns, first, stride, arrays, out, results):
    fields, lower, half, weight, base = arrays
    coupling, scale, start = results
    depth = fields.shape[-1]
    here = (0, 0, 0)

    def read(ref, lead, offset):
        dx = 0 if is_columns else offset[0]
        values = ref[(*lead, plane + dx, pl.ds(first + stride * offset[1], 8), slice(None))]
        return x_roll(values, offset[0], is_columns)

    def at(f, offset):
        return read(fields, (f, offset[2] + 1), offset)

    press = at(PRESS, here)
    w = [read(weight, (c,), here) for c in range(3)]
    mob = [at(MOB + c, here) for c in range(3)]
    own_mob = w[0] * mob[0] + w[1] * mob[1] + w[2] * mob[2]
    own_slope = w[0] * at(SLOPE, here) + w[1] * at(SLOPE + 1, here) + w[2] * at(SLOPE + 2, here)
    flux = [jnp.zeros((8, depth), f32) for _ in range(3)]
    drops = jnp.zeros((8, depth), f32)
    means = jnp.ones((8, depth), f32)
    for n, offset in enumerate(neighbour_offsets):
        if offset > here:
            link = read(half, (upper_offsets.index(offset),), here) * at(ACT, offset)
        else:
            k = upper_offsets.index(tuple(-o for o in offset))
            link = read(lower, (k,), offset)
        drop = link * (press - at(PRESS, offset))
        other = [at(MOB + c, offset) for c in range(3)]
        for c in range(3):
            flux[c] = flux[c] + drop * other[c]
        drops = drops + drop
        mean = link * (own_mob + (w[0] * other[0] + w[1] * other[1] + w[2] * other[2]))
        slope = (
            w[0] * at(SLOPE, offset) + w[1] * at(SLOPE + 1, offset) + w[2] * at(SLOPE + 2, offset)
        )
        means = means + mean
        coupling[n, plane, out, :] = drop * slope - mean
    flux = [flux[c] + mob[c] * drops for c in range(3)]
    rate = relax_weight / (means + own_slope * drops)
    right = read(base, (), here) + (w[0] * flux[0] + w[1] * flux[1] + w[2] * flux[2])
    scale[plane, out, :] = rate
    start[plane, out, :] = -rate * right
    return flux


def inner(x_axis, local, columns, xa, xb, *refs):
    tabs, results, halo_results, store = refs[0], refs[1:4], refs[4:7], refs[7]
    edges, arrays, halo, centre = refs[8:18], refs[18:23], refs[23:28], refs[28]
    planes, rows, depth = local.shape[1:]
    total = planes + 2 * W
    even_x = parity_of(x_axis)
    tiles = range(rows // 8)

    def cells(get, plane, is_columns=False):
        for tile in tiles:
            span = slice(8 * tile, 8 * tile + 8)
            to = slice(8 + 8 * tile, 16 + 8 * tile)

            def put(ref, lead, values, change=None):
                at = (*lead, to, slice(None))
                ref[at] = values if change is None else change(ref[at])

            properties(lambda c: get(c, span), plane, is_columns, put, tabs, arrays, halo, centre, span)

    cells(lambda c, span: columns[c, span, :], 0, True)

    @pl.loop(0, planes)
    def _(x):
        cells(lambda c, span: local[c, x, span, :], W + x)

    def from_x(n, low):
        a, b = xa, xb
        def get(c, span):
            i = n(c)
            if i is None:
                return jnp.zeros((8, depth), f32)
            u, v = xa[i, span, :], xb[i, span, :]
            return pick(even_x, v, u) if low else pick(even_x, u, v)
        return get

    @pl.loop(0, NEAR)
    def _(q):
        near = lambda c: c * NEAR + q
        cells(from_x(near, True), 1 + q)
        cells(from_x(near, False), W + planes + q)

    far = lambda c: CHANNELS * NEAR + c if c < FAR else None
    cells(from_x(far, True), 0)
    cells(from_x(far, False), total - 1)

    def hand_on(sources, targets, plane):
        for source, target in zip(sources, targets):
            for lead in itertools.product(*(range(n) for n in source.shape[:-3])):
                last = source[(*lead, plane, slice(6 + rows, 8 + rows), slice(None))]
                head = source[(*lead, plane, slice(8, 10), slice(None))]
                target[(*lead, plane, pl.ds(0, 2, stride=2), slice(None))] = last
                target[(*lead, plane, pl.ds(RING - 3, 2, stride=2), slice(None))] = head

    hand_on(halo, edges[5:], 0)

    @pl.loop(0, total)
    def _(plane):
        hand_on(arrays, edges[:5], plane)

    def links(plane, is_columns=False):
        for tile in tiles:
            out = slice(8 * tile, 8 * tile + 8)
            own = (halo, out, halo_results) if is_columns else (arrays, out, results)
            res = link_cells(plane, is_columns, 8 + 8 * tile, 1, *own)
            if not is_columns:
                for c in range(3):
                    store[c, plane, out, :] = res[c]

    links(0, True)

    @pl.loop(1, total - 1)
    def _(plane):
        links(plane)


RING = 2 * (W + 2)


def finish(axis, count_y, local, *refs):
    tabs, accum, ys, more_ys = refs[0], refs[1], refs[2 : 2 + count_y], refs[2 + count_y : 2 + 2 * count_y]
    refs = refs[2 + 2 * count_y :]
    results, halo_results, store = refs[:3], refs[3:6], refs[6]
    residual, update = refs[17:19]
    arrays, halo = refs[19:24], refs[24:29]
    edge_store, raw, centre = refs[29:32]
    edge_results, edge_halo_results = refs[32:35], refs[35:38]
    sols, halo_sols, edge_sols, edge_halo_sols = (refs[38 + 2 * i : 40 + 2 * i] for i in range(4))
    planes, rows, depth = local.shape[1:]
    total = planes + 2 * W
    even_y = parity_of(axis)

    def halo_rows(c, plane, sources, n):
        low = high = jnp.zeros((W, depth), f32)
        if count_y:
            a = sources[0][n]
            b = sources[1][n] if count_y > 1 else None
            low, high = pick(even_y, b, a), pick(even_y, a, b)
        raw[c, plane, 0:W, :] = low
        raw[c, plane, W : 2 * W, :] = high

    @pl.loop(0, CHANNELS)
    def _(c):
        for x in range(planes):
            halo_rows(c, W + x, ys, c * planes + x)
        for q in range(NEAR):
            halo_rows(c, 1 + q, more_ys, c * NEAR + q)
            halo_rows(c, W + planes + q, more_ys, XMAIN + c * NEAR + q)
        halo_rows(c, total, more_ys, 2 * XMAIN + c)

    @pl.loop(0, FAR)
    def _(c):
        halo_rows(c, 0, more_ys, CHANNELS * NEAR + c)
        halo_rows(c, total - 1, more_ys, XMAIN + CHANNELS * NEAR + c)

    for c in range(FAR, CHANNELS):
        for plane in (0, total - 1):
            raw[c, plane] = jnp.zeros((2 * W, depth), f32)

    def cells(plane, is_columns=False):
        def put(ref, lead, values, change=None):
            low = (*lead, pl.ds(1, W, stride=2), slice(None))
            high = (*lead, pl.ds(4, W, stride=2), slice(None))
            if change is not None:
                values = change(jnp.concatenate([ref[low], ref[high]], axis=0))
            ref[low] = values[:W]
            ref[high] = values[W:]

        get = lambda c: raw[c, plane, :, :]
        properties(
            get, 0 if is_columns else plane, is_columns, put, tabs, arrays, halo, centre, slice(0, 8)
        )

    cells(total, True)

    @pl.loop(0, total, unroll=2)
    def _(plane):
        cells(plane)

    def links(plane, is_columns=False):
        out = slice(0, 8)
        own = (halo, out, edge_halo_results) if is_columns else (arrays, out, edge_results)
        res = link_cells(plane, is_columns, 2, 2, *own)
        if not is_columns:
            for c in range(3):
                edge_store[c, plane] = res[c]

    links(0, True)

    @pl.loop(1, total - 1)
    def _(plane):
        links(plane)

    tiles = rows // 8

    row = lax.broadcasted_iota(jnp.int32, (8, depth), 0)

    def merged(mains, edge):
        first, last = pltpu.roll(edge, 1, 0), pltpu.roll(edge, 7, 0)
        mains = [jnp.where(row == 0, first, mains[0])] + mains[1:]
        return mains[:-1] + [jnp.where(row == 7, last, mains[-1])]

    def put_parts(is_columns, slot, step, plane, mains, edge):
        to, edge_to = (
            (halo_sols[slot], edge_halo_sols[slot]) if is_columns else (sols[slot], edge_sols[slot])
        )
        for tile, values in enumerate(mains):
            to[step + 1, plane, 8 + 8 * tile : 16 + 8 * tile, :] = values
        edge_to[step + 1, plane, 2:10, :] = edge
        to[step + 1, plane, 7:8, :] = edge[5:6]
        to[step + 1, plane, 8 + rows : 9 + rows, :] = edge[2:3]
        edge_to[step + 1, plane, 0:1, :] = mains[-1][6:7]
        edge_to[step + 1, plane, RING - 1 : RING, :] = mains[0][1:2]

    def halo_parts(slot, step):
        mains = [
            halo_sols[slot][step + 1, 0, 8 + 8 * tile : 16 + 8 * tile, :] for tile in range(tiles)
        ]
        return mains, edge_halo_sols[slot][step + 1, 0, 2:10, :]

    def put_solution(slot, plane, mains, edge, is_columns=False):
        mains = merged(mains, edge)
        put_parts(is_columns, slot, 0, plane, mains, edge)
        for step in (-1, 1):
            if is_columns:
                shift = lambda values: z_shift_columns(values, step)
                put_parts(True, slot, step, plane, [shift(u) for u in mains], shift(edge))
                continue
            shift = lambda u, v: z_shift(u, v, plane, step)
            halo_mains, halo_edge = halo_parts(slot, 0)
            shifted = [shift(u, v) for u, v in zip(mains, halo_mains)]
            put_parts(False, slot, step, plane, shifted, shift(edge, halo_edge))
            shift = lambda u, v: z_edge(u, v, plane, step)
            halo_mains, halo_edge = halo_parts(slot, step)
            shifted = [shift(u, v) for u, v in zip(halo_mains, mains)]
            put_parts(True, slot, step, 0, shifted, shift(halo_edge, edge))

    def relaxed(slot, plane, tile, is_columns=False):
        if tile is None:
            ref = (edge_halo_sols if is_columns else edge_sols)[slot]
            first, stride, out = 2, 2, slice(0, 8)
            coupling, scale, start = edge_halo_results if is_columns else edge_results
        else:
            ref = (halo_sols if is_columns else sols)[slot]
            first, stride = 8 + 8 * tile, 1
            out = slice(8 * tile, 8 * tile + 8)
            coupling, scale, start = halo_results if is_columns else results

        def get(offset):
            dx = 0 if is_columns else offset[0]
            values = ref[offset[2] + 1, plane + dx, pl.ds(first + stride * offset[1], 8), :]
            return x_roll(values, offset[0], is_columns)

        parts = [jnp.zeros((8, depth), f32) for _ in range(2)]
        for n, offset in enumerate(neighbour_offsets):
            parts[n % 2] = parts[n % 2] + coupling[n, plane, out, :] * get(offset)
        return (
            (1.0 - relax_weight) * get((0, 0, 0))
            + start[plane, out, :]
            - scale[plane, out, :] * (parts[0] + parts[1])
        )

    def first_sweep(plane, is_columns=False):
        start = (halo_results if is_columns else results)[2]
        edge = (edge_halo_results if is_columns else edge_results)[2]
        mains = [start[plane, 8 * tile : 8 * tile + 8, :] for tile in range(tiles)]
        put_solution(0, plane, mains, edge[plane], is_columns)

    first_sweep(0, True)

    @pl.loop(1, total - 1, unroll=2)
    def _(plane):
        first_sweep(plane)

    def sweep_of(slot, plane, is_columns=False):
        mains = [relaxed(slot, plane, tile, is_columns) for tile in range(tiles)]
        put_solution(1 - slot, plane, mains, relaxed(slot, plane, None, is_columns), is_columns)

    for sweep in range(2, SWEEPS):
        slot = sweep % 2
        sweep_of(slot, 0, True)

        @pl.loop(sweep, total - sweep, unroll=2)
        def _(plane):
            sweep_of(slot, plane)

    @pl.loop(0, planes, unroll=2)
    def _(x):
        slot, plane = SWEEPS % 2, W + x
        edge = relaxed(slot, plane, None)
        for tile in range(tiles):
            span = slice(8 * tile, 8 * tile + 8)
            update[x, span, :] = relaxed(slot, plane, tile)
            active = local[3, x, span, :]
            for c in range(3):
                flow = store[c, plane, span, :]
                residual[c, x, span, :] = active * (accum[c, x, span, :] + flow)
        for row_of, edge_row in ((0, 7), (rows - 1, 0)):
            to, source = slice(row_of, row_of + 1), slice(edge_row, edge_row + 1)
            update[x, to, :] = edge[source]
            active = local[3, x, to, :]
            for c in range(3):
                flow = edge_store[c, plane, source, :]
                residual[c, x, to, :] = active * (accum[c, x, to, :] + flow)


def call(kernel, name, mib, **options):
    return pl.pallas_call(
        kernel,
        name=name,
        compiler_params=pltpu.CompilerParams(vmem_limit_bytes=mib << 20),
        **options,
    )


def cell_shapes(total, height, depth):
    return [
        (*lead, count, height, depth)
        for count in (total, 1)
        for lead in ((SHIFTED, 3), (UP,), (UP,), (3,), ())
    ]


def result_shapes(total, height, depth):
    return [
        shape
        for count in (total, 1)
        for shape in ((2 * UP, count, height, depth), (count, height, depth), (count, height, depth))
    ]


def body(
    cell_state,
    old_mass,
    pore_volume,
    transmissibility,
    active_mask,
    pvt_region,
    formation_factor,
    compressibility,
    inverse_viscosity,
):
    ax, ay, az = "gx", "gy", "gz"
    planes, rows, depth = pore_volume.shape
    total = planes + 2 * W
    per, groups = groups_of(planes, depth)
    assert per >= 1 and 2 * W * total <= depth and rows % 8 == 0 and RING <= 16
    tables = (formation_factor, compressibility, inverse_viscosity)
    like = lambda *shape: jax.ShapeDtypeStruct(shape, f32)
    fill = lambda shape, got: [jnp.zeros(shape.shape, f32) if one is None else one for one in got]

    arguments = (
        *(cell_state, old_mass, pore_volume, transmissibility, active_mask, pvt_region),
        *tables,
    )
    z_shape = like(groups, rows, depth)
    cells = like(3, planes, rows, depth)
    local, accum, tabs, *z_send = call(
        functools.partial(pack_z, az),
        "pack_z",
        8,
        out_shape=(like(CHANNELS, planes, rows, depth), cells, like(9, 8, depth), z_shape, z_shape),
        in_specs=[HBM] * 9,
        out_specs=(VMEM,) * 5,
        scratch_shapes=[
            pltpu.VMEM((2, planes, rows, depth), jnp.int32),
            pltpu.VMEM(cells.shape, f32),
            pltpu.VMEM((planes, rows, depth), f32),
            pltpu.VMEM((3, *formation_factor.shape), f32),
            pltpu.SemaphoreType.DMA((10,)),
        ],
    )(*(pltpu.with_memory_space_constraint(array, pltpu.MemorySpace.HBM) for array in arguments))
    za, zb = fill(z_shape, swaps(az, *z_send))

    x_shape = like(XMAIN, rows, depth)
    x_send = call(functools.partial(pack_x, ax), "pack_x", 8, out_shape=(x_shape, x_shape))(local)
    xa, xb = fill(x_shape, swaps(ax, *x_send))

    count_y = min(lax.axis_size(ay) - 1, 2)
    ys, more_ys = [], []
    c_shape = like(groups_of(W, depth)[1], rows, depth)
    sent = call(
        functools.partial(join_x, ax, ay),
        "join_x",
        8,
        out_shape=(c_shape, c_shape) + (like(CHANNELS * planes, W, depth),) * count_y,
    )(za, zb, local)
    c_send, y_send = sent[:2], sent[2:]
    ca, cb = fill(c_shape, swaps(ax, *c_send))
    if count_y:
        ys = swaps(ay, y_send[0], y_send[-1])[:count_y]
    columns, *y_send = call(
        functools.partial(join_y, ay, ax, planes),
        "join_y",
        8,
        out_shape=(like(CHANNELS, rows, depth),)
        + (like(2 * XMAIN + CHANNELS, W, depth),) * count_y,
        in_specs=[VMEM] * 6 + [ANY] * count_y,
    )(za, zb, xa, xb, ca, cb, *ys)
    if count_y:
        more_ys = swaps(ay, y_send[0], y_send[-1])[:count_y]

    vmem = lambda shapes: [pltpu.VMEM(shape, f32) for shape in shapes]
    flow = (3, total, rows, depth)
    edges = cell_shapes(total, 16, depth)
    shapes = result_shapes(total, rows, depth) + [flow] + edges
    halves = call(
        functools.partial(inner, ax),
        "inner",
        24,
        out_shape=[like(*shape) for shape in shapes],
        in_specs=[VMEM] * 5,
        out_specs=[VMEM] * len(shapes),
        scratch_shapes=vmem(cell_shapes(total, rows + 16, depth) + [(SHIFTED + UP, rows, depth)]),
    )(local, columns, xa, xb, tabs)

    solutions = [
        (3, count, height, depth) for height in (rows + 16, 16) for count in (total, 1) for _ in range(2)
    ]
    before = 3 + 2 * count_y + 7
    residual, update, *_ = call(
        functools.partial(finish, ay, count_y),
        "finish",
        24,
        out_shape=[cells, like(planes, rows, depth)] + [like(*shape) for shape in edges],
        in_specs=[VMEM] * (before + len(edges)),
        out_specs=[VMEM] * (2 + len(edges)),
        scratch_shapes=vmem(
            [
                (3, total, 8, depth),
                (CHANNELS, total + 1, 2 * W, depth),
                (SHIFTED + UP, 2 * W, depth),
                *result_shapes(total, 8, depth),
                *solutions,
            ]
        ),
        input_output_aliases={before + i: 2 + i for i in range(len(edges))},
    )(local, tabs, accum, *ys, *more_ys, *halves)
    return residual, update


def solution(mesh):
    return jax.shard_map(
        body,
        mesh=mesh,
        in_specs=(
            P(None, "gx", "gy", "gz"),
            P(None, "gx", "gy", "gz"),
            P("gx", "gy", "gz"),
            P(None, "gx", "gy", "gz"),
            P("gx", "gy", "gz"),
            P("gx", "gy", "gz"),
            P(),
            P(),
            P(),
        ),
        out_specs=(P(None, "gx", "gy", "gz"), P("gx", "gy", "gz")),
        check_vma=False,
    )
```

```python
import functools
import itertools

import jax
import jax.numpy as jnp
from jax import lax
from jax.experimental import pallas as pl
from jax.experimental.pallas import tpu as pltpu
from jax.sharding import PartitionSpec as P

SWEEPS = 4
W = SWEEPS
relax_weight = 0.7

neighbour_offsets = [
    (along_x, along_y, along_z)
    for along_x in (-1, 0, 1)
    for along_y in (-1, 0, 1)
    for along_z in (-1, 0, 1)
    if (along_x, along_y, along_z) != (0, 0, 0)
]
upper_offsets = [offset for offset in neighbour_offsets if offset > (0, 0, 0)]
UP = len(upper_offsets)
FLAT = sum(1 for offset in upper_offsets if offset[0] == 0)
STEP = UP - FLAT

FAR = 5 + STEP
CHANNELS = FAR + FLAT + 2
STORAGE, OWN = FAR + FLAT, FAR + FLAT + 1
NEAR = W - 1
XMAIN = CHANNELS * NEAR + FAR
VMEM = pl.BlockSpec(memory_space=pltpu.VMEM)
ANY = pl.BlockSpec(memory_space=pl.ANY)
HBM = pl.BlockSpec(memory_space=pltpu.MemorySpace.HBM)
f32 = jnp.float32


def t_channel(k):
    return FAR + k if k < FLAT else 5 + k - FLAT


def pick(parity, even, odd):
    shape = (even if odd is None else odd).shape
    if even is None:
        even = jnp.zeros(shape, f32)
    if odd is None:
        odd = jnp.zeros(shape, f32)
    return jnp.where(jnp.full(shape, parity, jnp.int32) == 0, even, odd)


def parity_of(axis):
    return lax.rem(lax.axis_index(axis), 2)


def swaps(axis, first, second):
    count = lax.axis_size(axis)
    got = []
    for start, message in ((0, first), (1, second)):
        pairs = [(i, i + 1) for i in range(start, count - 1, 2)]
        if not pairs:
            got.append(None)
            continue
        got.append(lax.ppermute(message, axis, pairs + [(b, a) for a, b in pairs]))
    return got


def lanes_of(shape):
    return lax.broadcasted_iota(jnp.int32, shape, len(shape) - 1)


def span_of(planes):
    return 2 * W * planes


def groups_of(planes, depth):
    per = depth // span_of(planes)
    return per, -(-CHANNELS // per)


def lookups(tabs, region, numbers):
    index = region.astype(jnp.int32)
    return [
        jnp.take_along_axis(tabs[n], index, axis=1, mode="promise_in_bounds") for n in numbers
    ]


def pack_z(axis, *refs):
    state, mass, pore, trans, active, region, *tables = refs[:9]
    local, accum, tabs, first, second = refs[9:14]
    flags, masses, pores, small, sems = refs[14:]
    planes, rows, depth = pore.shape
    copies = [
        pltpu.make_async_copy(active, flags.at[0], sems.at[0]),
        pltpu.make_async_copy(region, flags.at[1], sems.at[1]),
        pltpu.make_async_copy(state, local.at[0:3], sems.at[2]),
        pltpu.make_async_copy(mass, masses, sems.at[3]),
        pltpu.make_async_copy(pore, pores, sems.at[4]),
    ]
    copies += [
        pltpu.make_async_copy(table, small.at[n], sems.at[5 + n]) for n, table in enumerate(tables)
    ]
    late = [
        pltpu.make_async_copy(trans.at[FLAT:UP], local.at[5:FAR], sems.at[8]),
        pltpu.make_async_copy(trans.at[0:FLAT], local.at[FAR : FAR + FLAT], sems.at[9]),
    ]
    for copy in copies + late:
        copy.start()
    for copy in copies:
        copy.wait()
    regions = tables[0].shape[1]
    for n in range(3):
        for c in range(3):
            tabs[3 * n + c, :, 0:regions] = jnp.broadcast_to(small[n, c : c + 1, :], (8, regions))
    for x in range(planes):
        for tile in range(rows // 8):
            span = slice(8 * tile, 8 * tile + 8)
            on = flags[0, x, span, :].astype(f32)
            level = flags[1, x, span, :]
            local[3, x, span, :] = on
            local[4, x, span, :] = level.astype(f32)
            press, water, gas = (local[c, x, span, :] for c in range(3))
            look = lookups(tabs, level, range(6))
            sat = (water, 1.0 - water - gas, gas)
            expand = [look[c] * jnp.exp(look[3 + c] * (press - 0.5)) for c in range(3)]
            volume = pores[x, span, :]
            stored = volume * (look[3] * sat[0] + look[4] * sat[1] + look[5] * sat[2])
            stored = jnp.where(on > 0, stored, 1.0)
            own = jnp.zeros((8, depth), f32)
            for c in range(3):
                value = volume * expand[c] * sat[c] - masses[c, x, span, :]
                accum[c, x, span, :] = value
                own = own + value / (expand[c] * stored)
            local[STORAGE, x, span, :] = stored
            local[OWN, x, span, :] = on * own
    for copy in late:
        copy.wait()

    per, groups = groups_of(planes, depth)
    even = parity_of(axis)
    lane = lanes_of((8, depth))

    @pl.loop(0, rows // 8)
    def _(tile):
        span = pl.ds(pl.multiple_of(8 * tile, 8), 8)
        for group in range(groups):
            high = jnp.zeros((8, depth), f32)
            low = jnp.zeros((8, depth), f32)
            for c in range(group * per, min(CHANNELS, group * per + per)):
                for x in range(planes):
                    base = (c % per) * span_of(planes) + 2 * W * x
                    values = local[c, x, span, :]
                    here = (lane >= base + W) & (lane < base + 2 * W)
                    high = jnp.where(here, pltpu.roll(values, (base + 2 * W) % depth, 1), high)
                    here = (lane >= base) & (lane < base + W)
                    low = jnp.where(here, pltpu.roll(values, base % depth, 1), low)
            first[group, span, :] = pick(even, high, low)
            second[group, span, :] = pick(even, low, high)


def pack_x(axis, local, *outs):
    planes = local.shape[1]
    even = parity_of(axis)
    for out, up in zip(outs, (even == 0, even != 0)):
        near = jnp.where(up, planes - NEAR, 0)
        far = jnp.where(up, planes - W, W - 1)
        for c in range(CHANNELS):
            for q in range(NEAR):
                out[c * NEAR + q] = local[c, near + q]
            if c < FAR:
                out[CHANNELS * NEAR + c] = local[c, far]


def put_rows(outs, n, values, even):
    head, tail = values[:W], values[values.shape[0] - W :]
    for out, up, down in zip(outs, (tail, head), (head, tail)):
        out[n] = pick(even, up, down)


def join_x(axis, y_axis, za, zb, local, *outs):
    planes = local.shape[1]
    even_y = parity_of(y_axis)
    for c in range(CHANNELS):
        for x in range(planes):
            put_rows(outs[2:], c * planes + x, local[c, x], even_y)
    rows, depth = za.shape[1:]
    even = parity_of(axis)
    per, _ = groups_of(planes, depth)
    per_x, groups_x = groups_of(W, depth)
    lane = lanes_of((rows, depth))
    for group in range(groups_x):
        sides = [jnp.zeros((rows, depth), f32) for _ in range(2)]
        for c in range(group * per_x, min(CHANNELS, group * per_x + per_x)):
            values = za[c // per] + zb[c // per]
            to = (c % per_x) * span_of(W)
            here = (lane >= to) & (lane < to + span_of(W))
            for n, plane in enumerate((planes - W, 0)):
                source = (c % per) * span_of(planes) + 2 * W * plane
                sides[n] = jnp.where(here, pltpu.roll(values, (to - source) % depth, 1), sides[n])
        outs[0][group] = pick(even, *sides)
        outs[1][group] = pick(even, *sides[::-1])


def join_y(axis, x_axis, planes, za, zb, xa, xb, ca, cb, *refs):
    count = len(refs) // 2
    columns, *outs = refs[count:]
    rows, depth = xa.shape[1:]
    even = parity_of(axis)
    even_x = parity_of(x_axis)
    per_x, _ = groups_of(W, depth)
    lane = lanes_of((rows, depth))
    for c in range(CHANNELS):
        own = own_columns(c, za, zb, planes, slice(0, rows))
        group, base = c // per_x, (c % per_x) * span_of(W)
        a, b = ca[group], cb[group]
        below = pltpu.roll(pick(even_x, b, a), (depth - base) % depth, 1)
        above = pltpu.roll(pick(even_x, a, b), (2 * W * (planes + W) - base) % depth, 1)
        values = jnp.where(lane < 2 * W * W, below, jnp.where(lane < 2 * W * (W + planes), own, above))
        columns[c] = values
        put_rows(outs, 2 * XMAIN + c, values, even)

    @pl.loop(0, XMAIN // 2)
    def _(i):
        for j in range(2):
            n = 2 * i + j
            a, b = xa[n], xb[n]
            put_rows(outs, n, pick(even_x, b, a), even)
            put_rows(outs, XMAIN + n, pick(even_x, a, b), even)


PRESS, MOB, SLOPE, ACT = 0, 1, 4, 7
SHIFTED = 8


def z_shift(values, columns, plane, step):
    depth = values.shape[-1]
    lane = lanes_of(values.shape)
    if step > 0:
        edge = pltpu.roll(columns, depth - 1 - 2 * W * plane, 1)
        return jnp.where(lane == depth - 1, edge, pltpu.roll(values, depth - 1, 1))
    edge = pltpu.roll(columns, depth - 2 * W * plane - 2 * W + 1, 1)
    return jnp.where(lane == 0, edge, pltpu.roll(values, 1, 1))


def z_shift_columns(values, step):
    return pltpu.roll(values, values.shape[-1] - 1 if step > 0 else 1, 1)


def z_edge(current, values, plane, step):
    lane = lanes_of(values.shape)
    if step > 0:
        at = 2 * W * plane + 2 * W - 1
        return jnp.where(lane == at, pltpu.roll(values, at, 1), current)
    at = 2 * W * plane
    return jnp.where(lane == at, pltpu.roll(values, at + 1, 1), current)


def properties(get, plane, is_columns, put, tabs, arrays, halo, centre, span):
    fields, lower, half, weight, base = halo if is_columns else arrays
    halo_fields, halo_lower = halo[:2]
    press, water, gas, active, region = (get(c) for c in range(5))
    look = lookups(tabs, region, range(9))
    formation, compress, viscous = look[:3], look[3:6], look[6:]
    sat = (water, 1.0 - water - gas, gas)
    expand = [formation[c] * jnp.exp(compress[c] * (press - 0.5)) for c in range(3)]
    mob = [viscous[c] * expand[c] * sat[c] * sat[c] for c in range(3)]
    stored = get(STORAGE)
    stored = jnp.where(stored > 0, stored, 1.0)
    for c in range(3):
        put(weight, (c, plane), active / (expand[c] * stored))
    put(base, (plane,), get(OWN))
    shifts = []
    one = [press] + mob + [compress[c] * mob[c] for c in range(3)] + [active]
    for f, values in enumerate(one):
        put(fields, (f, 1, plane), values)
        shifts += [(0, (f, step + 1), step, values, f) for step in (-1, 1)]
    for k, offset in enumerate(upper_offsets):
        values = 0.5 * get(t_channel(k))
        put(half, (k, plane), values)
        values = values * active
        if offset[2] == 0:
            put(lower, (k, plane), values)
        else:
            shifts.append((1, (k,), -offset[2], values, SHIFTED + k))
    for array, lead, step, values, slot in shifts:
        if is_columns:
            centre[slot, span, :] = values
            put((fields, lower)[array], (*lead, 0), z_shift_columns(values, step))
        else:
            put((fields, lower)[array], (*lead, plane), z_shift(values, centre[slot, span, :], plane, step))
            put((halo_fields, halo_lower)[array], (*lead, 0), None, lambda now: z_edge(now, values, plane, step))


def x_roll(values, step, is_columns):
    if not is_columns or step == 0:
        return values
    depth = values.shape[-1]
    return pltpu.roll(values, (depth - 2 * W * step) % depth, 1)


def link_cells(plane, is_columns, first, stride, arrays, out, results):
    fields, lower, half, weight, base = arrays
    coupling, scale, start = results
    depth = fields.shape[-1]
    here = (0, 0, 0)

    def read(ref, lead, offset):
        dx = 0 if is_columns else offset[0]
        values = ref[(*lead, plane + dx, pl.ds(first + stride * offset[1], 8), slice(None))]
        return x_roll(values, offset[0], is_columns)

    def at(f, offset):
        return read(fields, (f, offset[2] + 1), offset)

    press = at(PRESS, here)
    w = [read(weight, (c,), here) for c in range(3)]
    mob = [at(MOB + c, here) for c in range(3)]
    own_mob = w[0] * mob[0] + w[1] * mob[1] + w[2] * mob[2]
    own_slope = w[0] * at(SLOPE, here) + w[1] * at(SLOPE + 1, here) + w[2] * at(SLOPE + 2, here)
    flux = [jnp.zeros((8, depth), f32) for _ in range(3)]
    drops = jnp.zeros((8, depth), f32)
    means = jnp.ones((8, depth), f32)
    for n, offset in enumerate(neighbour_offsets):
        if offset > here:
            link = read(half, (upper_offsets.index(offset),), here) * at(ACT, offset)
        else:
            k = upper_offsets.index(tuple(-o for o in offset))
            link = read(lower, (k,), offset)
        drop = link * (press - at(PRESS, offset))
        other = [at(MOB + c, offset) for c in range(3)]
        for c in range(3):
            flux[c] = flux[c] + drop * other[c]
        drops = drops + drop
        mean = link * (own_mob + (w[0] * other[0] + w[1] * other[1] + w[2] * other[2]))
        slope = (
            w[0] * at(SLOPE, offset) + w[1] * at(SLOPE + 1, offset) + w[2] * at(SLOPE + 2, offset)
        )
        means = means + mean
        coupling[n, plane, out, :] = drop * slope - mean
    flux = [flux[c] + mob[c] * drops for c in range(3)]
    rate = relax_weight / (means + own_slope * drops)
    right = read(base, (), here) + (w[0] * flux[0] + w[1] * flux[1] + w[2] * flux[2])
    scale[plane, out, :] = rate
    start[plane, out, :] = -rate * right
    return flux


def row_cells(tiles, tabs, arrays, halo, centre):
    def cells(get, plane, is_columns=False):
        for tile in range(tiles):
            span, to = slice(8 * tile, 8 * tile + 8), slice(8 + 8 * tile, 16 + 8 * tile)

            def put(ref, lead, values, change=None):
                at = (*lead, to, slice(None))
                ref[at] = values if change is None else change(ref[at])

            properties(
                lambda c: get(c, span), plane, is_columns, put, tabs, arrays, halo, centre, span
            )

    return cells


def row_links(tiles, plane, is_columns, arrays, results, store=None):
    for tile in range(tiles):
        out = slice(8 * tile, 8 * tile + 8)
        flow = link_cells(plane, is_columns, 8 + 8 * tile, 1, arrays, out, results)
        if store is not None:
            for c in range(3):
                store[c, plane, out, :] = flow[c]


def own_columns(c, za, zb, planes, span):
    depth = za.shape[-1]
    per, _ = groups_of(planes, depth)
    group, base = c // per, (c % per) * span_of(planes)
    return pltpu.roll(za[group, span, :] + zb[group, span, :], (2 * W * W - base) % depth, 1)


def among_own(planes, shape):
    lane = lanes_of(shape)
    return (lane >= 2 * W * W) & (lane < 2 * W * (W + planes))


def inner_local(local, za, zb, tabs, *refs):
    arrays, results, store, parts = refs[:5], refs[5:8], refs[8], refs[9:11]
    halo, centre = (*parts, *refs[11:14]), refs[14]
    planes, rows, depth = local.shape[1:]
    tiles = rows // 8
    cells = row_cells(tiles, tabs, arrays, halo, centre)

    def columns(c, span):
        values = own_columns(c, za, zb, planes, span)
        return jnp.where(among_own(planes, values.shape), values, 0.0)

    cells(columns, 0, True)

    @pl.loop(0, planes)
    def _(x):
        cells(lambda c, span: local[c, x, span, :], W + x)

    @pl.loop(W + 1, W + planes - 1)
    def _(plane):
        row_links(tiles, plane, False, arrays, results, store)


def inner(x_axis, planes, columns, xa, xb, tabs, *refs):
    parts, refs = refs[:2], refs[11:]
    results, halo_results, store = refs[:3], refs[3:6], refs[6]
    edges, arrays, halo, centre = refs[7:17], refs[17:22], refs[22:27], refs[27]
    rows, depth = xa.shape[1:]
    total = planes + 2 * W
    even_x = parity_of(x_axis)
    tiles = rows // 8
    cells = row_cells(tiles, tabs, arrays, halo, centre)

    cells(lambda c, span: columns[c, span, :], 0, True)
    own = among_own(planes, (8, depth))
    for array, part in zip(halo, parts):
        for lead in itertools.product(*(range(n) for n in part.shape[:-2])):
            for tile in range(tiles):
                at = (*lead, slice(8 + 8 * tile, 16 + 8 * tile), slice(None))
                array[at] = jnp.where(own, part[at], array[at])

    def from_x(n, low):
        def get(c, span):
            i = n(c)
            if i is None:
                return jnp.zeros((8, depth), f32)
            u, v = xa[i, span, :], xb[i, span, :]
            return pick(even_x, v, u) if low else pick(even_x, u, v)

        return get

    @pl.loop(0, NEAR)
    def _(q):
        near = lambda c: c * NEAR + q
        cells(from_x(near, True), 1 + q)
        cells(from_x(near, False), W + planes + q)

    far = lambda c: CHANNELS * NEAR + c if c < FAR else None
    cells(from_x(far, True), 0)
    cells(from_x(far, False), total - 1)

    def hand_on(sources, targets, plane):
        for source, target in zip(sources, targets):
            for lead in itertools.product(*(range(n) for n in source.shape[:-3])):
                last = source[(*lead, plane, slice(6 + rows, 8 + rows), slice(None))]
                head = source[(*lead, plane, slice(8, 10), slice(None))]
                target[(*lead, plane, pl.ds(0, 2, stride=2), slice(None))] = last
                target[(*lead, plane, pl.ds(RING - 3, 2, stride=2), slice(None))] = head

    hand_on(halo, edges[5:], 0)

    @pl.loop(0, total)
    def _(plane):
        hand_on(arrays, edges[:5], plane)

    row_links(tiles, 0, True, halo, halo_results)

    @pl.loop(0, W)
    def _(n):
        row_links(tiles, 1 + n, False, arrays, results, store)
        row_links(tiles, W + planes - 1 + n, False, arrays, results, store)


RING = 2 * (W + 2)


def finish(axis, count_y, local, *refs):
    tabs, accum, ys, more_ys = refs[0], refs[1], refs[2 : 2 + count_y], refs[2 + count_y : 2 + 2 * count_y]
    refs = refs[2 + 2 * count_y :]
    results, halo_results, store = refs[:3], refs[3:6], refs[6]
    residual, update = refs[17:19]
    arrays, halo = refs[19:24], refs[24:29]
    edge_store, raw, centre = refs[29:32]
    edge_results, edge_halo_results = refs[32:35], refs[35:38]
    sols, halo_sols, edge_sols, edge_halo_sols = (refs[38 + 2 * i : 40 + 2 * i] for i in range(4))
    planes, rows, depth = local.shape[1:]
    total = planes + 2 * W
    even_y = parity_of(axis)

    def halo_rows(c, plane, sources, n):
        low = high = jnp.zeros((W, depth), f32)
        if count_y:
            a = sources[0][n]
            b = sources[1][n] if count_y > 1 else None
            low, high = pick(even_y, b, a), pick(even_y, a, b)
        raw[c, plane, 0:W, :] = low
        raw[c, plane, W : 2 * W, :] = high

    @pl.loop(0, CHANNELS)
    def _(c):
        for x in range(planes):
            halo_rows(c, W + x, ys, c * planes + x)
        for q in range(NEAR):
            halo_rows(c, 1 + q, more_ys, c * NEAR + q)
            halo_rows(c, W + planes + q, more_ys, XMAIN + c * NEAR + q)
        halo_rows(c, total, more_ys, 2 * XMAIN + c)

    @pl.loop(0, FAR)
    def _(c):
        halo_rows(c, 0, more_ys, CHANNELS * NEAR + c)
        halo_rows(c, total - 1, more_ys, XMAIN + CHANNELS * NEAR + c)

    for c in range(FAR, CHANNELS):
        for plane in (0, total - 1):
            raw[c, plane] = jnp.zeros((2 * W, depth), f32)

    def cells(plane, is_columns=False):
        def put(ref, lead, values, change=None):
            low = (*lead, pl.ds(1, W, stride=2), slice(None))
            high = (*lead, pl.ds(4, W, stride=2), slice(None))
            if change is not None:
                values = change(jnp.concatenate([ref[low], ref[high]], axis=0))
            ref[low] = values[:W]
            ref[high] = values[W:]

        get = lambda c: raw[c, plane, :, :]
        properties(
            get, 0 if is_columns else plane, is_columns, put, tabs, arrays, halo, centre, slice(0, 8)
        )

    cells(total, True)

    @pl.loop(0, total, unroll=2)
    def _(plane):
        cells(plane)

    def links(plane, is_columns=False):
        out = slice(0, 8)
        own = (halo, out, edge_halo_results) if is_columns else (arrays, out, edge_results)
        res = link_cells(plane, is_columns, 2, 2, *own)
        if not is_columns:
            for c in range(3):
                edge_store[c, plane] = res[c]

    links(0, True)

    @pl.loop(1, total - 1)
    def _(plane):
        links(plane)

    tiles = rows // 8

    row = lax.broadcasted_iota(jnp.int32, (8, depth), 0)

    def merged(mains, edge):
        first, last = pltpu.roll(edge, 1, 0), pltpu.roll(edge, 7, 0)
        mains = [jnp.where(row == 0, first, mains[0])] + mains[1:]
        return mains[:-1] + [jnp.where(row == 7, last, mains[-1])]

    def put_parts(is_columns, slot, step, plane, mains, edge):
        to, edge_to = (
            (halo_sols[slot], edge_halo_sols[slot]) if is_columns else (sols[slot], edge_sols[slot])
        )
        for tile, values in enumerate(mains):
            to[step + 1, plane, 8 + 8 * tile : 16 + 8 * tile, :] = values
        edge_to[step + 1, plane, 2:10, :] = edge
        to[step + 1, plane, 7:8, :] = edge[5:6]
        to[step + 1, plane, 8 + rows : 9 + rows, :] = edge[2:3]
        edge_to[step + 1, plane, 0:1, :] = mains[-1][6:7]
        edge_to[step + 1, plane, RING - 1 : RING, :] = mains[0][1:2]

    def halo_parts(slot, step):
        mains = [
            halo_sols[slot][step + 1, 0, 8 + 8 * tile : 16 + 8 * tile, :] for tile in range(tiles)
        ]
        return mains, edge_halo_sols[slot][step + 1, 0, 2:10, :]

    def put_solution(slot, plane, mains, edge, is_columns=False):
        mains = merged(mains, edge)
        put_parts(is_columns, slot, 0, plane, mains, edge)
        for step in (-1, 1):
            if is_columns:
                shift = lambda values: z_shift_columns(values, step)
                put_parts(True, slot, step, plane, [shift(u) for u in mains], shift(edge))
                continue
            shift = lambda u, v: z_shift(u, v, plane, step)
            halo_mains, halo_edge = halo_parts(slot, 0)
            shifted = [shift(u, v) for u, v in zip(mains, halo_mains)]
            put_parts(False, slot, step, plane, shifted, shift(edge, halo_edge))
            shift = lambda u, v: z_edge(u, v, plane, step)
            halo_mains, halo_edge = halo_parts(slot, step)
            shifted = [shift(u, v) for u, v in zip(halo_mains, mains)]
            put_parts(True, slot, step, 0, shifted, shift(halo_edge, edge))

    def relaxed(slot, plane, tile, is_columns=False):
        if tile is None:
            ref = (edge_halo_sols if is_columns else edge_sols)[slot]
            first, stride, out = 2, 2, slice(0, 8)
            coupling, scale, start = edge_halo_results if is_columns else edge_results
        else:
            ref = (halo_sols if is_columns else sols)[slot]
            first, stride = 8 + 8 * tile, 1
            out = slice(8 * tile, 8 * tile + 8)
            coupling, scale, start = halo_results if is_columns else results

        def get(offset):
            dx = 0 if is_columns else offset[0]
            values = ref[offset[2] + 1, plane + dx, pl.ds(first + stride * offset[1], 8), :]
            return x_roll(values, offset[0], is_columns)

        parts = [jnp.zeros((8, depth), f32) for _ in range(2)]
        for n, offset in enumerate(neighbour_offsets):
            parts[n % 2] = parts[n % 2] + coupling[n, plane, out, :] * get(offset)
        return (
            (1.0 - relax_weight) * get((0, 0, 0))
            + start[plane, out, :]
            - scale[plane, out, :] * (parts[0] + parts[1])
        )

    def first_sweep(plane, is_columns=False):
        start = (halo_results if is_columns else results)[2]
        edge = (edge_halo_results if is_columns else edge_results)[2]
        mains = [start[plane, 8 * tile : 8 * tile + 8, :] for tile in range(tiles)]
        put_solution(0, plane, mains, edge[plane], is_columns)

    first_sweep(0, True)

    @pl.loop(1, total - 1, unroll=2)
    def _(plane):
        first_sweep(plane)

    def sweep_of(slot, plane, is_columns=False):
        mains = [relaxed(slot, plane, tile, is_columns) for tile in range(tiles)]
        put_solution(1 - slot, plane, mains, relaxed(slot, plane, None, is_columns), is_columns)

    for sweep in range(2, SWEEPS):
        slot = sweep % 2
        sweep_of(slot, 0, True)

        @pl.loop(sweep, total - sweep, unroll=2)
        def _(plane):
            sweep_of(slot, plane)

    @pl.loop(0, planes, unroll=2)
    def _(x):
        slot, plane = SWEEPS % 2, W + x
        edge = relaxed(slot, plane, None)
        for tile in range(tiles):
            span = slice(8 * tile, 8 * tile + 8)
            update[x, span, :] = relaxed(slot, plane, tile)
            active = local[3, x, span, :]
            for c in range(3):
                flow = store[c, plane, span, :]
                residual[c, x, span, :] = active * (accum[c, x, span, :] + flow)
        for row_of, edge_row in ((0, 7), (rows - 1, 0)):
            to, source = slice(row_of, row_of + 1), slice(edge_row, edge_row + 1)
            update[x, to, :] = edge[source]
            active = local[3, x, to, :]
            for c in range(3):
                flow = edge_store[c, plane, source, :]
                residual[c, x, to, :] = active * (accum[c, x, to, :] + flow)


def call(kernel, name, mib, **options):
    return pl.pallas_call(
        kernel,
        name=name,
        compiler_params=pltpu.CompilerParams(vmem_limit_bytes=mib << 20),
        **options,
    )


def cell_shapes(total, height, depth):
    return [
        (*lead, count, height, depth)
        for count in (total, 1)
        for lead in ((SHIFTED, 3), (UP,), (UP,), (3,), ())
    ]


def result_shapes(total, height, depth):
    return [
        shape
        for count in (total, 1)
        for shape in ((2 * UP, count, height, depth), (count, height, depth), (count, height, depth))
    ]


def body(
    cell_state,
    old_mass,
    pore_volume,
    transmissibility,
    active_mask,
    pvt_region,
    formation_factor,
    compressibility,
    inverse_viscosity,
):
    ax, ay, az = "gx", "gy", "gz"
    planes, rows, depth = pore_volume.shape
    total = planes + 2 * W
    per, groups = groups_of(planes, depth)
    assert per >= 1 and 2 * W * total <= depth and rows % 8 == 0 and RING <= 16
    tables = (formation_factor, compressibility, inverse_viscosity)
    like = lambda *shape: jax.ShapeDtypeStruct(shape, f32)
    fill = lambda shape, got: [jnp.zeros(shape.shape, f32) if one is None else one for one in got]

    arguments = (
        *(cell_state, old_mass, pore_volume, transmissibility, active_mask, pvt_region),
        *tables,
    )
    z_shape = like(groups, rows, depth)
    cells = like(3, planes, rows, depth)
    local, accum, tabs, *z_send = call(
        functools.partial(pack_z, az),
        "pack_z",
        8,
        out_shape=(like(CHANNELS, planes, rows, depth), cells, like(9, 8, depth), z_shape, z_shape),
        in_specs=[HBM] * 9,
        out_specs=(VMEM,) * 5,
        scratch_shapes=[
            pltpu.VMEM((2, planes, rows, depth), jnp.int32),
            pltpu.VMEM(cells.shape, f32),
            pltpu.VMEM((planes, rows, depth), f32),
            pltpu.VMEM((3, *formation_factor.shape), f32),
            pltpu.SemaphoreType.DMA((10,)),
        ],
    )(*(pltpu.with_memory_space_constraint(array, pltpu.MemorySpace.HBM) for array in arguments))
    za, zb = fill(z_shape, swaps(az, *z_send))

    x_shape = like(XMAIN, rows, depth)
    x_send = call(functools.partial(pack_x, ax), "pack_x", 8, out_shape=(x_shape, x_shape))(local)
    xa, xb = fill(x_shape, swaps(ax, *x_send))

    count_y = min(lax.axis_size(ay) - 1, 2)
    ys, more_ys = [], []
    c_shape = like(groups_of(W, depth)[1], rows, depth)
    sent = call(
        functools.partial(join_x, ax, ay),
        "join_x",
        8,
        out_shape=(c_shape, c_shape) + (like(CHANNELS * planes, W, depth),) * count_y,
    )(za, zb, local)
    c_send, y_send = sent[:2], sent[2:]
    ca, cb = fill(c_shape, swaps(ax, *c_send))
    if count_y:
        ys = swaps(ay, y_send[0], y_send[-1])[:count_y]
    vmem = lambda shapes: [pltpu.VMEM(shape, f32) for shape in shapes]
    flow = (3, total, rows, depth)
    tall = cell_shapes(total, rows + 16, depth)
    wide = result_shapes(total, rows, depth)
    centre = (SHIFTED + UP, rows, depth)
    shapes = tall[:5] + wide[:3] + [flow] + tall[5:7]
    found = call(
        inner_local,
        "inner_local",
        16,
        out_shape=[like(*shape) for shape in shapes],
        in_specs=[VMEM] * 4,
        out_specs=[VMEM] * len(shapes),
        scratch_shapes=vmem(tall[7:] + [centre]),
    )(local, za, zb, tabs)
    arrays, found, parts = found[:5], found[5:9], found[9:]

    columns, *y_send = call(
        functools.partial(join_y, ay, ax, planes),
        "join_y",
        8,
        out_shape=(like(CHANNELS, rows, depth),)
        + (like(2 * XMAIN + CHANNELS, W, depth),) * count_y,
        in_specs=[VMEM] * 6 + [ANY] * (count_y + 1),
    )(za, zb, xa, xb, ca, cb, *ys, parts[1])
    if count_y:
        more_ys = swaps(ay, y_send[0], y_send[-1])[:count_y]

    edges = cell_shapes(total, 16, depth)
    shapes = wide + [flow] + edges + tall[:5]
    halves = call(
        functools.partial(inner, ax, planes),
        "inner",
        16,
        out_shape=[like(*shape) for shape in shapes],
        in_specs=[VMEM] * 15,
        out_specs=[VMEM] * len(shapes),
        scratch_shapes=vmem(tall[5:] + [centre]),
        input_output_aliases={6: 0, 7: 1, 8: 2, 9: 6, **{10 + i: 17 + i for i in range(5)}},
    )(columns, xa, xb, tabs, *parts, *found, *arrays)[:17]

    solutions = [
        (3, count, height, depth) for height in (rows + 16, 16) for count in (total, 1) for _ in range(2)
    ]
    before = 3 + 2 * count_y + 7
    residual, update, *_ = call(
        functools.partial(finish, ay, count_y),
        "finish",
        24,
        out_shape=[cells, like(planes, rows, depth)] + [like(*shape) for shape in edges],
        in_specs=[VMEM] * (before + len(edges)),
        out_specs=[VMEM] * (2 + len(edges)),
        scratch_shapes=vmem(
            [
                (3, total, 8, depth),
                (CHANNELS, total + 1, 2 * W, depth),
                (SHIFTED + UP, 2 * W, depth),
                *result_shapes(total, 8, depth),
                *solutions,
            ]
        ),
        input_output_aliases={before + i: 2 + i for i in range(len(edges))},
    )(local, tabs, accum, *ys, *more_ys, *halves)
    return residual, update


def solution(mesh):
    return jax.shard_map(
        body,
        mesh=mesh,
        in_specs=(
            P(None, "gx", "gy", "gz"),
            P(None, "gx", "gy", "gz"),
            P("gx", "gy", "gz"),
            P(None, "gx", "gy", "gz"),
            P("gx", "gy", "gz"),
            P("gx", "gy", "gz"),
            P(),
            P(),
            P(),
        ),
        out_specs=(P(None, "gx", "gy", "gz"), P("gx", "gy", "gz")),
        check_vma=False,
    )
```

```python
import functools
import itertools

import jax
import jax.numpy as jnp
from jax import lax
from jax.experimental import pallas as pl
from jax.experimental.pallas import tpu as pltpu
from jax.sharding import PartitionSpec as P

SWEEPS = 4
W = SWEEPS
relax_weight = 0.7

neighbour_offsets = [
    (along_x, along_y, along_z)
    for along_x in (-1, 0, 1)
    for along_y in (-1, 0, 1)
    for along_z in (-1, 0, 1)
    if (along_x, along_y, along_z) != (0, 0, 0)
]
upper_offsets = [offset for offset in neighbour_offsets if offset > (0, 0, 0)]
UP = len(upper_offsets)
FLAT = sum(1 for offset in upper_offsets if offset[0] == 0)
STEP = UP - FLAT

FAR = 5 + STEP
CHANNELS = FAR + FLAT + 2
STORAGE, OWN = FAR + FLAT, FAR + FLAT + 1
NEAR = W - 1
XMAIN = CHANNELS * NEAR + FAR
VMEM = pl.BlockSpec(memory_space=pltpu.VMEM)
ANY = pl.BlockSpec(memory_space=pl.ANY)
HBM = pl.BlockSpec(memory_space=pltpu.MemorySpace.HBM)
f32 = jnp.float32


def t_channel(k):
    return FAR + k if k < FLAT else 5 + k - FLAT


def pick(parity, even, odd):
    shape = (even if odd is None else odd).shape
    if even is None:
        even = jnp.zeros(shape, f32)
    if odd is None:
        odd = jnp.zeros(shape, f32)
    return jnp.where(jnp.full(shape, parity, jnp.int32) == 0, even, odd)


def parity_of(axis):
    return lax.rem(lax.axis_index(axis), 2)


def swaps(axis, first, second):
    count = lax.axis_size(axis)
    got = []
    for start, message in ((0, first), (1, second)):
        pairs = [(i, i + 1) for i in range(start, count - 1, 2)]
        if not pairs:
            got.append(None)
            continue
        got.append(lax.ppermute(message, axis, pairs + [(b, a) for a, b in pairs]))
    return got


def lanes_of(shape):
    return lax.broadcasted_iota(jnp.int32, shape, len(shape) - 1)


def span_of(planes):
    return 2 * W * planes


def groups_of(planes, depth):
    per = depth // span_of(planes)
    return per, -(-CHANNELS // per)


def lookups(tabs, region, numbers):
    index = region.astype(jnp.int32)
    return [
        jnp.take_along_axis(tabs[n], index, axis=1, mode="promise_in_bounds") for n in numbers
    ]


def pack_z(axis, *refs):
    state, mass, pore, trans, active, region, *tables = refs[:9]
    local, accum, tabs, first, second = refs[9:14]
    flags, masses, pores, small, sems = refs[14:]
    planes, rows, depth = pore.shape
    copies = [
        pltpu.make_async_copy(active, flags.at[0], sems.at[0]),
        pltpu.make_async_copy(region, flags.at[1], sems.at[1]),
        pltpu.make_async_copy(state, local.at[0:3], sems.at[2]),
        pltpu.make_async_copy(mass, masses, sems.at[3]),
        pltpu.make_async_copy(pore, pores, sems.at[4]),
    ]
    copies += [
        pltpu.make_async_copy(table, small.at[n], sems.at[5 + n]) for n, table in enumerate(tables)
    ]
    late = [
        pltpu.make_async_copy(trans.at[FLAT:UP], local.at[5:FAR], sems.at[8]),
        pltpu.make_async_copy(trans.at[0:FLAT], local.at[FAR : FAR + FLAT], sems.at[9]),
    ]
    for copy in copies + late:
        copy.start()
    for copy in copies:
        copy.wait()
    regions = tables[0].shape[1]
    for n in range(3):
        for c in range(3):
            tabs[3 * n + c, :, 0:regions] = jnp.broadcast_to(small[n, c : c + 1, :], (8, regions))
    for x in range(planes):
        for tile in range(rows // 8):
            span = slice(8 * tile, 8 * tile + 8)
            on = flags[0, x, span, :].astype(f32)
            level = flags[1, x, span, :]
            local[3, x, span, :] = on
            local[4, x, span, :] = level.astype(f32)
            press, water, gas = (local[c, x, span, :] for c in range(3))
            look = lookups(tabs, level, range(6))
            sat = (water, 1.0 - water - gas, gas)
            expand = [look[c] * jnp.exp(look[3 + c] * (press - 0.5)) for c in range(3)]
            volume = pores[x, span, :]
            stored = volume * (look[3] * sat[0] + look[4] * sat[1] + look[5] * sat[2])
            stored = jnp.where(on > 0, stored, 1.0)
            own = jnp.zeros((8, depth), f32)
            for c in range(3):
                value = volume * expand[c] * sat[c] - masses[c, x, span, :]
                accum[c, x, span, :] = value
                own = own + value / (expand[c] * stored)
            local[STORAGE, x, span, :] = stored
            local[OWN, x, span, :] = on * own
    for copy in late:
        copy.wait()

    per, groups = groups_of(planes, depth)
    even = parity_of(axis)
    lane = lanes_of((8, depth))

    @pl.loop(0, rows // 8)
    def _(tile):
        span = pl.ds(pl.multiple_of(8 * tile, 8), 8)
        for group in range(groups):
            high = jnp.zeros((8, depth), f32)
            low = jnp.zeros((8, depth), f32)
            for c in range(group * per, min(CHANNELS, group * per + per)):
                for x in range(planes):
                    base = (c % per) * span_of(planes) + 2 * W * x
                    values = local[c, x, span, :]
                    here = (lane >= base + W) & (lane < base + 2 * W)
                    high = jnp.where(here, pltpu.roll(values, (base + 2 * W) % depth, 1), high)
                    here = (lane >= base) & (lane < base + W)
                    low = jnp.where(here, pltpu.roll(values, base % depth, 1), low)
            first[group, span, :] = pick(even, high, low)
            second[group, span, :] = pick(even, low, high)


def pack_x(axis, local, *outs):
    planes = local.shape[1]
    even = parity_of(axis)
    for out, up in zip(outs, (even == 0, even != 0)):
        near = jnp.where(up, planes - NEAR, 0)
        far = jnp.where(up, planes - W, W - 1)
        for c in range(CHANNELS):
            for q in range(NEAR):
                out[c * NEAR + q] = local[c, near + q]
            if c < FAR:
                out[CHANNELS * NEAR + c] = local[c, far]


def put_rows(outs, n, values, even):
    head, tail = values[:W], values[values.shape[0] - W :]
    for out, up, down in zip(outs, (tail, head), (head, tail)):
        out[n] = pick(even, up, down)


def join_x(axis, y_axis, za, zb, local, *outs):
    planes = local.shape[1]
    even_y = parity_of(y_axis)
    for c in range(CHANNELS):
        for x in range(planes):
            put_rows(outs[2:], c * planes + x, local[c, x], even_y)
    for group in range(za.shape[0]):
        put_rows(outs[2:], CHANNELS * planes + group, za[group] + zb[group], even_y)
    rows, depth = za.shape[1:]
    even = parity_of(axis)
    per, _ = groups_of(planes, depth)
    per_x, groups_x = groups_of(W, depth)
    lane = lanes_of((rows, depth))
    for group in range(groups_x):
        sides = [jnp.zeros((rows, depth), f32) for _ in range(2)]
        for c in range(group * per_x, min(CHANNELS, group * per_x + per_x)):
            values = za[c // per] + zb[c // per]
            to = (c % per_x) * span_of(W)
            here = (lane >= to) & (lane < to + span_of(W))
            for n, plane in enumerate((planes - W, 0)):
                source = (c % per) * span_of(planes) + 2 * W * plane
                sides[n] = jnp.where(here, pltpu.roll(values, (to - source) % depth, 1), sides[n])
        outs[0][group] = pick(even, *sides)
        outs[1][group] = pick(even, *sides[::-1])


def join_y(axis, x_axis, planes, za, zb, xa, xb, ca, cb, *refs):
    count = len(refs) // 2
    columns, *outs = refs[count:]
    rows, depth = xa.shape[1:]
    even = parity_of(axis)
    even_x = parity_of(x_axis)
    per_x, _ = groups_of(W, depth)
    lane = lanes_of((rows, depth))
    for c in range(CHANNELS):
        own = own_columns(c, za, zb, planes, slice(0, rows))
        group, base = c // per_x, (c % per_x) * span_of(W)
        a, b = ca[group], cb[group]
        below = pltpu.roll(pick(even_x, b, a), (depth - base) % depth, 1)
        above = pltpu.roll(pick(even_x, a, b), (2 * W * (planes + W) - base) % depth, 1)
        values = jnp.where(lane < 2 * W * W, below, jnp.where(lane < 2 * W * (W + planes), own, above))
        columns[c] = values
        put_rows(outs, 2 * XMAIN + c, values, even)

    @pl.loop(0, XMAIN // 2)
    def _(i):
        for j in range(2):
            n = 2 * i + j
            a, b = xa[n], xb[n]
            put_rows(outs, n, pick(even_x, b, a), even)
            put_rows(outs, XMAIN + n, pick(even_x, a, b), even)


PRESS, MOB, SLOPE, ACT = 0, 1, 4, 7
SHIFTED = 8


def z_shift(values, columns, plane, step):
    depth = values.shape[-1]
    lane = lanes_of(values.shape)
    if step > 0:
        edge = pltpu.roll(columns, depth - 1 - 2 * W * plane, 1)
        return jnp.where(lane == depth - 1, edge, pltpu.roll(values, depth - 1, 1))
    edge = pltpu.roll(columns, depth - 2 * W * plane - 2 * W + 1, 1)
    return jnp.where(lane == 0, edge, pltpu.roll(values, 1, 1))


def z_shift_columns(values, step):
    return pltpu.roll(values, values.shape[-1] - 1 if step > 0 else 1, 1)


def z_edge(current, values, plane, step):
    lane = lanes_of(values.shape)
    if step > 0:
        at = 2 * W * plane + 2 * W - 1
        return jnp.where(lane == at, pltpu.roll(values, at, 1), current)
    at = 2 * W * plane
    return jnp.where(lane == at, pltpu.roll(values, at + 1, 1), current)


def properties(get, plane, is_columns, put, tabs, arrays, halo, centre, span, done=None):
    fields, lower, half, weight, base = halo if is_columns else arrays
    halo_fields, halo_lower = halo[:2]
    press, water, gas, active, region = (get(c) for c in range(5))
    look = lookups(tabs, region, range(9))
    formation, compress, viscous = look[:3], look[3:6], look[6:]
    sat = (water, 1.0 - water - gas, gas)
    expand = [formation[c] * jnp.exp(compress[c] * (press - 0.5)) for c in range(3)]
    mob = [viscous[c] * expand[c] * sat[c] * sat[c] for c in range(3)]
    stored = get(STORAGE)
    stored = jnp.where(stored > 0, stored, 1.0)
    for c in range(3):
        put(weight, (c, plane), active / (expand[c] * stored))
    put(base, (plane,), get(OWN))
    shifts = []
    one = [press] + mob + [compress[c] * mob[c] for c in range(3)] + [active]
    for f, values in enumerate(one):
        put(fields, (f, 1, plane), values)
        shifts += [(0, (f, step + 1), step, values, f) for step in (-1, 1)]
    for k, offset in enumerate(upper_offsets):
        values = 0.5 * get(t_channel(k))
        put(half, (k, plane), values)
        values = values * active
        if offset[2] == 0:
            put(lower, (k, plane), values)
        else:
            shifts.append((1, (k,), -offset[2], values, SHIFTED + k))
    for array, lead, step, values, slot in shifts:
        if is_columns:
            centre[slot, span, :] = values
            shifted = z_shift_columns(values, step)
            if done is None:
                put((fields, lower)[array], (*lead, 0), shifted)
            else:
                keep = lambda now: jnp.where(done, now, shifted)
                put((fields, lower)[array], (*lead, 0), None, keep)
        else:
            put((fields, lower)[array], (*lead, plane), z_shift(values, centre[slot, span, :], plane, step))
            put((halo_fields, halo_lower)[array], (*lead, 0), None, lambda now: z_edge(now, values, plane, step))


def x_roll(values, step, is_columns):
    if not is_columns or step == 0:
        return values
    depth = values.shape[-1]
    return pltpu.roll(values, (depth - 2 * W * step) % depth, 1)


def link_cells(plane, is_columns, first, stride, arrays, out, results):
    fields, lower, half, weight, base = arrays
    coupling, scale, start = results
    depth = fields.shape[-1]
    here = (0, 0, 0)

    def read(ref, lead, offset):
        dx = 0 if is_columns else offset[0]
        values = ref[(*lead, plane + dx, pl.ds(first + stride * offset[1], 8), slice(None))]
        return x_roll(values, offset[0], is_columns)

    def at(f, offset):
        return read(fields, (f, offset[2] + 1), offset)

    press = at(PRESS, here)
    w = [read(weight, (c,), here) for c in range(3)]
    mob = [at(MOB + c, here) for c in range(3)]
    own_mob = w[0] * mob[0] + w[1] * mob[1] + w[2] * mob[2]
    own_slope = w[0] * at(SLOPE, here) + w[1] * at(SLOPE + 1, here) + w[2] * at(SLOPE + 2, here)
    flux = [jnp.zeros((8, depth), f32) for _ in range(3)]
    drops = jnp.zeros((8, depth), f32)
    means = jnp.ones((8, depth), f32)
    for n, offset in enumerate(neighbour_offsets):
        if offset > here:
            link = read(half, (upper_offsets.index(offset),), here) * at(ACT, offset)
        else:
            k = upper_offsets.index(tuple(-o for o in offset))
            link = read(lower, (k,), offset)
        drop = link * (press - at(PRESS, offset))
        other = [at(MOB + c, offset) for c in range(3)]
        for c in range(3):
            flux[c] = flux[c] + drop * other[c]
        drops = drops + drop
        mean = link * (own_mob + (w[0] * other[0] + w[1] * other[1] + w[2] * other[2]))
        slope = (
            w[0] * at(SLOPE, offset) + w[1] * at(SLOPE + 1, offset) + w[2] * at(SLOPE + 2, offset)
        )
        means = means + mean
        coupling[n, plane, out, :] = drop * slope - mean
    flux = [flux[c] + mob[c] * drops for c in range(3)]
    rate = relax_weight / (means + own_slope * drops)
    right = read(base, (), here) + (w[0] * flux[0] + w[1] * flux[1] + w[2] * flux[2])
    scale[plane, out, :] = rate
    start[plane, out, :] = -rate * right
    return flux


def row_cells(tiles, tabs, arrays, halo, centre):
    def cells(get, plane, is_columns=False):
        for tile in range(tiles):
            span, to = slice(8 * tile, 8 * tile + 8), slice(8 + 8 * tile, 16 + 8 * tile)

            def put(ref, lead, values, change=None):
                at = (*lead, to, slice(None))
                ref[at] = values if change is None else change(ref[at])

            properties(
                lambda c: get(c, span), plane, is_columns, put, tabs, arrays, halo, centre, span
            )

    return cells


def row_links(tiles, plane, is_columns, arrays, results, store=None):
    for tile in range(tiles):
        out = slice(8 * tile, 8 * tile + 8)
        flow = link_cells(plane, is_columns, 8 + 8 * tile, 1, arrays, out, results)
        if store is not None:
            for c in range(3):
                store[c, plane, out, :] = flow[c]


def own_columns(c, za, zb, planes, span):
    depth = za.shape[-1]
    per, _ = groups_of(planes, depth)
    group, base = c // per, (c % per) * span_of(planes)
    return pltpu.roll(za[group, span, :] + zb[group, span, :], (2 * W * W - base) % depth, 1)


def among_own(planes, shape):
    lane = lanes_of(shape)
    return (lane >= 2 * W * W) & (lane < 2 * W * (W + planes))


def inner_local(local, za, zb, tabs, *refs):
    arrays, results, store, parts = refs[:5], refs[5:8], refs[8], refs[9:11]
    halo, centre = (*parts, *refs[11:14]), refs[14]
    planes, rows, depth = local.shape[1:]
    tiles = rows // 8
    cells = row_cells(tiles, tabs, arrays, halo, centre)

    def columns(c, span):
        values = own_columns(c, za, zb, planes, span)
        return jnp.where(among_own(planes, values.shape), values, 0.0)

    cells(columns, 0, True)

    @pl.loop(0, planes)
    def _(x):
        cells(lambda c, span: local[c, x, span, :], W + x)

    @pl.loop(W + 1, W + planes - 1)
    def _(plane):
        row_links(tiles, plane, False, arrays, results, store)


def inner(x_axis, planes, columns, xa, xb, tabs, *refs):
    parts, refs = refs[:2], refs[11:]
    results, halo_results, store = refs[:3], refs[3:6], refs[6]
    edges, arrays, halo, centre = refs[7:17], refs[17:22], refs[22:27], refs[27]
    rows, depth = xa.shape[1:]
    total = planes + 2 * W
    even_x = parity_of(x_axis)
    tiles = rows // 8
    cells = row_cells(tiles, tabs, arrays, halo, centre)

    cells(lambda c, span: columns[c, span, :], 0, True)
    own = among_own(planes, (8, depth))
    for array, part in zip(halo, parts):
        for lead in itertools.product(*(range(n) for n in part.shape[:-2])):
            for tile in range(tiles):
                at = (*lead, slice(8 + 8 * tile, 16 + 8 * tile), slice(None))
                array[at] = jnp.where(own, part[at], array[at])

    def from_x(n, low):
        def get(c, span):
            i = n(c)
            if i is None:
                return jnp.zeros((8, depth), f32)
            u, v = xa[i, span, :], xb[i, span, :]
            return pick(even_x, v, u) if low else pick(even_x, u, v)

        return get

    @pl.loop(0, NEAR)
    def _(q):
        near = lambda c: c * NEAR + q
        cells(from_x(near, True), 1 + q)
        cells(from_x(near, False), W + planes + q)

    far = lambda c: CHANNELS * NEAR + c if c < FAR else None
    cells(from_x(far, True), 0)
    cells(from_x(far, False), total - 1)

    def hand_on(sources, targets, plane):
        for source, target in zip(sources, targets):
            for lead in itertools.product(*(range(n) for n in source.shape[:-3])):
                last = source[(*lead, plane, slice(6 + rows, 8 + rows), slice(None))]
                head = source[(*lead, plane, slice(8, 10), slice(None))]
                target[(*lead, plane, pl.ds(0, 2, stride=2), slice(None))] = last
                target[(*lead, plane, pl.ds(RING - 3, 2, stride=2), slice(None))] = head

    hand_on(halo, edges[5:], 0)

    @pl.loop(0, total)
    def _(plane):
        hand_on(arrays, edges[:5], plane)

    row_links(tiles, 0, True, halo, halo_results)

    @pl.loop(0, W)
    def _(n):
        row_links(tiles, 1 + n, False, arrays, results, store)
        row_links(tiles, W + planes - 1 + n, False, arrays, results, store)


RING = 2 * (W + 2)


def put_ring(ref, lead, values, change=None):
    low = (*lead, pl.ds(1, W, stride=2), slice(None))
    high = (*lead, pl.ds(4, W, stride=2), slice(None))
    if change is not None:
        values = change(jnp.concatenate([ref[low], ref[high]], axis=0))
    ref[low] = values[:W]
    ref[high] = values[W:]


def halo_rows(even_y, sources, n, target, at):
    shape = target.shape[-1:]
    low = high = jnp.zeros((W, *shape), f32)
    if sources:
        a = sources[0][n]
        b = sources[1][n] if len(sources) > 1 else None
        low, high = pick(even_y, b, a), pick(even_y, a, b)
    target[(*at, slice(0, W), slice(None))] = low
    target[(*at, slice(W, 2 * W), slice(None))] = high


def ring_links(plane, is_columns, arrays, results, store):
    flow = link_cells(plane, is_columns, 2, 2, arrays, slice(0, 8), results)
    if not is_columns:
        for c in range(3):
            store[c, plane] = flow[c]


def finish_local(axis, count_y, planes, tabs, *refs):
    ys, refs = refs[:count_y], refs[count_y + 10 :]
    arrays, halo, results, store = refs[:5], refs[5:10], refs[10:13], refs[13]
    raw, packed, centre = refs[14:]
    depth = raw.shape[-1]
    even_y = parity_of(axis)
    per, groups = groups_of(planes, depth)
    for group in range(groups):
        halo_rows(even_y, ys, CHANNELS * planes + group, packed, (group,))

    @pl.loop(0, CHANNELS)
    def _(c):
        for x in range(planes):
            halo_rows(even_y, ys, c * planes + x, raw, (c, x))

    def cells(get, plane, is_columns=False):
        span = slice(0, 2 * W)
        properties(get, plane, is_columns, put_ring, tabs, arrays, halo, centre, span)

    own = among_own(planes, (2 * W, depth))

    def columns(c):
        base = (c % per) * span_of(planes)
        return jnp.where(own, pltpu.roll(packed[c // per], (2 * W * W - base) % depth, 1), 0.0)

    cells(columns, 0, True)

    @pl.loop(0, planes, unroll=2)
    def _(x):
        cells(lambda c: raw[c, x], W + x)

    @pl.loop(W + 1, W + planes - 1)
    def _(plane):
        ring_links(plane, False, arrays, results, store)


def finish(axis, count_y, local, *refs):
    tabs, accum, more_ys, refs = refs[0], refs[1], refs[2 : 2 + count_y], refs[2 + count_y :]
    results, halo_results, store = refs[:3], refs[3:6], refs[6]
    residual, update = refs[21:23]
    arrays, halo = refs[23:28], refs[28:33]
    edge_results, edge_store = refs[33:36], refs[36]
    raw, centre, edge_halo_results = refs[37], refs[38], refs[39:42]
    sols, halo_sols, edge_sols, edge_halo_sols = (refs[42 + 2 * i : 44 + 2 * i] for i in range(4))
    planes, rows, depth = local.shape[1:]
    total = planes + 2 * W
    even_y = parity_of(axis)

    @pl.loop(0, CHANNELS)
    def _(c):
        for q in range(NEAR):
            halo_rows(even_y, more_ys, c * NEAR + q, raw, (c, 1 + q))
            halo_rows(even_y, more_ys, XMAIN + c * NEAR + q, raw, (c, W + q))
        halo_rows(even_y, more_ys, 2 * XMAIN + c, raw, (c, 2 * W))

    @pl.loop(0, FAR)
    def _(c):
        halo_rows(even_y, more_ys, CHANNELS * NEAR + c, raw, (c, 0))
        halo_rows(even_y, more_ys, XMAIN + CHANNELS * NEAR + c, raw, (c, 2 * W - 1))

    for c in range(FAR, CHANNELS):
        for slot in (0, 2 * W - 1):
            raw[c, slot] = jnp.zeros((2 * W, depth), f32)

    def cells(slot, plane, is_columns=False):
        done = among_own(planes, (2 * W, depth)) if is_columns else None
        get, span = lambda c: raw[c, slot], slice(0, 2 * W)
        properties(get, plane, is_columns, put_ring, tabs, arrays, halo, centre, span, done)

    cells(2 * W, 0, True)

    @pl.loop(0, W)
    def _(n):
        cells(n, n)
        cells(W + n, W + planes + n)

    ring_links(0, True, halo, edge_halo_results, None)

    @pl.loop(0, W)
    def _(n):
        ring_links(1 + n, False, arrays, edge_results, edge_store)
        ring_links(W + planes - 1 + n, False, arrays, edge_results, edge_store)

    tiles = rows // 8

    row = lax.broadcasted_iota(jnp.int32, (8, depth), 0)

    def merged(mains, edge):
        first, last = pltpu.roll(edge, 1, 0), pltpu.roll(edge, 7, 0)
        mains = [jnp.where(row == 0, first, mains[0])] + mains[1:]
        return mains[:-1] + [jnp.where(row == 7, last, mains[-1])]

    def put_parts(is_columns, slot, step, plane, mains, edge):
        to, edge_to = (
            (halo_sols[slot], edge_halo_sols[slot]) if is_columns else (sols[slot], edge_sols[slot])
        )
        for tile, values in enumerate(mains):
            to[step + 1, plane, 8 + 8 * tile : 16 + 8 * tile, :] = values
        edge_to[step + 1, plane, 2:10, :] = edge
        to[step + 1, plane, 7:8, :] = edge[5:6]
        to[step + 1, plane, 8 + rows : 9 + rows, :] = edge[2:3]
        edge_to[step + 1, plane, 0:1, :] = mains[-1][6:7]
        edge_to[step + 1, plane, RING - 1 : RING, :] = mains[0][1:2]

    def halo_parts(slot, step):
        mains = [
            halo_sols[slot][step + 1, 0, 8 + 8 * tile : 16 + 8 * tile, :] for tile in range(tiles)
        ]
        return mains, edge_halo_sols[slot][step + 1, 0, 2:10, :]

    def put_solution(slot, plane, mains, edge, is_columns=False):
        mains = merged(mains, edge)
        put_parts(is_columns, slot, 0, plane, mains, edge)
        for step in (-1, 1):
            if is_columns:
                shift = lambda values: z_shift_columns(values, step)
                put_parts(True, slot, step, plane, [shift(u) for u in mains], shift(edge))
                continue
            shift = lambda u, v: z_shift(u, v, plane, step)
            halo_mains, halo_edge = halo_parts(slot, 0)
            shifted = [shift(u, v) for u, v in zip(mains, halo_mains)]
            put_parts(False, slot, step, plane, shifted, shift(edge, halo_edge))
            shift = lambda u, v: z_edge(u, v, plane, step)
            halo_mains, halo_edge = halo_parts(slot, step)
            shifted = [shift(u, v) for u, v in zip(halo_mains, mains)]
            put_parts(True, slot, step, 0, shifted, shift(halo_edge, edge))

    def relaxed(slot, plane, tile, is_columns=False):
        if tile is None:
            ref = (edge_halo_sols if is_columns else edge_sols)[slot]
            first, stride, out = 2, 2, slice(0, 8)
            coupling, scale, start = edge_halo_results if is_columns else edge_results
        else:
            ref = (halo_sols if is_columns else sols)[slot]
            first, stride = 8 + 8 * tile, 1
            out = slice(8 * tile, 8 * tile + 8)
            coupling, scale, start = halo_results if is_columns else results

        def get(offset):
            dx = 0 if is_columns else offset[0]
            values = ref[offset[2] + 1, plane + dx, pl.ds(first + stride * offset[1], 8), :]
            return x_roll(values, offset[0], is_columns)

        parts = [jnp.zeros((8, depth), f32) for _ in range(2)]
        for n, offset in enumerate(neighbour_offsets):
            parts[n % 2] = parts[n % 2] + coupling[n, plane, out, :] * get(offset)
        return (
            (1.0 - relax_weight) * get((0, 0, 0))
            + start[plane, out, :]
            - scale[plane, out, :] * (parts[0] + parts[1])
        )

    def first_sweep(plane, is_columns=False):
        start = (halo_results if is_columns else results)[2]
        edge = (edge_halo_results if is_columns else edge_results)[2]
        mains = [start[plane, 8 * tile : 8 * tile + 8, :] for tile in range(tiles)]
        put_solution(0, plane, mains, edge[plane], is_columns)

    first_sweep(0, True)

    @pl.loop(1, total - 1, unroll=2)
    def _(plane):
        first_sweep(plane)

    def sweep_of(slot, plane, is_columns=False):
        mains = [relaxed(slot, plane, tile, is_columns) for tile in range(tiles)]
        put_solution(1 - slot, plane, mains, relaxed(slot, plane, None, is_columns), is_columns)

    for sweep in range(2, SWEEPS):
        slot = sweep % 2
        sweep_of(slot, 0, True)

        @pl.loop(sweep, total - sweep, unroll=2)
        def _(plane):
            sweep_of(slot, plane)

    @pl.loop(0, planes, unroll=2)
    def _(x):
        slot, plane = SWEEPS % 2, W + x
        edge = relaxed(slot, plane, None)
        for tile in range(tiles):
            span = slice(8 * tile, 8 * tile + 8)
            update[x, span, :] = relaxed(slot, plane, tile)
            active = local[3, x, span, :]
            for c in range(3):
                flow = store[c, plane, span, :]
                residual[c, x, span, :] = active * (accum[c, x, span, :] + flow)
        for row_of, edge_row in ((0, 7), (rows - 1, 0)):
            to, source = slice(row_of, row_of + 1), slice(edge_row, edge_row + 1)
            update[x, to, :] = edge[source]
            active = local[3, x, to, :]
            for c in range(3):
                flow = edge_store[c, plane, source, :]
                residual[c, x, to, :] = active * (accum[c, x, to, :] + flow)


def call(kernel, name, mib, **options):
    return pl.pallas_call(
        kernel,
        name=name,
        compiler_params=pltpu.CompilerParams(vmem_limit_bytes=mib << 20),
        **options,
    )


def cell_shapes(total, height, depth):
    return [
        (*lead, count, height, depth)
        for count in (total, 1)
        for lead in ((SHIFTED, 3), (UP,), (UP,), (3,), ())
    ]


def result_shapes(total, height, depth):
    return [
        shape
        for count in (total, 1)
        for shape in ((2 * UP, count, height, depth), (count, height, depth), (count, height, depth))
    ]


def body(
    cell_state,
    old_mass,
    pore_volume,
    transmissibility,
    active_mask,
    pvt_region,
    formation_factor,
    compressibility,
    inverse_viscosity,
):
    ax, ay, az = "gx", "gy", "gz"
    planes, rows, depth = pore_volume.shape
    total = planes + 2 * W
    per, groups = groups_of(planes, depth)
    assert per >= 1 and 2 * W * total <= depth and rows % 8 == 0 and RING <= 16
    tables = (formation_factor, compressibility, inverse_viscosity)
    like = lambda *shape: jax.ShapeDtypeStruct(shape, f32)
    fill = lambda shape, got: [jnp.zeros(shape.shape, f32) if one is None else one for one in got]

    arguments = (
        *(cell_state, old_mass, pore_volume, transmissibility, active_mask, pvt_region),
        *tables,
    )
    z_shape = like(groups, rows, depth)
    cells = like(3, planes, rows, depth)
    local, accum, tabs, *z_send = call(
        functools.partial(pack_z, az),
        "pack_z",
        8,
        out_shape=(like(CHANNELS, planes, rows, depth), cells, like(9, 8, depth), z_shape, z_shape),
        in_specs=[HBM] * 9,
        out_specs=(VMEM,) * 5,
        scratch_shapes=[
            pltpu.VMEM((2, planes, rows, depth), jnp.int32),
            pltpu.VMEM(cells.shape, f32),
            pltpu.VMEM((planes, rows, depth), f32),
            pltpu.VMEM((3, *formation_factor.shape), f32),
            pltpu.SemaphoreType.DMA((10,)),
        ],
    )(*(pltpu.with_memory_space_constraint(array, pltpu.MemorySpace.HBM) for array in arguments))
    za, zb = fill(z_shape, swaps(az, *z_send))

    x_shape = like(XMAIN, rows, depth)
    x_send = call(functools.partial(pack_x, ax), "pack_x", 8, out_shape=(x_shape, x_shape))(local)
    xa, xb = fill(x_shape, swaps(ax, *x_send))

    count_y = min(lax.axis_size(ay) - 1, 2)
    ys, more_ys = [], []
    c_shape = like(groups_of(W, depth)[1], rows, depth)
    sent = call(
        functools.partial(join_x, ax, ay),
        "join_x",
        8,
        out_shape=(c_shape, c_shape) + (like(CHANNELS * planes + groups, W, depth),) * count_y,
    )(za, zb, local)
    c_send, y_send = sent[:2], sent[2:]
    ca, cb = fill(c_shape, swaps(ax, *c_send))
    if count_y:
        ys = swaps(ay, y_send[0], y_send[-1])[:count_y]
    vmem = lambda shapes: [pltpu.VMEM(shape, f32) for shape in shapes]
    flow = (3, total, rows, depth)
    tall = cell_shapes(total, rows + 16, depth)
    wide = result_shapes(total, rows, depth)
    centre = (SHIFTED + UP, rows, depth)
    shapes = tall[:5] + wide[:3] + [flow] + tall[5:7]
    found = call(
        inner_local,
        "inner_local",
        16,
        out_shape=[like(*shape) for shape in shapes],
        in_specs=[VMEM] * 4,
        out_specs=[VMEM] * len(shapes),
        scratch_shapes=vmem(tall[7:] + [centre]),
    )(local, za, zb, tabs)
    arrays, found, parts = found[:5], found[5:9], found[9:]

    columns, *y_send = call(
        functools.partial(join_y, ay, ax, planes),
        "join_y",
        8,
        out_shape=(like(CHANNELS, rows, depth),)
        + (like(2 * XMAIN + CHANNELS, W, depth),) * count_y,
        in_specs=[VMEM] * 6 + [ANY] * (count_y + 1),
    )(za, zb, xa, xb, ca, cb, *ys, parts[1])
    if count_y:
        more_ys = swaps(ay, y_send[0], y_send[-1])[:count_y]

    edges = cell_shapes(total, 16, depth)
    shapes = wide + [flow] + edges + tall[:5]
    halves = call(
        functools.partial(inner, ax, planes),
        "inner",
        16,
        out_shape=[like(*shape) for shape in shapes],
        in_specs=[VMEM] * 15,
        out_specs=[VMEM] * len(shapes),
        scratch_shapes=vmem(tall[5:] + [centre]),
        input_output_aliases={6: 0, 7: 1, 8: 2, 9: 6, **{10 + i: 17 + i for i in range(5)}},
    )(columns, xa, xb, tabs, *parts, *found, *arrays)[:17]

    solutions = [
        (3, count, height, depth) for height in (rows + 16, 16) for count in (total, 1) for _ in range(2)
    ]
    edge_shapes = result_shapes(total, 2 * W, depth)
    shapes = edges + edge_shapes[:3] + [(3, total, 2 * W, depth)]
    found = call(
        functools.partial(finish_local, ay, count_y, planes),
        "finish_local",
        16,
        out_shape=[like(*shape) for shape in shapes],
        in_specs=[VMEM] * (1 + count_y + 10),
        out_specs=[VMEM] * len(shapes),
        scratch_shapes=vmem(
            [
                (CHANNELS, planes, 2 * W, depth),
                (groups, 2 * W, depth),
                (SHIFTED + UP, 2 * W, depth),
            ]
        ),
        input_output_aliases={1 + count_y + i: i for i in range(10)},
    )(tabs, *ys, *halves[7:])
    before = 3 + count_y + 7
    residual, update, *_ = call(
        functools.partial(finish, ay, count_y),
        "finish",
        16,
        out_shape=[cells, like(planes, rows, depth)] + [like(*shape) for shape in shapes],
        in_specs=[VMEM] * (before + len(shapes)),
        out_specs=[VMEM] * (2 + len(shapes)),
        scratch_shapes=vmem(
            [
                (CHANNELS, 2 * W + 1, 2 * W, depth),
                (SHIFTED + UP, 2 * W, depth),
                *edge_shapes[3:],
                *solutions,
            ]
        ),
        input_output_aliases={before + i: 2 + i for i in range(len(shapes))},
    )(local, tabs, accum, *more_ys, *halves[:7], *found)
    return residual, update


def solution(mesh):
    return jax.shard_map(
        body,
        mesh=mesh,
        in_specs=(
            P(None, "gx", "gy", "gz"),
            P(None, "gx", "gy", "gz"),
            P("gx", "gy", "gz"),
            P(None, "gx", "gy", "gz"),
            P("gx", "gy", "gz"),
            P("gx", "gy", "gz"),
            P(),
            P(),
            P(),
        ),
        out_specs=(P(None, "gx", "gy", "gz"), P("gx", "gy", "gz")),
        check_vma=False,
    )
```

```python
import functools
import itertools

import jax
import jax.numpy as jnp
from jax import lax
from jax.experimental import pallas as pl
from jax.experimental.pallas import tpu as pltpu
from jax.sharding import PartitionSpec as P

SWEEPS = 4
W = SWEEPS
relax_weight = 0.7

neighbour_offsets = [
    (along_x, along_y, along_z)
    for along_x in (-1, 0, 1)
    for along_y in (-1, 0, 1)
    for along_z in (-1, 0, 1)
    if (along_x, along_y, along_z) != (0, 0, 0)
]
upper_offsets = [offset for offset in neighbour_offsets if offset > (0, 0, 0)]
UP = len(upper_offsets)
FLAT = sum(1 for offset in upper_offsets if offset[0] == 0)
STEP = UP - FLAT

FAR = 5 + STEP
CHANNELS = FAR + FLAT + 2
STORAGE, OWN = FAR + FLAT, FAR + FLAT + 1
NEAR = W - 1
XMAIN = CHANNELS * NEAR + FAR
VMEM = pl.BlockSpec(memory_space=pltpu.VMEM)
ANY = pl.BlockSpec(memory_space=pl.ANY)
HBM = pl.BlockSpec(memory_space=pltpu.MemorySpace.HBM)
f32 = jnp.float32


def t_channel(k):
    return FAR + k if k < FLAT else 5 + k - FLAT


def pick(parity, even, odd):
    shape = (even if odd is None else odd).shape
    if even is None:
        even = jnp.zeros(shape, f32)
    if odd is None:
        odd = jnp.zeros(shape, f32)
    return jnp.where(jnp.full(shape, parity, jnp.int32) == 0, even, odd)


def parity_of(axis):
    return lax.rem(lax.axis_index(axis), 2)


def swaps(axis, first, second):
    count = lax.axis_size(axis)
    got = []
    for start, message in ((0, first), (1, second)):
        pairs = [(i, i + 1) for i in range(start, count - 1, 2)]
        if not pairs:
            got.append(None)
            continue
        got.append(lax.ppermute(message, axis, pairs + [(b, a) for a, b in pairs]))
    return got


def lanes_of(shape):
    return lax.broadcasted_iota(jnp.int32, shape, len(shape) - 1)


def span_of(planes):
    return 2 * W * planes


def groups_of(planes, depth):
    per = depth // span_of(planes)
    return per, -(-CHANNELS // per)


def lookups(tabs, region, numbers):
    index = region.astype(jnp.int32)
    return [
        jnp.take_along_axis(tabs[n], index, axis=1, mode="promise_in_bounds") for n in numbers
    ]


def pack_z(axis, *refs):
    state, mass, pore, trans, active, region, *tables = refs[:9]
    local, accum, tabs, first, second = refs[9:14]
    flags, masses, pores, small, sems = refs[14:]
    planes, rows, depth = pore.shape
    copies = [
        pltpu.make_async_copy(active, flags.at[0], sems.at[0]),
        pltpu.make_async_copy(region, flags.at[1], sems.at[1]),
        pltpu.make_async_copy(state, local.at[0:3], sems.at[2]),
        pltpu.make_async_copy(mass, masses, sems.at[3]),
        pltpu.make_async_copy(pore, pores, sems.at[4]),
    ]
    copies += [
        pltpu.make_async_copy(table, small.at[n], sems.at[5 + n]) for n, table in enumerate(tables)
    ]
    late = [
        pltpu.make_async_copy(trans.at[FLAT:UP], local.at[5:FAR], sems.at[8]),
        pltpu.make_async_copy(trans.at[0:FLAT], local.at[FAR : FAR + FLAT], sems.at[9]),
    ]
    for copy in copies + late:
        copy.start()
    for copy in copies:
        copy.wait()
    regions = tables[0].shape[1]
    for n in range(3):
        for c in range(3):
            tabs[3 * n + c, :, 0:regions] = jnp.broadcast_to(small[n, c : c + 1, :], (8, regions))
    for x in range(planes):
        for tile in range(rows // 8):
            span = slice(8 * tile, 8 * tile + 8)
            on = flags[0, x, span, :].astype(f32)
            level = flags[1, x, span, :]
            local[3, x, span, :] = on
            local[4, x, span, :] = level.astype(f32)
            press, water, gas = (local[c, x, span, :] for c in range(3))
            look = lookups(tabs, level, range(6))
            sat = (water, 1.0 - water - gas, gas)
            expand = [look[c] * jnp.exp(look[3 + c] * (press - 0.5)) for c in range(3)]
            volume = pores[x, span, :]
            stored = volume * (look[3] * sat[0] + look[4] * sat[1] + look[5] * sat[2])
            stored = jnp.where(on > 0, stored, 1.0)
            own = jnp.zeros((8, depth), f32)
            for c in range(3):
                value = volume * expand[c] * sat[c] - masses[c, x, span, :]
                accum[c, x, span, :] = value
                own = own + value / (expand[c] * stored)
            local[STORAGE, x, span, :] = stored
            local[OWN, x, span, :] = on * own
    for copy in late:
        copy.wait()

    per, groups = groups_of(planes, depth)
    even = parity_of(axis)
    lane = lanes_of((8, depth))

    @pl.loop(0, rows // 8, unroll=True)
    def _(tile):
        span = pl.ds(pl.multiple_of(8 * tile, 8), 8)
        for group in range(groups):
            high = jnp.zeros((8, depth), f32)
            low = jnp.zeros((8, depth), f32)
            for c in range(group * per, min(CHANNELS, group * per + per)):
                for x in range(planes):
                    base = (c % per) * span_of(planes) + 2 * W * x
                    values = local[c, x, span, :]
                    here = (lane >= base + W) & (lane < base + 2 * W)
                    high = jnp.where(here, pltpu.roll(values, (base + 2 * W) % depth, 1), high)
                    here = (lane >= base) & (lane < base + W)
                    low = jnp.where(here, pltpu.roll(values, base % depth, 1), low)
            first[group, span, :] = pick(even, high, low)
            second[group, span, :] = pick(even, low, high)


def pack_x(axis, local, *outs):
    planes = local.shape[1]
    even = parity_of(axis)
    for out, up in zip(outs, (even == 0, even != 0)):
        near = jnp.where(up, planes - NEAR, 0)
        far = jnp.where(up, planes - W, W - 1)
        for c in range(CHANNELS):
            for q in range(NEAR):
                out[c * NEAR + q] = local[c, near + q]
            if c < FAR:
                out[CHANNELS * NEAR + c] = local[c, far]


def put_rows(outs, n, values, even):
    head, tail = values[:W], values[values.shape[0] - W :]
    for out, up, down in zip(outs, (tail, head), (head, tail)):
        out[n] = pick(even, up, down)


def join_x(axis, y_axis, za, zb, local, *outs):
    planes = local.shape[1]
    even_y = parity_of(y_axis)
    for c in range(CHANNELS):
        for x in range(planes):
            put_rows(outs[2:], c * planes + x, local[c, x], even_y)
    for group in range(za.shape[0]):
        put_rows(outs[2:], CHANNELS * planes + group, za[group] + zb[group], even_y)
    rows, depth = za.shape[1:]
    even = parity_of(axis)
    per, _ = groups_of(planes, depth)
    per_x, groups_x = groups_of(W, depth)
    lane = lanes_of((rows, depth))
    for group in range(groups_x):
        sides = [jnp.zeros((rows, depth), f32) for _ in range(2)]
        for c in range(group * per_x, min(CHANNELS, group * per_x + per_x)):
            values = za[c // per] + zb[c // per]
            to = (c % per_x) * span_of(W)
            here = (lane >= to) & (lane < to + span_of(W))
            for n, plane in enumerate((planes - W, 0)):
                source = (c % per) * span_of(planes) + 2 * W * plane
                sides[n] = jnp.where(here, pltpu.roll(values, (to - source) % depth, 1), sides[n])
        outs[0][group] = pick(even, *sides)
        outs[1][group] = pick(even, *sides[::-1])


def join_y(axis, x_axis, planes, za, zb, xa, xb, ca, cb, *refs):
    count = len(refs) // 2
    columns, *outs = refs[count:]
    rows, depth = xa.shape[1:]
    even = parity_of(axis)
    even_x = parity_of(x_axis)
    per_x, _ = groups_of(W, depth)
    lane = lanes_of((rows, depth))
    for c in range(CHANNELS):
        own = own_columns(c, za, zb, planes, slice(0, rows))
        group, base = c // per_x, (c % per_x) * span_of(W)
        a, b = ca[group], cb[group]
        below = pltpu.roll(pick(even_x, b, a), (depth - base) % depth, 1)
        above = pltpu.roll(pick(even_x, a, b), (2 * W * (planes + W) - base) % depth, 1)
        values = jnp.where(lane < 2 * W * W, below, jnp.where(lane < 2 * W * (W + planes), own, above))
        columns[c] = values
        put_rows(outs, 2 * XMAIN + c, values, even)

    @pl.loop(0, XMAIN // 2, unroll=True)
    def _(i):
        for j in range(2):
            n = 2 * i + j
            a, b = xa[n], xb[n]
            put_rows(outs, n, pick(even_x, b, a), even)
            put_rows(outs, XMAIN + n, pick(even_x, a, b), even)


PRESS, MOB, SLOPE, ACT = 0, 1, 4, 7
SHIFTED = 8


def z_shift(values, columns, plane, step):
    depth = values.shape[-1]
    lane = lanes_of(values.shape)
    if step > 0:
        edge = pltpu.roll(columns, depth - 1 - 2 * W * plane, 1)
        return jnp.where(lane == depth - 1, edge, pltpu.roll(values, depth - 1, 1))
    edge = pltpu.roll(columns, depth - 2 * W * plane - 2 * W + 1, 1)
    return jnp.where(lane == 0, edge, pltpu.roll(values, 1, 1))


def z_shift_columns(values, step):
    return pltpu.roll(values, values.shape[-1] - 1 if step > 0 else 1, 1)


def z_edge(current, values, plane, step):
    lane = lanes_of(values.shape)
    if step > 0:
        at = 2 * W * plane + 2 * W - 1
        return jnp.where(lane == at, pltpu.roll(values, at, 1), current)
    at = 2 * W * plane
    return jnp.where(lane == at, pltpu.roll(values, at + 1, 1), current)


def properties(get, plane, is_columns, put, tabs, arrays, halo, centre, span, done=None):
    fields, lower, half, weight, base = halo if is_columns else arrays
    halo_fields, halo_lower = halo[:2]
    press, water, gas, active, region = (get(c) for c in range(5))
    look = lookups(tabs, region, range(9))
    formation, compress, viscous = look[:3], look[3:6], look[6:]
    sat = (water, 1.0 - water - gas, gas)
    expand = [formation[c] * jnp.exp(compress[c] * (press - 0.5)) for c in range(3)]
    mob = [viscous[c] * expand[c] * sat[c] * sat[c] for c in range(3)]
    stored = get(STORAGE)
    stored = jnp.where(stored > 0, stored, 1.0)
    for c in range(3):
        put(weight, (c, plane), active / (expand[c] * stored))
    put(base, (plane,), get(OWN))
    shifts = []
    one = [press] + mob + [compress[c] * mob[c] for c in range(3)] + [active]
    for f, values in enumerate(one):
        put(fields, (f, 1, plane), values)
        shifts += [(0, (f, step + 1), step, values, f) for step in (-1, 1)]
    for k, offset in enumerate(upper_offsets):
        values = 0.5 * get(t_channel(k))
        put(half, (k, plane), values)
        values = values * active
        if offset[2] == 0:
            put(lower, (k, plane), values)
        else:
            shifts.append((1, (k,), -offset[2], values, SHIFTED + k))
    for array, lead, step, values, slot in shifts:
        if is_columns:
            centre[slot, span, :] = values
            shifted = z_shift_columns(values, step)
            if done is None:
                put((fields, lower)[array], (*lead, 0), shifted)
            else:
                keep = lambda now: jnp.where(done, now, shifted)
                put((fields, lower)[array], (*lead, 0), None, keep)
        else:
            put((fields, lower)[array], (*lead, plane), z_shift(values, centre[slot, span, :], plane, step))
            put((halo_fields, halo_lower)[array], (*lead, 0), None, lambda now: z_edge(now, values, plane, step))


def x_roll(values, step, is_columns):
    if not is_columns or step == 0:
        return values
    depth = values.shape[-1]
    return pltpu.roll(values, (depth - 2 * W * step) % depth, 1)


def link_cells(plane, is_columns, first, stride, arrays, out, results):
    fields, lower, half, weight, base = arrays
    coupling, scale, start = results
    depth = fields.shape[-1]
    here = (0, 0, 0)

    def read(ref, lead, offset):
        dx = 0 if is_columns else offset[0]
        values = ref[(*lead, plane + dx, pl.ds(first + stride * offset[1], 8), slice(None))]
        return x_roll(values, offset[0], is_columns)

    def at(f, offset):
        return read(fields, (f, offset[2] + 1), offset)

    press = at(PRESS, here)
    w = [read(weight, (c,), here) for c in range(3)]
    mob = [at(MOB + c, here) for c in range(3)]
    own_mob = w[0] * mob[0] + w[1] * mob[1] + w[2] * mob[2]
    own_slope = w[0] * at(SLOPE, here) + w[1] * at(SLOPE + 1, here) + w[2] * at(SLOPE + 2, here)
    flux = [jnp.zeros((8, depth), f32) for _ in range(3)]
    drops = jnp.zeros((8, depth), f32)
    means = jnp.ones((8, depth), f32)
    for n, offset in enumerate(neighbour_offsets):
        if offset > here:
            link = read(half, (upper_offsets.index(offset),), here) * at(ACT, offset)
        else:
            k = upper_offsets.index(tuple(-o for o in offset))
            link = read(lower, (k,), offset)
        drop = link * (press - at(PRESS, offset))
        other = [at(MOB + c, offset) for c in range(3)]
        for c in range(3):
            flux[c] = flux[c] + drop * other[c]
        drops = drops + drop
        mean = link * (own_mob + (w[0] * other[0] + w[1] * other[1] + w[2] * other[2]))
        slope = (
            w[0] * at(SLOPE, offset) + w[1] * at(SLOPE + 1, offset) + w[2] * at(SLOPE + 2, offset)
        )
        means = means + mean
        coupling[n, plane, out, :] = drop * slope - mean
    flux = [flux[c] + mob[c] * drops for c in range(3)]
    rate = relax_weight / (means + own_slope * drops)
    right = read(base, (), here) + (w[0] * flux[0] + w[1] * flux[1] + w[2] * flux[2])
    scale[plane, out, :] = rate
    start[plane, out, :] = -rate * right
    return flux


def row_cells(tiles, tabs, arrays, halo, centre):
    def cells(get, plane, is_columns=False):
        for tile in range(tiles):
            span, to = slice(8 * tile, 8 * tile + 8), slice(8 + 8 * tile, 16 + 8 * tile)

            def put(ref, lead, values, change=None):
                at = (*lead, to, slice(None))
                ref[at] = values if change is None else change(ref[at])

            properties(
                lambda c: get(c, span), plane, is_columns, put, tabs, arrays, halo, centre, span
            )

    return cells


def row_links(tiles, plane, is_columns, arrays, results, store=None):
    for tile in range(tiles):
        out = slice(8 * tile, 8 * tile + 8)
        flow = link_cells(plane, is_columns, 8 + 8 * tile, 1, arrays, out, results)
        if store is not None:
            for c in range(3):
                store[c, plane, out, :] = flow[c]


def own_columns(c, za, zb, planes, span):
    depth = za.shape[-1]
    per, _ = groups_of(planes, depth)
    group, base = c // per, (c % per) * span_of(planes)
    return pltpu.roll(za[group, span, :] + zb[group, span, :], (2 * W * W - base) % depth, 1)


def among_own(planes, shape):
    lane = lanes_of(shape)
    return (lane >= 2 * W * W) & (lane < 2 * W * (W + planes))


def inner_local(local, za, zb, tabs, *refs):
    arrays, results, store, parts = refs[:5], refs[5:8], refs[8], refs[9:11]
    halo, centre = (*parts, *refs[11:14]), refs[14]
    planes, rows, depth = local.shape[1:]
    tiles = rows // 8
    cells = row_cells(tiles, tabs, arrays, halo, centre)

    def columns(c, span):
        values = own_columns(c, za, zb, planes, span)
        return jnp.where(among_own(planes, values.shape), values, 0.0)

    cells(columns, 0, True)

    @pl.loop(0, planes, unroll=True)
    def _(x):
        cells(lambda c, span: local[c, x, span, :], W + x)

    @pl.loop(W + 1, W + planes - 1, unroll=True)
    def _(plane):
        row_links(tiles, plane, False, arrays, results, store)


def inner(x_axis, planes, columns, xa, xb, tabs, *refs):
    parts, refs = refs[:2], refs[11:]
    results, halo_results, store = refs[:3], refs[3:6], refs[6]
    edges, arrays, halo, centre = refs[7:17], refs[17:22], refs[22:27], refs[27]
    rows, depth = xa.shape[1:]
    total = planes + 2 * W
    even_x = parity_of(x_axis)
    tiles = rows // 8
    cells = row_cells(tiles, tabs, arrays, halo, centre)

    cells(lambda c, span: columns[c, span, :], 0, True)
    own = among_own(planes, (8, depth))
    for array, part in zip(halo, parts):
        for lead in itertools.product(*(range(n) for n in part.shape[:-2])):
            for tile in range(tiles):
                at = (*lead, slice(8 + 8 * tile, 16 + 8 * tile), slice(None))
                array[at] = jnp.where(own, part[at], array[at])

    def from_x(n, low):
        def get(c, span):
            i = n(c)
            if i is None:
                return jnp.zeros((8, depth), f32)
            u, v = xa[i, span, :], xb[i, span, :]
            return pick(even_x, v, u) if low else pick(even_x, u, v)

        return get

    @pl.loop(0, NEAR, unroll=True)
    def _(q):
        near = lambda c: c * NEAR + q
        cells(from_x(near, True), 1 + q)
        cells(from_x(near, False), W + planes + q)

    far = lambda c: CHANNELS * NEAR + c if c < FAR else None
    cells(from_x(far, True), 0)
    cells(from_x(far, False), total - 1)

    def hand_on(sources, targets, plane):
        for source, target in zip(sources, targets):
            for lead in itertools.product(*(range(n) for n in source.shape[:-3])):
                last = source[(*lead, plane, slice(6 + rows, 8 + rows), slice(None))]
                head = source[(*lead, plane, slice(8, 10), slice(None))]
                target[(*lead, plane, pl.ds(0, 2, stride=2), slice(None))] = last
                target[(*lead, plane, pl.ds(RING - 3, 2, stride=2), slice(None))] = head

    hand_on(halo, edges[5:], 0)

    @pl.loop(0, total, unroll=True)
    def _(plane):
        hand_on(arrays, edges[:5], plane)

    row_links(tiles, 0, True, halo, halo_results)

    @pl.loop(0, W, unroll=True)
    def _(n):
        row_links(tiles, 1 + n, False, arrays, results, store)
        row_links(tiles, W + planes - 1 + n, False, arrays, results, store)


RING = 2 * (W + 2)


def put_ring(ref, lead, values, change=None):
    low = (*lead, pl.ds(1, W, stride=2), slice(None))
    high = (*lead, pl.ds(4, W, stride=2), slice(None))
    if change is not None:
        values = change(jnp.concatenate([ref[low], ref[high]], axis=0))
    ref[low] = values[:W]
    ref[high] = values[W:]


def halo_rows(even_y, sources, n, target, at):
    shape = target.shape[-1:]
    low = high = jnp.zeros((W, *shape), f32)
    if sources:
        a = sources[0][n]
        b = sources[1][n] if len(sources) > 1 else None
        low, high = pick(even_y, b, a), pick(even_y, a, b)
    target[(*at, slice(0, W), slice(None))] = low
    target[(*at, slice(W, 2 * W), slice(None))] = high


def ring_links(plane, is_columns, arrays, results, store):
    flow = link_cells(plane, is_columns, 2, 2, arrays, slice(0, 8), results)
    if not is_columns:
        for c in range(3):
            store[c, plane] = flow[c]


def finish_local(axis, count_y, planes, tabs, *refs):
    ys, refs = refs[:count_y], refs[count_y + 10 :]
    arrays, halo, results, store = refs[:5], refs[5:10], refs[10:13], refs[13]
    raw, packed, centre = refs[14:]
    depth = raw.shape[-1]
    even_y = parity_of(axis)
    per, groups = groups_of(planes, depth)
    for group in range(groups):
        halo_rows(even_y, ys, CHANNELS * planes + group, packed, (group,))

    @pl.loop(0, CHANNELS, unroll=True)
    def _(c):
        for x in range(planes):
            halo_rows(even_y, ys, c * planes + x, raw, (c, x))

    def cells(get, plane, is_columns=False):
        span = slice(0, 2 * W)
        properties(get, plane, is_columns, put_ring, tabs, arrays, halo, centre, span)

    own = among_own(planes, (2 * W, depth))

    def columns(c):
        base = (c % per) * span_of(planes)
        return jnp.where(own, pltpu.roll(packed[c // per], (2 * W * W - base) % depth, 1), 0.0)

    cells(columns, 0, True)

    @pl.loop(0, planes, unroll=True)
    def _(x):
        cells(lambda c: raw[c, x], W + x)

    @pl.loop(W + 1, W + planes - 1, unroll=True)
    def _(plane):
        ring_links(plane, False, arrays, results, store)


def finish(axis, count_y, local, *refs):
    tabs, accum, more_ys, refs = refs[0], refs[1], refs[2 : 2 + count_y], refs[2 + count_y :]
    results, halo_results, store = refs[:3], refs[3:6], refs[6]
    residual, update = refs[21:23]
    arrays, halo = refs[23:28], refs[28:33]
    edge_results, edge_store = refs[33:36], refs[36]
    raw, centre, edge_halo_results = refs[37], refs[38], refs[39:42]
    sols, halo_sols, edge_sols, edge_halo_sols = (refs[42 + 2 * i : 44 + 2 * i] for i in range(4))
    planes, rows, depth = local.shape[1:]
    total = planes + 2 * W
    even_y = parity_of(axis)

    @pl.loop(0, CHANNELS, unroll=True)
    def _(c):
        for q in range(NEAR):
            halo_rows(even_y, more_ys, c * NEAR + q, raw, (c, 1 + q))
            halo_rows(even_y, more_ys, XMAIN + c * NEAR + q, raw, (c, W + q))
        halo_rows(even_y, more_ys, 2 * XMAIN + c, raw, (c, 2 * W))

    @pl.loop(0, FAR, unroll=True)
    def _(c):
        halo_rows(even_y, more_ys, CHANNELS * NEAR + c, raw, (c, 0))
        halo_rows(even_y, more_ys, XMAIN + CHANNELS * NEAR + c, raw, (c, 2 * W - 1))

    for c in range(FAR, CHANNELS):
        for slot in (0, 2 * W - 1):
            raw[c, slot] = jnp.zeros((2 * W, depth), f32)

    def cells(slot, plane, is_columns=False):
        done = among_own(planes, (2 * W, depth)) if is_columns else None
        get, span = lambda c: raw[c, slot], slice(0, 2 * W)
        properties(get, plane, is_columns, put_ring, tabs, arrays, halo, centre, span, done)

    cells(2 * W, 0, True)

    @pl.loop(0, W, unroll=True)
    def _(n):
        cells(n, n)
        cells(W + n, W + planes + n)

    ring_links(0, True, halo, edge_halo_results, None)

    @pl.loop(0, W, unroll=True)
    def _(n):
        ring_links(1 + n, False, arrays, edge_results, edge_store)
        ring_links(W + planes - 1 + n, False, arrays, edge_results, edge_store)

    tiles = rows // 8

    row = lax.broadcasted_iota(jnp.int32, (8, depth), 0)

    def merged(mains, edge):
        first, last = pltpu.roll(edge, 1, 0), pltpu.roll(edge, 7, 0)
        mains = [jnp.where(row == 0, first, mains[0])] + mains[1:]
        return mains[:-1] + [jnp.where(row == 7, last, mains[-1])]

    def put_parts(is_columns, slot, step, plane, mains, edge):
        to, edge_to = (
            (halo_sols[slot], edge_halo_sols[slot]) if is_columns else (sols[slot], edge_sols[slot])
        )
        for tile, values in enumerate(mains):
            to[step + 1, plane, 8 + 8 * tile : 16 + 8 * tile, :] = values
        edge_to[step + 1, plane, 2:10, :] = edge
        to[step + 1, plane, 7:8, :] = edge[5:6]
        to[step + 1, plane, 8 + rows : 9 + rows, :] = edge[2:3]
        edge_to[step + 1, plane, 0:1, :] = mains[-1][6:7]
        edge_to[step + 1, plane, RING - 1 : RING, :] = mains[0][1:2]

    def halo_parts(slot, step):
        mains = [
            halo_sols[slot][step + 1, 0, 8 + 8 * tile : 16 + 8 * tile, :] for tile in range(tiles)
        ]
        return mains, edge_halo_sols[slot][step + 1, 0, 2:10, :]

    def put_solution(slot, plane, mains, edge, is_columns=False):
        mains = merged(mains, edge)
        put_parts(is_columns, slot, 0, plane, mains, edge)
        for step in (-1, 1):
            if is_columns:
                shift = lambda values: z_shift_columns(values, step)
                put_parts(True, slot, step, plane, [shift(u) for u in mains], shift(edge))
                continue
            shift = lambda u, v: z_shift(u, v, plane, step)
            halo_mains, halo_edge = halo_parts(slot, 0)
            shifted = [shift(u, v) for u, v in zip(mains, halo_mains)]
            put_parts(False, slot, step, plane, shifted, shift(edge, halo_edge))
            shift = lambda u, v: z_edge(u, v, plane, step)
            halo_mains, halo_edge = halo_parts(slot, step)
            shifted = [shift(u, v) for u, v in zip(halo_mains, mains)]
            put_parts(True, slot, step, 0, shifted, shift(halo_edge, edge))

    def relaxed(slot, plane, tile, is_columns=False):
        if tile is None:
            ref = (edge_halo_sols if is_columns else edge_sols)[slot]
            first, stride, out = 2, 2, slice(0, 8)
            coupling, scale, start = edge_halo_results if is_columns else edge_results
        else:
            ref = (halo_sols if is_columns else sols)[slot]
            first, stride = 8 + 8 * tile, 1
            out = slice(8 * tile, 8 * tile + 8)
            coupling, scale, start = halo_results if is_columns else results

        def get(offset):
            dx = 0 if is_columns else offset[0]
            values = ref[offset[2] + 1, plane + dx, pl.ds(first + stride * offset[1], 8), :]
            return x_roll(values, offset[0], is_columns)

        parts = [jnp.zeros((8, depth), f32) for _ in range(2)]
        for n, offset in enumerate(neighbour_offsets):
            parts[n % 2] = parts[n % 2] + coupling[n, plane, out, :] * get(offset)
        return (
            (1.0 - relax_weight) * get((0, 0, 0))
            + start[plane, out, :]
            - scale[plane, out, :] * (parts[0] + parts[1])
        )

    def first_sweep(plane, is_columns=False):
        start = (halo_results if is_columns else results)[2]
        edge = (edge_halo_results if is_columns else edge_results)[2]
        mains = [start[plane, 8 * tile : 8 * tile + 8, :] for tile in range(tiles)]
        put_solution(0, plane, mains, edge[plane], is_columns)

    first_sweep(0, True)

    @pl.loop(1, total - 1, unroll=True)
    def _(plane):
        first_sweep(plane)

    def sweep_of(slot, plane, is_columns=False):
        mains = [relaxed(slot, plane, tile, is_columns) for tile in range(tiles)]
        put_solution(1 - slot, plane, mains, relaxed(slot, plane, None, is_columns), is_columns)

    for sweep in range(2, SWEEPS):
        slot = sweep % 2
        sweep_of(slot, 0, True)

        @pl.loop(sweep, total - sweep, unroll=True)
        def _(plane):
            sweep_of(slot, plane)

    @pl.loop(0, planes, unroll=True)
    def _(x):
        slot, plane = SWEEPS % 2, W + x
        edge = relaxed(slot, plane, None)
        for tile in range(tiles):
            span = slice(8 * tile, 8 * tile + 8)
            update[x, span, :] = relaxed(slot, plane, tile)
            active = local[3, x, span, :]
            for c in range(3):
                flow = store[c, plane, span, :]
                residual[c, x, span, :] = active * (accum[c, x, span, :] + flow)
        for row_of, edge_row in ((0, 7), (rows - 1, 0)):
            to, source = slice(row_of, row_of + 1), slice(edge_row, edge_row + 1)
            update[x, to, :] = edge[source]
            active = local[3, x, to, :]
            for c in range(3):
                flow = edge_store[c, plane, source, :]
                residual[c, x, to, :] = active * (accum[c, x, to, :] + flow)


def call(kernel, name, mib, **options):
    return pl.pallas_call(
        kernel,
        name=name,
        compiler_params=pltpu.CompilerParams(vmem_limit_bytes=mib << 20),
        **options,
    )


def cell_shapes(total, height, depth):
    return [
        (*lead, count, height, depth)
        for count in (total, 1)
        for lead in ((SHIFTED, 3), (UP,), (UP,), (3,), ())
    ]


def result_shapes(total, height, depth):
    return [
        shape
        for count in (total, 1)
        for shape in ((2 * UP, count, height, depth), (count, height, depth), (count, height, depth))
    ]


def body(
    cell_state,
    old_mass,
    pore_volume,
    transmissibility,
    active_mask,
    pvt_region,
    formation_factor,
    compressibility,
    inverse_viscosity,
):
    ax, ay, az = "gx", "gy", "gz"
    planes, rows, depth = pore_volume.shape
    total = planes + 2 * W
    per, groups = groups_of(planes, depth)
    assert per >= 1 and 2 * W * total <= depth and rows % 8 == 0 and RING <= 16
    tables = (formation_factor, compressibility, inverse_viscosity)
    like = lambda *shape: jax.ShapeDtypeStruct(shape, f32)
    fill = lambda shape, got: [jnp.zeros(shape.shape, f32) if one is None else one for one in got]

    arguments = (
        *(cell_state, old_mass, pore_volume, transmissibility, active_mask, pvt_region),
        *tables,
    )
    z_shape = like(groups, rows, depth)
    cells = like(3, planes, rows, depth)
    local, accum, tabs, *z_send = call(
        functools.partial(pack_z, az),
        "pack_z",
        8,
        out_shape=(like(CHANNELS, planes, rows, depth), cells, like(9, 8, depth), z_shape, z_shape),
        in_specs=[HBM] * 9,
        out_specs=(VMEM,) * 5,
        scratch_shapes=[
            pltpu.VMEM((2, planes, rows, depth), jnp.int32),
            pltpu.VMEM(cells.shape, f32),
            pltpu.VMEM((planes, rows, depth), f32),
            pltpu.VMEM((3, *formation_factor.shape), f32),
            pltpu.SemaphoreType.DMA((10,)),
        ],
    )(*(pltpu.with_memory_space_constraint(array, pltpu.MemorySpace.HBM) for array in arguments))
    za, zb = fill(z_shape, swaps(az, *z_send))

    x_shape = like(XMAIN, rows, depth)
    x_send = call(functools.partial(pack_x, ax), "pack_x", 8, out_shape=(x_shape, x_shape))(local)
    xa, xb = fill(x_shape, swaps(ax, *x_send))

    count_y = min(lax.axis_size(ay) - 1, 2)
    ys, more_ys = [], []
    c_shape = like(groups_of(W, depth)[1], rows, depth)
    sent = call(
        functools.partial(join_x, ax, ay),
        "join_x",
        8,
        out_shape=(c_shape, c_shape) + (like(CHANNELS * planes + groups, W, depth),) * count_y,
    )(za, zb, local)
    c_send, y_send = sent[:2], sent[2:]
    ca, cb = fill(c_shape, swaps(ax, *c_send))
    if count_y:
        ys = swaps(ay, y_send[0], y_send[-1])[:count_y]
    vmem = lambda shapes: [pltpu.VMEM(shape, f32) for shape in shapes]
    flow = (3, total, rows, depth)
    tall = cell_shapes(total, rows + 16, depth)
    wide = result_shapes(total, rows, depth)
    centre = (SHIFTED + UP, rows, depth)
    shapes = tall[:5] + wide[:3] + [flow] + tall[5:7]
    found = call(
        inner_local,
        "inner_local",
        16,
        out_shape=[like(*shape) for shape in shapes],
        in_specs=[VMEM] * 4,
        out_specs=[VMEM] * len(shapes),
        scratch_shapes=vmem(tall[7:] + [centre]),
    )(local, za, zb, tabs)
    arrays, found, parts = found[:5], found[5:9], found[9:]

    columns, *y_send = call(
        functools.partial(join_y, ay, ax, planes),
        "join_y",
        8,
        out_shape=(like(CHANNELS, rows, depth),)
        + (like(2 * XMAIN + CHANNELS, W, depth),) * count_y,
        in_specs=[VMEM] * 6 + [ANY] * (count_y + 1),
    )(za, zb, xa, xb, ca, cb, *ys, parts[1])
    if count_y:
        more_ys = swaps(ay, y_send[0], y_send[-1])[:count_y]

    edges = cell_shapes(total, 16, depth)
    shapes = wide + [flow] + edges + tall[:5]
    halves = call(
        functools.partial(inner, ax, planes),
        "inner",
        16,
        out_shape=[like(*shape) for shape in shapes],
        in_specs=[VMEM] * 15,
        out_specs=[VMEM] * len(shapes),
        scratch_shapes=vmem(tall[5:] + [centre]),
        input_output_aliases={6: 0, 7: 1, 8: 2, 9: 6, **{10 + i: 17 + i for i in range(5)}},
    )(columns, xa, xb, tabs, *parts, *found, *arrays)[:17]

    solutions = [
        (3, count, height, depth) for height in (rows + 16, 16) for count in (total, 1) for _ in range(2)
    ]
    edge_shapes = result_shapes(total, 2 * W, depth)
    shapes = edges + edge_shapes[:3] + [(3, total, 2 * W, depth)]
    found = call(
        functools.partial(finish_local, ay, count_y, planes),
        "finish_local",
        16,
        out_shape=[like(*shape) for shape in shapes],
        in_specs=[VMEM] * (1 + count_y + 10),
        out_specs=[VMEM] * len(shapes),
        scratch_shapes=vmem(
            [
                (CHANNELS, planes, 2 * W, depth),
                (groups, 2 * W, depth),
                (SHIFTED + UP, 2 * W, depth),
            ]
        ),
        input_output_aliases={1 + count_y + i: i for i in range(10)},
    )(tabs, *ys, *halves[7:])
    before = 3 + count_y + 7
    residual, update, *_ = call(
        functools.partial(finish, ay, count_y),
        "finish",
        16,
        out_shape=[cells, like(planes, rows, depth)] + [like(*shape) for shape in shapes],
        in_specs=[VMEM] * (before + len(shapes)),
        out_specs=[VMEM] * (2 + len(shapes)),
        scratch_shapes=vmem(
            [
                (CHANNELS, 2 * W + 1, 2 * W, depth),
                (SHIFTED + UP, 2 * W, depth),
                *edge_shapes[3:],
                *solutions,
            ]
        ),
        input_output_aliases={before + i: 2 + i for i in range(len(shapes))},
    )(local, tabs, accum, *more_ys, *halves[:7], *found)
    return residual, update


def solution(mesh):
    return jax.shard_map(
        body,
        mesh=mesh,
        in_specs=(
            P(None, "gx", "gy", "gz"),
            P(None, "gx", "gy", "gz"),
            P("gx", "gy", "gz"),
            P(None, "gx", "gy", "gz"),
            P("gx", "gy", "gz"),
            P("gx", "gy", "gz"),
            P(),
            P(),
            P(),
        ),
        out_specs=(P(None, "gx", "gy", "gz"), P("gx", "gy", "gz")),
        check_vma=False,
    )
```

```python
import functools
import itertools

import jax
import jax.numpy as jnp
from jax import lax
from jax.experimental import pallas as pl
from jax.experimental.pallas import tpu as pltpu
from jax.sharding import PartitionSpec as P

SWEEPS = 4
W = SWEEPS
relax_weight = 0.7

neighbour_offsets = [
    (along_x, along_y, along_z)
    for along_x in (-1, 0, 1)
    for along_y in (-1, 0, 1)
    for along_z in (-1, 0, 1)
    if (along_x, along_y, along_z) != (0, 0, 0)
]
upper_offsets = [offset for offset in neighbour_offsets if offset > (0, 0, 0)]
UP = len(upper_offsets)
FLAT = sum(1 for offset in upper_offsets if offset[0] == 0)
STEP = UP - FLAT

FAR = 5 + STEP
CHANNELS = FAR + FLAT + 2
STORAGE, OWN = FAR + FLAT, FAR + FLAT + 1
NEAR = W - 1
XMAIN = CHANNELS * NEAR + FAR
VMEM = pl.BlockSpec(memory_space=pltpu.VMEM)
ANY = pl.BlockSpec(memory_space=pl.ANY)
HBM = pl.BlockSpec(memory_space=pltpu.MemorySpace.HBM)
f32 = jnp.float32


def t_channel(k):
    return FAR + k if k < FLAT else 5 + k - FLAT


def pick(parity, even, odd):
    shape = (even if odd is None else odd).shape
    if even is None:
        even = jnp.zeros(shape, f32)
    if odd is None:
        odd = jnp.zeros(shape, f32)
    return jnp.where(jnp.full(shape, parity, jnp.int32) == 0, even, odd)


def parity_of(axis):
    return lax.rem(lax.axis_index(axis), 2)


def swaps(axis, first, second):
    count = lax.axis_size(axis)
    got = []
    for start, message in ((0, first), (1, second)):
        pairs = [(i, i + 1) for i in range(start, count - 1, 2)]
        if not pairs:
            got.append(None)
            continue
        got.append(lax.ppermute(message, axis, pairs + [(b, a) for a, b in pairs]))
    return got


def lanes_of(shape):
    return lax.broadcasted_iota(jnp.int32, shape, len(shape) - 1)


def span_of(planes):
    return 2 * W * planes


def groups_of(planes, depth):
    per = depth // span_of(planes)
    return per, -(-CHANNELS // per)


def lookups(tabs, region, numbers):
    index = region.astype(jnp.int32)
    return [
        jnp.take_along_axis(tabs[n], index, axis=1, mode="promise_in_bounds") for n in numbers
    ]


def pack_z(axis, *refs):
    state, mass, pore, trans, active, region, *tables = refs[:9]
    local, accum, tabs, first, second = refs[9:14]
    flags, masses, pores, small, sems = refs[14:]
    planes, rows, depth = pore.shape
    copies = [
        pltpu.make_async_copy(active, flags.at[0], sems.at[0]),
        pltpu.make_async_copy(region, flags.at[1], sems.at[1]),
        pltpu.make_async_copy(state, local.at[0:3], sems.at[2]),
        pltpu.make_async_copy(mass, masses, sems.at[3]),
        pltpu.make_async_copy(pore, pores, sems.at[4]),
    ]
    copies += [
        pltpu.make_async_copy(table, small.at[n], sems.at[5 + n]) for n, table in enumerate(tables)
    ]
    late = [
        pltpu.make_async_copy(trans.at[FLAT:UP], local.at[5:FAR], sems.at[8]),
        pltpu.make_async_copy(trans.at[0:FLAT], local.at[FAR : FAR + FLAT], sems.at[9]),
    ]
    for copy in copies + late:
        copy.start()
    for copy in copies:
        copy.wait()
    regions = tables[0].shape[1]
    for n in range(3):
        for c in range(3):
            tabs[3 * n + c, :, 0:regions] = jnp.broadcast_to(small[n, c : c + 1, :], (8, regions))
    for x in range(planes):
        for tile in range(rows // 8):
            span = slice(8 * tile, 8 * tile + 8)
            on = flags[0, x, span, :].astype(f32)
            level = flags[1, x, span, :]
            local[3, x, span, :] = on
            local[4, x, span, :] = level.astype(f32)
            press, water, gas = (local[c, x, span, :] for c in range(3))
            look = lookups(tabs, level, range(6))
            sat = (water, 1.0 - water - gas, gas)
            expand = [look[c] * jnp.exp(look[3 + c] * (press - 0.5)) for c in range(3)]
            volume = pores[x, span, :]
            stored = volume * (look[3] * sat[0] + look[4] * sat[1] + look[5] * sat[2])
            stored = jnp.where(on > 0, stored, 1.0)
            own = jnp.zeros((8, depth), f32)
            for c in range(3):
                value = volume * expand[c] * sat[c] - masses[c, x, span, :]
                accum[c, x, span, :] = value
                own = own + value / (expand[c] * stored)
            local[STORAGE, x, span, :] = stored
            local[OWN, x, span, :] = on * own
    for copy in late:
        copy.wait()

    per, groups = groups_of(planes, depth)
    even = parity_of(axis)
    lane = lanes_of((8, depth))

    @pl.loop(0, rows // 8, unroll=True)
    def _(tile):
        span = pl.ds(pl.multiple_of(8 * tile, 8), 8)
        for group in range(groups):
            high = jnp.zeros((8, depth), f32)
            low = jnp.zeros((8, depth), f32)
            for c in range(group * per, min(CHANNELS, group * per + per)):
                for x in range(planes):
                    base = (c % per) * span_of(planes) + 2 * W * x
                    values = local[c, x, span, :]
                    here = (lane >= base + W) & (lane < base + 2 * W)
                    high = jnp.where(here, pltpu.roll(values, (base + 2 * W) % depth, 1), high)
                    here = (lane >= base) & (lane < base + W)
                    low = jnp.where(here, pltpu.roll(values, base % depth, 1), low)
            first[group, span, :] = pick(even, high, low)
            second[group, span, :] = pick(even, low, high)


def pack_x(axis, local, *outs):
    planes = local.shape[1]
    even = parity_of(axis)
    for out, up in zip(outs, (even == 0, even != 0)):
        near = jnp.where(up, planes - NEAR, 0)
        far = jnp.where(up, planes - W, W - 1)
        for c in range(CHANNELS):
            for q in range(NEAR):
                out[c * NEAR + q] = local[c, near + q]
            if c < FAR:
                out[CHANNELS * NEAR + c] = local[c, far]


def put_rows(outs, n, values, even):
    head, tail = values[:W], values[values.shape[0] - W :]
    for out, up, down in zip(outs, (tail, head), (head, tail)):
        out[n] = pick(even, up, down)


def join_x(axis, y_axis, za, zb, local, *outs):
    planes = local.shape[1]
    even_y = parity_of(y_axis)
    for c in range(CHANNELS):
        for x in range(planes):
            put_rows(outs[2:], c * planes + x, local[c, x], even_y)
    for group in range(za.shape[0]):
        put_rows(outs[2:], CHANNELS * planes + group, za[group] + zb[group], even_y)
    rows, depth = za.shape[1:]
    even = parity_of(axis)
    per, _ = groups_of(planes, depth)
    per_x, groups_x = groups_of(W, depth)
    lane = lanes_of((rows, depth))
    for group in range(groups_x):
        sides = [jnp.zeros((rows, depth), f32) for _ in range(2)]
        for c in range(group * per_x, min(CHANNELS, group * per_x + per_x)):
            values = za[c // per] + zb[c // per]
            to = (c % per_x) * span_of(W)
            here = (lane >= to) & (lane < to + span_of(W))
            for n, plane in enumerate((planes - W, 0)):
                source = (c % per) * span_of(planes) + 2 * W * plane
                sides[n] = jnp.where(here, pltpu.roll(values, (to - source) % depth, 1), sides[n])
        outs[0][group] = pick(even, *sides)
        outs[1][group] = pick(even, *sides[::-1])


def join_y(axis, x_axis, planes, za, zb, xa, xb, ca, cb, *refs):
    count = len(refs) // 2
    columns, *outs = refs[count:]
    rows, depth = xa.shape[1:]
    even = parity_of(axis)
    even_x = parity_of(x_axis)
    per_x, groups_x = groups_of(W, depth)
    lane = lanes_of((rows, depth))
    for group in range(groups_x):
        a, b = ca[group], cb[group]
        put_rows(outs, 2 * XMAIN + group, pick(even_x, b, a), even)
        put_rows(outs, 2 * XMAIN + groups_x + group, pick(even_x, a, b), even)
    for c in range(CHANNELS):
        own = own_columns(c, za, zb, planes, slice(0, rows))
        group, base = c // per_x, (c % per_x) * span_of(W)
        a, b = ca[group], cb[group]
        below = pltpu.roll(pick(even_x, b, a), (depth - base) % depth, 1)
        above = pltpu.roll(pick(even_x, a, b), (2 * W * (planes + W) - base) % depth, 1)
        values = jnp.where(lane < 2 * W * W, below, jnp.where(lane < 2 * W * (W + planes), own, above))
        columns[c] = values

    @pl.loop(0, XMAIN // 2, unroll=True)
    def _(i):
        for j in range(2):
            n = 2 * i + j
            a, b = xa[n], xb[n]
            put_rows(outs, n, pick(even_x, b, a), even)
            put_rows(outs, XMAIN + n, pick(even_x, a, b), even)


PRESS, MOB, SLOPE, ACT = 0, 1, 4, 7
SHIFTED = 8


def z_shift(values, columns, plane, step):
    depth = values.shape[-1]
    lane = lanes_of(values.shape)
    if step > 0:
        edge = pltpu.roll(columns, depth - 1 - 2 * W * plane, 1)
        return jnp.where(lane == depth - 1, edge, pltpu.roll(values, depth - 1, 1))
    edge = pltpu.roll(columns, depth - 2 * W * plane - 2 * W + 1, 1)
    return jnp.where(lane == 0, edge, pltpu.roll(values, 1, 1))


def z_shift_columns(values, step):
    return pltpu.roll(values, values.shape[-1] - 1 if step > 0 else 1, 1)


def z_edge(current, values, plane, step):
    lane = lanes_of(values.shape)
    if step > 0:
        at = 2 * W * plane + 2 * W - 1
        return jnp.where(lane == at, pltpu.roll(values, at, 1), current)
    at = 2 * W * plane
    return jnp.where(lane == at, pltpu.roll(values, at + 1, 1), current)


def properties(get, plane, is_columns, put, tabs, arrays, halo, centre, span, done=None):
    fields, lower, half, weight, base = halo if is_columns else arrays
    halo_fields, halo_lower = halo[:2]
    press, water, gas, active, region = (get(c) for c in range(5))
    look = lookups(tabs, region, range(9))
    formation, compress, viscous = look[:3], look[3:6], look[6:]
    sat = (water, 1.0 - water - gas, gas)
    expand = [formation[c] * jnp.exp(compress[c] * (press - 0.5)) for c in range(3)]
    mob = [viscous[c] * expand[c] * sat[c] * sat[c] for c in range(3)]
    stored = get(STORAGE)
    stored = jnp.where(stored > 0, stored, 1.0)
    for c in range(3):
        put(weight, (c, plane), active / (expand[c] * stored))
    put(base, (plane,), get(OWN))
    shifts = []
    one = [press] + mob + [compress[c] * mob[c] for c in range(3)] + [active]
    for f, values in enumerate(one):
        put(fields, (f, 1, plane), values)
        shifts += [(0, (f, step + 1), step, values, f) for step in (-1, 1)]
    for k, offset in enumerate(upper_offsets):
        values = 0.5 * get(t_channel(k))
        put(half, (k, plane), values)
        values = values * active
        if offset[2] == 0:
            put(lower, (k, plane), values)
        else:
            shifts.append((1, (k,), -offset[2], values, SHIFTED + k))
    for array, lead, step, values, slot in shifts:
        if is_columns:
            centre[slot, span, :] = values
            shifted = z_shift_columns(values, step)
            if done is None:
                put((fields, lower)[array], (*lead, 0), shifted)
            else:
                keep = lambda now: jnp.where(done, now, shifted)
                put((fields, lower)[array], (*lead, 0), None, keep)
        else:
            put((fields, lower)[array], (*lead, plane), z_shift(values, centre[slot, span, :], plane, step))
            put((halo_fields, halo_lower)[array], (*lead, 0), None, lambda now: z_edge(now, values, plane, step))


def x_roll(values, step, is_columns):
    if not is_columns or step == 0:
        return values
    depth = values.shape[-1]
    return pltpu.roll(values, (depth - 2 * W * step) % depth, 1)


def link_cells(plane, is_columns, first, stride, arrays, out, results):
    fields, lower, half, weight, base = arrays
    coupling, scale, start = results
    depth = fields.shape[-1]
    here = (0, 0, 0)

    def read(ref, lead, offset):
        dx = 0 if is_columns else offset[0]
        values = ref[(*lead, plane + dx, pl.ds(first + stride * offset[1], 8), slice(None))]
        return x_roll(values, offset[0], is_columns)

    def at(f, offset):
        return read(fields, (f, offset[2] + 1), offset)

    press = at(PRESS, here)
    w = [read(weight, (c,), here) for c in range(3)]
    mob = [at(MOB + c, here) for c in range(3)]
    own_mob = w[0] * mob[0] + w[1] * mob[1] + w[2] * mob[2]
    own_slope = w[0] * at(SLOPE, here) + w[1] * at(SLOPE + 1, here) + w[2] * at(SLOPE + 2, here)
    flux = [jnp.zeros((8, depth), f32) for _ in range(3)]
    drops = jnp.zeros((8, depth), f32)
    means = jnp.ones((8, depth), f32)
    for n, offset in enumerate(neighbour_offsets):
        if offset > here:
            link = read(half, (upper_offsets.index(offset),), here) * at(ACT, offset)
        else:
            k = upper_offsets.index(tuple(-o for o in offset))
            link = read(lower, (k,), offset)
        drop = link * (press - at(PRESS, offset))
        other = [at(MOB + c, offset) for c in range(3)]
        for c in range(3):
            flux[c] = flux[c] + drop * other[c]
        drops = drops + drop
        mean = link * (own_mob + (w[0] * other[0] + w[1] * other[1] + w[2] * other[2]))
        slope = (
            w[0] * at(SLOPE, offset) + w[1] * at(SLOPE + 1, offset) + w[2] * at(SLOPE + 2, offset)
        )
        means = means + mean
        coupling[n, plane, out, :] = drop * slope - mean
    flux = [flux[c] + mob[c] * drops for c in range(3)]
    rate = relax_weight / (means + own_slope * drops)
    right = read(base, (), here) + (w[0] * flux[0] + w[1] * flux[1] + w[2] * flux[2])
    scale[plane, out, :] = rate
    start[plane, out, :] = -rate * right
    return flux


def row_cells(tiles, tabs, arrays, halo, centre):
    def cells(get, plane, is_columns=False):
        for tile in range(tiles):
            span, to = slice(8 * tile, 8 * tile + 8), slice(8 + 8 * tile, 16 + 8 * tile)

            def put(ref, lead, values, change=None):
                at = (*lead, to, slice(None))
                ref[at] = values if change is None else change(ref[at])

            properties(
                lambda c: get(c, span), plane, is_columns, put, tabs, arrays, halo, centre, span
            )

    return cells


def row_links(tiles, plane, is_columns, arrays, results, store=None):
    for tile in range(tiles):
        out = slice(8 * tile, 8 * tile + 8)
        flow = link_cells(plane, is_columns, 8 + 8 * tile, 1, arrays, out, results)
        if store is not None:
            for c in range(3):
                store[c, plane, out, :] = flow[c]


def own_columns(c, za, zb, planes, span):
    depth = za.shape[-1]
    per, _ = groups_of(planes, depth)
    group, base = c // per, (c % per) * span_of(planes)
    return pltpu.roll(za[group, span, :] + zb[group, span, :], (2 * W * W - base) % depth, 1)


def among_own(planes, shape):
    lane = lanes_of(shape)
    return (lane >= 2 * W * W) & (lane < 2 * W * (W + planes))


def inner_local(local, za, zb, tabs, *refs):
    arrays, results, store, parts = refs[:5], refs[5:8], refs[8], refs[9:11]
    halo, centre = (*parts, *refs[11:14]), refs[14]
    planes, rows, depth = local.shape[1:]
    tiles = rows // 8
    cells = row_cells(tiles, tabs, arrays, halo, centre)

    def columns(c, span):
        values = own_columns(c, za, zb, planes, span)
        return jnp.where(among_own(planes, values.shape), values, 0.0)

    cells(columns, 0, True)

    @pl.loop(0, planes, unroll=True)
    def _(x):
        cells(lambda c, span: local[c, x, span, :], W + x)

    @pl.loop(W + 1, W + planes - 1, unroll=True)
    def _(plane):
        row_links(tiles, plane, False, arrays, results, store)


def inner(x_axis, planes, columns, xa, xb, tabs, *refs):
    parts, refs = refs[:2], refs[11:]
    results, halo_results, store = refs[:3], refs[3:6], refs[6]
    edges, arrays, halo, centre = refs[7:17], refs[17:22], refs[22:27], refs[27]
    rows, depth = xa.shape[1:]
    total = planes + 2 * W
    even_x = parity_of(x_axis)
    tiles = rows // 8
    cells = row_cells(tiles, tabs, arrays, halo, centre)

    cells(lambda c, span: columns[c, span, :], 0, True)
    own = among_own(planes, (8, depth))
    for array, part in zip(halo, parts):
        for lead in itertools.product(*(range(n) for n in part.shape[:-2])):
            for tile in range(tiles):
                at = (*lead, slice(8 + 8 * tile, 16 + 8 * tile), slice(None))
                array[at] = jnp.where(own, part[at], array[at])

    def from_x(n, low):
        def get(c, span):
            i = n(c)
            if i is None:
                return jnp.zeros((8, depth), f32)
            u, v = xa[i, span, :], xb[i, span, :]
            return pick(even_x, v, u) if low else pick(even_x, u, v)

        return get

    @pl.loop(0, NEAR, unroll=True)
    def _(q):
        near = lambda c: c * NEAR + q
        cells(from_x(near, True), 1 + q)
        cells(from_x(near, False), W + planes + q)

    far = lambda c: CHANNELS * NEAR + c if c < FAR else None
    cells(from_x(far, True), 0)
    cells(from_x(far, False), total - 1)

    def hand_on(sources, targets, plane):
        for source, target in zip(sources, targets):
            for lead in itertools.product(*(range(n) for n in source.shape[:-3])):
                last = source[(*lead, plane, slice(6 + rows, 8 + rows), slice(None))]
                head = source[(*lead, plane, slice(8, 10), slice(None))]
                target[(*lead, plane, pl.ds(0, 2, stride=2), slice(None))] = last
                target[(*lead, plane, pl.ds(RING - 3, 2, stride=2), slice(None))] = head

    hand_on(halo, edges[5:], 0)

    @pl.loop(0, total, unroll=True)
    def _(plane):
        hand_on(arrays, edges[:5], plane)

    row_links(tiles, 0, True, halo, halo_results)

    @pl.loop(0, W, unroll=True)
    def _(n):
        row_links(tiles, 1 + n, False, arrays, results, store)
        row_links(tiles, W + planes - 1 + n, False, arrays, results, store)


RING = 2 * (W + 2)


def put_ring(ref, lead, values, change=None):
    low = (*lead, pl.ds(1, W, stride=2), slice(None))
    high = (*lead, pl.ds(4, W, stride=2), slice(None))
    if change is not None:
        values = change(jnp.concatenate([ref[low], ref[high]], axis=0))
    ref[low] = values[:W]
    ref[high] = values[W:]


def halo_rows(even_y, sources, n, target, at):
    shape = target.shape[-1:]
    low = high = jnp.zeros((W, *shape), f32)
    if sources:
        a = sources[0][n]
        b = sources[1][n] if len(sources) > 1 else None
        low, high = pick(even_y, b, a), pick(even_y, a, b)
    target[(*at, slice(0, W), slice(None))] = low
    target[(*at, slice(W, 2 * W), slice(None))] = high


def ring_links(plane, is_columns, arrays, results, store):
    flow = link_cells(plane, is_columns, 2, 2, arrays, slice(0, 8), results)
    if not is_columns:
        for c in range(3):
            store[c, plane] = flow[c]


def finish_local(axis, count_y, planes, tabs, *refs):
    ys, refs = refs[:count_y], refs[count_y + 10 :]
    arrays, halo, results, store = refs[:5], refs[5:10], refs[10:13], refs[13]
    raw, packed, centre = refs[14:]
    depth = raw.shape[-1]
    even_y = parity_of(axis)
    per, groups = groups_of(planes, depth)
    for group in range(groups):
        halo_rows(even_y, ys, CHANNELS * planes + group, packed, (group,))

    @pl.loop(0, CHANNELS, unroll=True)
    def _(c):
        for x in range(planes):
            halo_rows(even_y, ys, c * planes + x, raw, (c, x))

    def cells(get, plane, is_columns=False):
        span = slice(0, 2 * W)
        properties(get, plane, is_columns, put_ring, tabs, arrays, halo, centre, span)

    own = among_own(planes, (2 * W, depth))

    def columns(c):
        base = (c % per) * span_of(planes)
        return jnp.where(own, pltpu.roll(packed[c // per], (2 * W * W - base) % depth, 1), 0.0)

    cells(columns, 0, True)

    @pl.loop(0, planes, unroll=True)
    def _(x):
        cells(lambda c: raw[c, x], W + x)

    @pl.loop(W + 1, W + planes - 1, unroll=True)
    def _(plane):
        ring_links(plane, False, arrays, results, store)


def finish(axis, count_y, local, *refs):
    tabs, accum, ys, more_ys = refs[0], refs[1], refs[2 : 2 + count_y], refs[2 + count_y : 2 + 2 * count_y]
    refs = refs[2 + 2 * count_y :]
    results, halo_results, store = refs[:3], refs[3:6], refs[6]
    residual, update = refs[21:23]
    arrays, halo = refs[23:28], refs[28:33]
    edge_results, edge_store = refs[33:36], refs[36]
    raw, packed, centre, edge_halo_results = refs[37], refs[38], refs[39], refs[40:43]
    sols, halo_sols, edge_sols, edge_halo_sols = (refs[43 + 2 * i : 45 + 2 * i] for i in range(4))
    planes, rows, depth = local.shape[1:]
    total = planes + 2 * W
    even_y = parity_of(axis)

    @pl.loop(0, CHANNELS, unroll=True)
    def _(c):
        for q in range(NEAR):
            halo_rows(even_y, more_ys, c * NEAR + q, raw, (c, 1 + q))
            halo_rows(even_y, more_ys, XMAIN + c * NEAR + q, raw, (c, W + q))

    @pl.loop(0, FAR, unroll=True)
    def _(c):
        halo_rows(even_y, more_ys, CHANNELS * NEAR + c, raw, (c, 0))
        halo_rows(even_y, more_ys, XMAIN + CHANNELS * NEAR + c, raw, (c, 2 * W - 1))

    for c in range(FAR, CHANNELS):
        for slot in (0, 2 * W - 1):
            raw[c, slot] = jnp.zeros((2 * W, depth), f32)

    def cells(slot, plane, is_columns=False):
        done = among_own(planes, (2 * W, depth)) if is_columns else None
        get, span = lambda c: raw[c, slot], slice(0, 2 * W)
        properties(get, plane, is_columns, put_ring, tabs, arrays, halo, centre, span, done)

    per, groups = groups_of(planes, depth)
    per_x, groups_x = groups_of(W, depth)
    for group in range(groups):
        halo_rows(even_y, ys, CHANNELS * planes + group, packed, (group,))
    for group in range(2 * groups_x):
        halo_rows(even_y, more_ys, 2 * XMAIN + group, packed, (groups + group,))
    lane = lanes_of((2 * W, depth))
    for c in range(CHANNELS):
        base, base_x = (c % per) * span_of(planes), (c % per_x) * span_of(W)
        own = pltpu.roll(packed[c // per], (2 * W * W - base) % depth, 1)
        below = pltpu.roll(packed[groups + c // per_x], (depth - base_x) % depth, 1)
        above = packed[groups + groups_x + c // per_x]
        above = pltpu.roll(above, (2 * W * (planes + W) - base_x) % depth, 1)
        own = jnp.where(lane < 2 * W * (W + planes), own, above)
        raw[c, 2 * W] = jnp.where(lane < 2 * W * W, below, own)

    cells(2 * W, 0, True)

    @pl.loop(0, W, unroll=True)
    def _(n):
        cells(n, n)
        cells(W + n, W + planes + n)

    ring_links(0, True, halo, edge_halo_results, None)

    @pl.loop(0, W, unroll=True)
    def _(n):
        ring_links(1 + n, False, arrays, edge_results, edge_store)
        ring_links(W + planes - 1 + n, False, arrays, edge_results, edge_store)

    tiles = rows // 8

    row = lax.broadcasted_iota(jnp.int32, (8, depth), 0)

    def merged(mains, edge):
        first, last = pltpu.roll(edge, 1, 0), pltpu.roll(edge, 7, 0)
        mains = [jnp.where(row == 0, first, mains[0])] + mains[1:]
        return mains[:-1] + [jnp.where(row == 7, last, mains[-1])]

    def put_parts(is_columns, slot, step, plane, mains, edge):
        to, edge_to = (
            (halo_sols[slot], edge_halo_sols[slot]) if is_columns else (sols[slot], edge_sols[slot])
        )
        for tile, values in enumerate(mains):
            to[step + 1, plane, 8 + 8 * tile : 16 + 8 * tile, :] = values
        edge_to[step + 1, plane, 2:10, :] = edge
        to[step + 1, plane, 7:8, :] = edge[5:6]
        to[step + 1, plane, 8 + rows : 9 + rows, :] = edge[2:3]
        edge_to[step + 1, plane, 0:1, :] = mains[-1][6:7]
        edge_to[step + 1, plane, RING - 1 : RING, :] = mains[0][1:2]

    def halo_parts(slot, step):
        mains = [
            halo_sols[slot][step + 1, 0, 8 + 8 * tile : 16 + 8 * tile, :] for tile in range(tiles)
        ]
        return mains, edge_halo_sols[slot][step + 1, 0, 2:10, :]

    def put_solution(slot, plane, mains, edge, is_columns=False):
        mains = merged(mains, edge)
        put_parts(is_columns, slot, 0, plane, mains, edge)
        for step in (-1, 1):
            if is_columns:
                shift = lambda values: z_shift_columns(values, step)
                put_parts(True, slot, step, plane, [shift(u) for u in mains], shift(edge))
                continue
            shift = lambda u, v: z_shift(u, v, plane, step)
            halo_mains, halo_edge = halo_parts(slot, 0)
            shifted = [shift(u, v) for u, v in zip(mains, halo_mains)]
            put_parts(False, slot, step, plane, shifted, shift(edge, halo_edge))
            shift = lambda u, v: z_edge(u, v, plane, step)
            halo_mains, halo_edge = halo_parts(slot, step)
            shifted = [shift(u, v) for u, v in zip(halo_mains, mains)]
            put_parts(True, slot, step, 0, shifted, shift(halo_edge, edge))

    def relaxed(slot, plane, tile, is_columns=False):
        if tile is None:
            ref = (edge_halo_sols if is_columns else edge_sols)[slot]
            first, stride, out = 2, 2, slice(0, 8)
            coupling, scale, start = edge_halo_results if is_columns else edge_results
        else:
            ref = (halo_sols if is_columns else sols)[slot]
            first, stride = 8 + 8 * tile, 1
            out = slice(8 * tile, 8 * tile + 8)
            coupling, scale, start = halo_results if is_columns else results

        def get(offset):
            dx = 0 if is_columns else offset[0]
            values = ref[offset[2] + 1, plane + dx, pl.ds(first + stride * offset[1], 8), :]
            return x_roll(values, offset[0], is_columns)

        parts = [jnp.zeros((8, depth), f32) for _ in range(2)]
        for n, offset in enumerate(neighbour_offsets):
            parts[n % 2] = parts[n % 2] + coupling[n, plane, out, :] * get(offset)
        return (
            (1.0 - relax_weight) * get((0, 0, 0))
            + start[plane, out, :]
            - scale[plane, out, :] * (parts[0] + parts[1])
        )

    def first_sweep(plane, is_columns=False):
        start = (halo_results if is_columns else results)[2]
        edge = (edge_halo_results if is_columns else edge_results)[2]
        mains = [start[plane, 8 * tile : 8 * tile + 8, :] for tile in range(tiles)]
        put_solution(0, plane, mains, edge[plane], is_columns)

    first_sweep(0, True)

    @pl.loop(1, total - 1, unroll=True)
    def _(plane):
        first_sweep(plane)

    def sweep_of(slot, plane, is_columns=False):
        mains = [relaxed(slot, plane, tile, is_columns) for tile in range(tiles)]
        put_solution(1 - slot, plane, mains, relaxed(slot, plane, None, is_columns), is_columns)

    for sweep in range(2, SWEEPS):
        slot = sweep % 2
        sweep_of(slot, 0, True)

        @pl.loop(sweep, total - sweep, unroll=True)
        def _(plane):
            sweep_of(slot, plane)

    @pl.loop(0, planes, unroll=True)
    def _(x):
        slot, plane = SWEEPS % 2, W + x
        edge = relaxed(slot, plane, None)
        for tile in range(tiles):
            span = slice(8 * tile, 8 * tile + 8)
            update[x, span, :] = relaxed(slot, plane, tile)
            active = local[3, x, span, :]
            for c in range(3):
                flow = store[c, plane, span, :]
                residual[c, x, span, :] = active * (accum[c, x, span, :] + flow)
        for row_of, edge_row in ((0, 7), (rows - 1, 0)):
            to, source = slice(row_of, row_of + 1), slice(edge_row, edge_row + 1)
            update[x, to, :] = edge[source]
            active = local[3, x, to, :]
            for c in range(3):
                flow = edge_store[c, plane, source, :]
                residual[c, x, to, :] = active * (accum[c, x, to, :] + flow)


def call(kernel, name, mib, **options):
    return pl.pallas_call(
        kernel,
        name=name,
        compiler_params=pltpu.CompilerParams(vmem_limit_bytes=mib << 20),
        **options,
    )


def cell_shapes(total, height, depth):
    return [
        (*lead, count, height, depth)
        for count in (total, 1)
        for lead in ((SHIFTED, 3), (UP,), (UP,), (3,), ())
    ]


def result_shapes(total, height, depth):
    return [
        shape
        for count in (total, 1)
        for shape in ((2 * UP, count, height, depth), (count, height, depth), (count, height, depth))
    ]


def body(
    cell_state,
    old_mass,
    pore_volume,
    transmissibility,
    active_mask,
    pvt_region,
    formation_factor,
    compressibility,
    inverse_viscosity,
):
    ax, ay, az = "gx", "gy", "gz"
    planes, rows, depth = pore_volume.shape
    total = planes + 2 * W
    per, groups = groups_of(planes, depth)
    assert per >= 1 and 2 * W * total <= depth and rows % 8 == 0 and RING <= 16
    tables = (formation_factor, compressibility, inverse_viscosity)
    like = lambda *shape: jax.ShapeDtypeStruct(shape, f32)
    fill = lambda shape, got: [jnp.zeros(shape.shape, f32) if one is None else one for one in got]

    arguments = (
        *(cell_state, old_mass, pore_volume, transmissibility, active_mask, pvt_region),
        *tables,
    )
    z_shape = like(groups, rows, depth)
    cells = like(3, planes, rows, depth)
    local, accum, tabs, *z_send = call(
        functools.partial(pack_z, az),
        "pack_z",
        8,
        out_shape=(like(CHANNELS, planes, rows, depth), cells, like(9, 8, depth), z_shape, z_shape),
        in_specs=[HBM] * 9,
        out_specs=(VMEM,) * 5,
        scratch_shapes=[
            pltpu.VMEM((2, planes, rows, depth), jnp.int32),
            pltpu.VMEM(cells.shape, f32),
            pltpu.VMEM((planes, rows, depth), f32),
            pltpu.VMEM((3, *formation_factor.shape), f32),
            pltpu.SemaphoreType.DMA((10,)),
        ],
    )(*(pltpu.with_memory_space_constraint(array, pltpu.MemorySpace.HBM) for array in arguments))
    za, zb = fill(z_shape, swaps(az, *z_send))

    x_shape = like(XMAIN, rows, depth)
    x_send = call(functools.partial(pack_x, ax), "pack_x", 8, out_shape=(x_shape, x_shape))(local)
    xa, xb = fill(x_shape, swaps(ax, *x_send))

    count_y = min(lax.axis_size(ay) - 1, 2)
    ys, more_ys = [], []
    c_shape = like(groups_of(W, depth)[1], rows, depth)
    sent = call(
        functools.partial(join_x, ax, ay),
        "join_x",
        8,
        out_shape=(c_shape, c_shape) + (like(CHANNELS * planes + groups, W, depth),) * count_y,
    )(za, zb, local)
    c_send, y_send = sent[:2], sent[2:]
    ca, cb = fill(c_shape, swaps(ax, *c_send))
    if count_y:
        ys = swaps(ay, y_send[0], y_send[-1])[:count_y]
    vmem = lambda shapes: [pltpu.VMEM(shape, f32) for shape in shapes]
    flow = (3, total, rows, depth)
    tall = cell_shapes(total, rows + 16, depth)
    wide = result_shapes(total, rows, depth)
    centre = (SHIFTED + UP, rows, depth)
    shapes = tall[:5] + wide[:3] + [flow] + tall[5:7]
    found = call(
        inner_local,
        "inner_local",
        16,
        out_shape=[like(*shape) for shape in shapes],
        in_specs=[VMEM] * 4,
        out_specs=[VMEM] * len(shapes),
        scratch_shapes=vmem(tall[7:] + [centre]),
    )(local, za, zb, tabs)
    arrays, found, parts = found[:5], found[5:9], found[9:]

    columns, *y_send = call(
        functools.partial(join_y, ay, ax, planes),
        "join_y",
        8,
        out_shape=(like(CHANNELS, rows, depth),)
        + (like(2 * XMAIN + 2 * groups_of(W, depth)[1], W, depth),) * count_y,
        in_specs=[VMEM] * 6 + [ANY] * (count_y + 1),
    )(za, zb, xa, xb, ca, cb, *ys, parts[1])
    if count_y:
        more_ys = swaps(ay, y_send[0], y_send[-1])[:count_y]

    edges = cell_shapes(total, 16, depth)
    shapes = wide + [flow] + edges + tall[:5]
    halves = call(
        functools.partial(inner, ax, planes),
        "inner",
        16,
        out_shape=[like(*shape) for shape in shapes],
        in_specs=[VMEM] * 15,
        out_specs=[VMEM] * len(shapes),
        scratch_shapes=vmem(tall[5:] + [centre]),
        input_output_aliases={6: 0, 7: 1, 8: 2, 9: 6, **{10 + i: 17 + i for i in range(5)}},
    )(columns, xa, xb, tabs, *parts, *found, *arrays)[:17]

    solutions = [
        (3, count, height, depth) for height in (rows + 16, 16) for count in (total, 1) for _ in range(2)
    ]
    edge_shapes = result_shapes(total, 2 * W, depth)
    groups_x = groups_of(W, depth)[1]
    shapes = edges + edge_shapes[:3] + [(3, total, 2 * W, depth)]
    found = call(
        functools.partial(finish_local, ay, count_y, planes),
        "finish_local",
        16,
        out_shape=[like(*shape) for shape in shapes],
        in_specs=[VMEM] * (1 + count_y + 10),
        out_specs=[VMEM] * len(shapes),
        scratch_shapes=vmem(
            [
                (CHANNELS, planes, 2 * W, depth),
                (groups, 2 * W, depth),
                (SHIFTED + UP, 2 * W, depth),
            ]
        ),
        input_output_aliases={1 + count_y + i: i for i in range(10)},
    )(tabs, *ys, *halves[7:])
    before = 3 + 2 * count_y + 7
    residual, update, *_ = call(
        functools.partial(finish, ay, count_y),
        "finish",
        16,
        out_shape=[cells, like(planes, rows, depth)] + [like(*shape) for shape in shapes],
        in_specs=[VMEM] * (before + len(shapes)),
        out_specs=[VMEM] * (2 + len(shapes)),
        scratch_shapes=vmem(
            [
                (CHANNELS, 2 * W + 1, 2 * W, depth),
                (groups + 2 * groups_x, 2 * W, depth),
                (SHIFTED + UP, 2 * W, depth),
                *edge_shapes[3:],
                *solutions,
            ]
        ),
        input_output_aliases={before + i: 2 + i for i in range(len(shapes))},
    )(local, tabs, accum, *ys, *more_ys, *halves[:7], *found)
    return residual, update


def solution(mesh):
    return jax.shard_map(
        body,
        mesh=mesh,
        in_specs=(
            P(None, "gx", "gy", "gz"),
            P(None, "gx", "gy", "gz"),
            P("gx", "gy", "gz"),
            P(None, "gx", "gy", "gz"),
            P("gx", "gy", "gz"),
            P("gx", "gy", "gz"),
            P(),
            P(),
            P(),
        ),
        out_specs=(P(None, "gx", "gy", "gz"), P("gx", "gy", "gz")),
        check_vma=False,
    )
```
